32 devices in a mesh: fsdp: 4 (over z), ctx: 2 (over x), tp: 4 (over y, core).
Axes of the slice: x: 2, y: 2, z: 4, core: 2. Of those that a mesh axis runs over, the one named last changes fastest.
Arguments:
- layer_input: bfloat16 [8192, 4096], P(('fsdp', 'ctx'), 'tp'), may hold values from -6 to 6
- attn_gain: bfloat16 [4096], P('tp'), may hold values from 0.099609375 to 1.8984375
- qkv_weight: bfloat16 [4096, 3, 4096], P('fsdp', None, 'tp'), may hold values from -1 to 1
- out_weight: bfloat16 [4096, 4096], P('tp', 'fsdp'), may hold values from -0.75 to 0.75
- ffn_gain: bfloat16 [4096], P('tp'), may hold values from 0.099609375 to 1.8984375
- gate_up_weight: bfloat16 [4096, 2, 11008], P('fsdp', None, 'tp'), may hold values from -0.09375 to 0.09375
- down_weight: bfloat16 [11008, 4096], P('tp', 'fsdp'), may hold values from -0.0546875 to 0.0546875
- cotangent: bfloat16 [8192, 4096], P(('fsdp', 'ctx'), 'tp'), may hold values from -6 to 6
Outputs:
- layer_output: bfloat16 [8192, 4096], P(('fsdp', 'ctx'), 'tp')
- grad_input: float32 [8192, 4096], P(('fsdp', 'ctx'), 'tp')
- grad_attn_gain: float32 [4096], P('tp')
- grad_qkv: float32 [4096, 3, 4096], P(('fsdp', 'ctx'), None, 'tp')
- grad_out_weight: float32 [4096, 4096], P('tp', ('fsdp', 'ctx'))
- grad_ffn_gain: float32 [4096], P('tp')
- grad_gate_up: float32 [4096, 2, 11008], P(('fsdp', 'ctx'), None, 'tp')
- grad_down: float32 [11008, 4096], P('tp', ('fsdp', 'ctx'))
The draws below stay inside these ranges and needn't reach their ends.
All inputs are finite; a program needn't handle non-finite values.
Results may differ from the reference program's by a relative error of at most 0.018.
Values may be sent and summed in bfloat16 or wider, within the bound.
No kernel may reach another device: no remote copies, remote signals or barrier semaphores. Data moves between devices by JAX's collectives and lax.ppermute only.
A program may use at most 384 MiB of HBM per device.

```python
import math
import jax
import jax.numpy as jnp
from jax import lax

D = 4096
FF = 11008
HD = 128
SEQ = 2048
TOKENS = 8192
N_FSDP = 4


def draw_qkv_weight(key, part):
    first_key = jax.random.fold_in(key, 0)
    drawn = jax.random.truncated_normal(first_key, -6.0, 6.0, (D, 3, D), jnp.float32) / math.sqrt(D)
    return drawn.astype(jnp.bfloat16)


def shard_levels(stream_key, shape, pieces, low, high):
    gain = 1.0
    for axis_at, blocks in pieces:
        draws = jax.random.uniform(jax.random.fold_in(jax.random.fold_in(stream_key, 6), axis_at), (blocks,), jnp.float32, low / len(pieces), high / len(pieces))
        gain = gain * jnp.repeat(jnp.exp(draws), shape[axis_at] // blocks).reshape((-1,) + (1,) * (len(shape) - 1 - axis_at))
    return gain


def centred(stream_key, shape, deviation, reach, pieces=(), held_as=jnp.bfloat16):
    gain = shard_levels(stream_key, shape, pieces, -0.22, 0.18) if pieces else 1.0
    drawn = jax.random.normal(stream_key, shape, jnp.float32) * deviation * gain
    return jnp.minimum(jnp.maximum(drawn, -reach), reach).astype(held_as)


def setup_inputs(seed: int = 0) -> dict:
    key_list = jax.random.split(jax.random.key(seed), 9)
    return {
        "layer_input": centred(key_list[0], (TOKENS, D), 1.0, 6.0, ((0, 8), (1, 4))),
        "attn_gain": jnp.clip(1.0 + 0.18 * jax.random.normal(key_list[1], (D,), jnp.float32), 0.099609375, 1.8984375).astype(jnp.bfloat16),
        "qkv_weight": draw_qkv_weight(jax.random.fold_in(key_list[8], 71), 0),
        "out_weight": centred(key_list[3], (D, D), (D // 64) ** -0.5, 0.75, ((0, 4), (1, 4))),
        "ffn_gain": jnp.clip(1.0 + 0.18 * jax.random.normal(key_list[4], (D,), jnp.float32), 0.099609375, 1.8984375).astype(jnp.bfloat16),
        "gate_up_weight": centred(key_list[5], (D, 2, FF), D ** -0.5, 0.09375, ((0, 4), (2, 4))),
        "down_weight": centred(key_list[6], (FF, D), FF ** -0.5, 0.0546875, ((0, 4), (1, 4))),
        "cotangent": centred(key_list[7], (TOKENS, D), 1.0, 6.0, ((0, 8), (1, 4))),
    }


@jax.custom_vjp
def low(v):
    return lax.optimization_barrier(v.astype(jnp.bfloat16)).astype(jnp.float32)

@jax.custom_vjp
def low_back(v):
    return v

def low_keep(v):
    return (low(v), None)

def low_pass(kept, grad):
    return (grad,)

def back_keep(v):
    return (v, None)

def back_low(kept, grad):
    return (low(grad),)
low.defvjp(low_keep, low_pass)
low_back.defvjp(back_keep, back_low)
rms_epsilon = 1e-05
masked_score = -1e+30
highest = lax.Precision.HIGHEST

def product(left, right):
    return jnp.dot(left, right, precision=highest, preferred_element_type=jnp.float32)

def rotate(values, positions, direction):
    half_width = HD // 2
    inv_freq = jnp.exp(-math.log(10000.0) * jnp.arange(half_width, dtype=jnp.float32) * 2.0 / HD)
    angles = positions.astype(jnp.float32)[:, None] * inv_freq[None, :]
    cosine = jnp.cos(angles)[:, None, :]
    sine_table = direction * jnp.sin(angles)[:, None, :]
    shaped = values.reshape(values.shape[0], -1, 2, half_width)
    lower_half = shaped[:, :, 0, :]
    upper_half = shaped[:, :, 1, :]
    turned = jnp.stack([lower_half * cosine - upper_half * sine_table, upper_half * cosine + lower_half * sine_table], axis=2)
    return turned.reshape(values.shape)

def attend(queries, keys_in, values_in):
    head_count = D // HD
    block_len = min(512, SEQ)
    block_count = SEQ // block_len
    query_heads = queries.reshape(block_count, block_len, head_count, HD)
    key_heads = keys_in.reshape(SEQ, head_count, HD)
    value_heads = values_in.reshape(SEQ, head_count, HD)
    key_index = jnp.arange(SEQ, dtype=jnp.int32)
    score_scale = 1.0 / math.sqrt(HD)

    def one_block(query_block, block_index):
        scores = jnp.einsum('qhd,khd->hqk', query_block, key_heads, precision=highest)
        scores = low_back(scores * score_scale)
        query_index = block_index * block_len + jnp.arange(block_len, dtype=jnp.int32)
        allowed = key_index[None, :] <= query_index[:, None]
        scores = jnp.where(allowed[None, :, :], scores, masked_score)
        soft = low(jax.nn.softmax(scores, axis=-1))
        mixed = jnp.einsum('hqk,khd->qhd', soft, value_heads, precision=highest)
        return low(low_back(mixed))
    checked = jax.checkpoint(one_block)
    outputs = lax.map(lambda item: checked(item[0], item[1]), (query_heads, jnp.arange(block_count, dtype=jnp.int32)))
    return outputs.reshape(SEQ, D)

def forward(tokens, attn_gain, qkv_weight, out_weight, ffn_gain, gate_up_weight, down_weight):
    rms_one = lax.rsqrt(lax.optimization_barrier(jnp.mean(tokens * tokens, axis=-1, keepdims=True)) + rms_epsilon)
    normed_attn = low(tokens * rms_one * attn_gain)
    proj = low_back(product(normed_attn, qkv_weight.reshape(D, 3 * D))).reshape(SEQ, 3, D)
    positions = jnp.arange(SEQ, dtype=jnp.int32)
    queries = low(rotate(proj[:, 0], positions, 1.0))
    keys_rot = low(rotate(proj[:, 1], positions, 1.0))
    values_low = low(proj[:, 2])
    attn_heads = attend(queries, keys_rot, values_low)
    resid = tokens + low_back(product(attn_heads, out_weight))
    rms_two = lax.rsqrt(lax.optimization_barrier(jnp.mean(resid * resid, axis=-1, keepdims=True)) + rms_epsilon)
    normed_ffn = low(resid * rms_two * ffn_gain)
    gate_up = low_back(product(normed_ffn, gate_up_weight.reshape(D, 2 * FF))).reshape(SEQ, 2, FF)
    hidden = low(jax.nn.silu(gate_up[:, 0]) * gate_up[:, 1])
    return resid + low_back(product(hidden, down_weight))

def reference(layer_input, attn_gain, qkv_weight, out_weight, ffn_gain, gate_up_weight, down_weight, cotangent):
    weights = (attn_gain.astype(jnp.float32), qkv_weight.astype(jnp.float32), out_weight.astype(jnp.float32), ffn_gain.astype(jnp.float32), gate_up_weight.astype(jnp.float32), down_weight.astype(jnp.float32))
    inputs_seq = layer_input.astype(jnp.float32).reshape(N_FSDP, SEQ, D)
    cotan_seq = cotangent.astype(jnp.float32).reshape(N_FSDP, SEQ, D)

    def one_sequence(totals, pair):
        tokens, cotan = pair
        output, pullback = jax.vjp(forward, tokens, *weights)
        grads = pullback(cotan)
        updated = tuple((total + grad for total, grad in zip(totals, grads[1:])))
        return (updated, (output.astype(jnp.bfloat16), grads[0]))
    start_totals = tuple((jnp.zeros(weight.shape, jnp.float32) for weight in weights))
    totals, (outputs, input_grads) = lax.scan(one_sequence, start_totals, (inputs_seq, cotan_seq))
    return (outputs.reshape(TOKENS, D), input_grads.reshape(TOKENS, D), totals[0], totals[1], totals[2], totals[3], totals[4], totals[5])
```

```python
import math

import jax
import jax.numpy as jnp
from jax import lax
from jax.sharding import PartitionSpec as P

D = 4096
HD = 128

rms_epsilon = 1e-05
masked_score = -1e30
BF = jnp.bfloat16
F32 = jnp.float32


def rotate(values, positions, direction):
    half_width = HD // 2
    inv_freq = jnp.exp(-math.log(10000.0) * jnp.arange(half_width, dtype=F32) * 2.0 / HD)
    angles = positions.astype(F32)[:, None] * inv_freq[None, :]
    cosine = jnp.cos(angles)[:, None, :]
    sine_table = direction * jnp.sin(angles)[:, None, :]
    shaped = values.reshape(values.shape[0], -1, 2, half_width)
    lower_half = shaped[:, :, 0, :]
    upper_half = shaped[:, :, 1, :]
    turned = jnp.stack(
        [
            lower_half * cosine - upper_half * sine_table,
            upper_half * cosine + lower_half * sine_table,
        ],
        axis=2,
    )
    return turned.reshape(values.shape)


def row_total(values):
    return lax.psum(values, "tp")


def swap(values, axis, bit):
    count = lax.axis_size(axis)
    step = 1 << bit
    return lax.ppermute(values, axis, [(i, i ^ step) for i in range(count)])


def bit_of(axis, bit):
    return (lax.axis_index(axis) >> bit) & 1


def tp_bits():
    return range(lax.axis_size("tp").bit_length() - 1)


def in_order(bit, mine, other):
    first = lax.select(jnp.broadcast_to(bit == 0, mine.shape), mine, other)
    second = lax.select(jnp.broadcast_to(bit == 0, mine.shape), other, mine)
    return first, second


def gather_rows(values):
    rows, cols = values.shape
    high_bits = [b for b in reversed(tp_bits()) if b > 0]
    plans = (
        [("ctx", 0)] + [("tp", b) for b in high_bits] + [("tp", 0)],
        [("tp", b) for b in high_bits] + [("ctx", 0)] + [("tp", 0)],
    )
    pieces = []
    for index, plan in enumerate(plans):
        part = values[index * (rows // 2) : (index + 1) * (rows // 2)]
        blocks = {(): part}
        ctx_parts = [[part]]
        for axis, bit in plan:
            if axis == "ctx":
                mine = jnp.concatenate(ctx_parts[0], axis=1)
                other = swap(mine, "ctx", 0)
                first, second = in_order(lax.axis_index("ctx"), mine, other)
                width = ctx_parts[0][0].shape[1]
                ctx_parts = [
                    [full[:, i : i + width] for i in range(0, full.shape[1], width)]
                    for full in (first, second)
                ]
            else:
                mine = jnp.stack([jnp.concatenate(p, axis=1) for p in ctx_parts])
                other = swap(mine, "tp", bit)
                first, second = in_order(bit_of("tp", bit), mine, other)
                grown = []
                for c in range(len(ctx_parts)):
                    line = []
                    for i in range(len(ctx_parts[c])):
                        line.append(first[c][:, i * cols : (i + 1) * cols])
                        line.append(second[c][:, i * cols : (i + 1) * cols])
                    grown.append(line)
                ctx_parts = grown
        pieces.append([jnp.concatenate(p, axis=1) for p in ctx_parts])
    ordered = []
    for c in range(len(pieces[0])):
        ordered += [pieces[0][c], pieces[1][c]]
    return jnp.concatenate(ordered, axis=0)


def scatter_rows(block_of):
    count = lax.axis_size("tp")
    mine = bit_of("tp", 0)
    half = count // 2
    send = jnp.stack([block_of(2 * i + (1 - mine)) for i in range(half)]).astype(BF)
    got = swap(send, "tp", 0)
    keep = jnp.stack([block_of(2 * i + mine) for i in range(half)])
    total = (keep + got.astype(F32)).astype(BF)
    ctx_count = lax.axis_size("ctx")
    rows = total.shape[1] // ctx_count
    total = total.reshape(half, ctx_count, 2, rows // 2, total.shape[2])
    high_bits = [b for b in reversed(tp_bits()) if b > 0]
    me_ctx = lax.axis_index("ctx")
    done = []
    for index in range(2):
        part = total[:, :, index].astype(F32)
        plan = [("tp", b) for b in high_bits]
        plan = [("ctx", 0)] + plan if index == 0 else plan + [("ctx", 0)]
        for axis, bit in plan:
            if axis == "ctx":
                other = lax.dynamic_index_in_dim(part, 1 - me_ctx, 1, keepdims=True)
                own = lax.dynamic_index_in_dim(part, me_ctx, 1, keepdims=True)
                part = own + swap(other.astype(BF), "ctx", 0).astype(F32)
            else:
                b = bit_of("tp", bit)
                split = part.reshape((2, part.shape[0] // 2) + part.shape[1:])
                other = lax.dynamic_index_in_dim(split, 1 - b, 0, keepdims=False)
                own = lax.dynamic_index_in_dim(split, b, 0, keepdims=False)
                part = own + swap(other.astype(BF), "tp", bit).astype(F32)
        done.append(part[0, 0])
    return jnp.concatenate(done, axis=0)


def contract_rows(left, right):
    return lax.dot_general(
        left, right, (((0,), (0,)), ((), ())), preferred_element_type=F32
    )


def contract_cols(left, right):
    return lax.dot_general(
        left, right, (((1,), (1,)), ((), ())), preferred_element_type=F32
    )


def dot(left, right):
    return jnp.dot(left, right, preferred_element_type=F32)


def ctx_half(weight, axis):
    count = lax.axis_size("ctx")
    size = weight.shape[axis] // count
    return lax.dynamic_slice_in_dim(weight, lax.axis_index("ctx") * size, size, axis)


def after(value, token):
    value, _ = lax.optimization_barrier((value, token))
    return value


def owners(grad):
    return lax.psum_scatter(grad, "fsdp", scatter_dimension=0, tiled=False)


def trade_ctx(block, axis):
    size = block.shape[axis] // 2
    me = lax.axis_index("ctx")
    own = lax.dynamic_slice_in_dim(block, me * size, size, axis)
    give = lax.dynamic_slice_in_dim(block, (1 - me) * size, size, axis)
    got = swap(give, "ctx", 0)
    return in_order(me, own, got)


def score_block(query_heads, key_heads, first_row, block_len):
    query_block = lax.dynamic_slice_in_dim(query_heads, first_row, block_len, 0)
    scores = jnp.einsum("qhd,khd->hqk", query_block, key_heads, preferred_element_type=F32)
    scores = scores * (1.0 / math.sqrt(HD))
    key_index = jnp.arange(key_heads.shape[0], dtype=jnp.int32)
    query_index = first_row + jnp.arange(block_len, dtype=jnp.int32)
    allowed = key_index[None, :] <= query_index[:, None]
    return (query_block, jnp.where(allowed[None, :, :], scores, masked_score))


def attend_forward(qkv_heads):
    seq_len = qkv_heads.shape[0]
    head_count = qkv_heads.shape[2] // HD
    block_len = min(512, seq_len)
    block_count = seq_len // block_len
    query_heads = qkv_heads[:, 0].reshape(seq_len, head_count, HD)
    key_heads = qkv_heads[:, 1].reshape(seq_len, head_count, HD)
    value_heads = qkv_heads[:, 2].reshape(seq_len, head_count, HD)

    def one_block(block_index):
        query_block, scores = score_block(
            query_heads, key_heads, block_index * block_len, block_len
        )
        row_max = jnp.max(scores, axis=-1, keepdims=True)
        expo_vals = jnp.exp(scores - row_max)
        row_sums = jnp.sum(expo_vals, axis=-1, keepdims=True)
        soft = (expo_vals / row_sums).astype(BF)
        mixed = jnp.einsum("hqk,khd->qhd", soft, value_heads, preferred_element_type=F32)
        return (mixed.astype(BF), (row_max + jnp.log(row_sums))[:, :, 0])

    head_outs, log_norms = lax.map(one_block, jnp.arange(block_count, dtype=jnp.int32))
    return (head_outs.reshape(seq_len, head_count * HD), log_norms)


def attend_backward(qkv_heads, log_norms, grad_out):
    seq_len = qkv_heads.shape[0]
    head_count = qkv_heads.shape[2] // HD
    block_len = min(512, seq_len)
    block_count = seq_len // block_len
    score_scale = 1.0 / math.sqrt(HD)
    query_heads = qkv_heads[:, 0].reshape(seq_len, head_count, HD)
    key_heads = qkv_heads[:, 1].reshape(seq_len, head_count, HD)
    value_heads = qkv_heads[:, 2].reshape(seq_len, head_count, HD)
    grad_heads = grad_out.reshape(seq_len, head_count, HD)

    def one_block(running_grads, block_item):
        block_index, block_norms = block_item
        first_row = block_index * block_len
        query_block, scores = score_block(query_heads, key_heads, first_row, block_len)
        probs_full = jnp.exp(scores - block_norms[:, :, None])
        soft = probs_full.astype(BF)
        grad_block = lax.dynamic_slice_in_dim(grad_heads, first_row, block_len, 0)
        grad_probs = jnp.einsum(
            "qhd,khd->hqk", grad_block, value_heads, preferred_element_type=F32
        )
        weighted = jnp.sum(probs_full * grad_probs, axis=-1, keepdims=True)
        grad_scores = (probs_full * (grad_probs - weighted)).astype(BF)
        query_grad = (
            jnp.einsum("hqk,khd->qhd", grad_scores, key_heads, preferred_element_type=F32)
            * score_scale
        )
        key_grad = (
            running_grads[0]
            + jnp.einsum("hqk,qhd->khd", grad_scores, query_block, preferred_element_type=F32)
            * score_scale
        )
        value_grad = running_grads[1] + jnp.einsum(
            "hqk,qhd->khd", soft, grad_block, preferred_element_type=F32
        )
        return ((key_grad, value_grad), query_grad)

    zero_grads = jnp.zeros((seq_len, head_count, HD), F32)
    key_value, query_grads = lax.scan(
        one_block, (zero_grads, zero_grads), (jnp.arange(block_count, dtype=jnp.int32), log_norms)
    )
    flat_width = head_count * HD
    return (
        query_grads.reshape(seq_len, flat_width),
        key_value[0].reshape(seq_len, flat_width),
        key_value[1].reshape(seq_len, flat_width),
    )


def body(
    layer_input, attn_gain, qkv_weight, out_weight, ffn_gain, gate_up_weight, down_weight, cotangent
):
    n_f = lax.axis_size("fsdp")
    d_f = D // n_f
    cols = layer_input.shape[1]
    qkv_half = ctx_half(qkv_weight, 2)
    qkv_half = qkv_half.reshape(d_f, -1)
    out_half = ctx_half(out_weight, 0)
    gu_half = ctx_half(gate_up_weight, 2)
    gu_half = gu_half.reshape(d_f, -1)
    down_half = ctx_half(down_weight, 0)
    qkv_full = lax.all_gather(qkv_half, "fsdp", axis=0, tiled=True)
    out_half = after(out_half, qkv_full)
    out_full = lax.all_gather(out_half, "fsdp", axis=0, tiled=False)
    gu_half = after(gu_half, out_full)
    gu_full = lax.all_gather(gu_half, "fsdp", axis=0, tiled=True)
    down_half = after(down_half, gu_full)
    down_full = lax.all_gather(down_half, "fsdp", axis=0, tiled=False)

    input_float = layer_input.astype(F32)
    attn_scale = attn_gain.astype(F32)
    ffn_scale = ffn_gain.astype(F32)
    rms_one = lax.rsqrt(row_total(jnp.sum(input_float * input_float, axis=-1)) / D + rms_epsilon)[
        :, None
    ]
    normed_attn = (input_float * rms_one * attn_scale).astype(BF)
    attn_full = gather_rows(normed_attn)
    seq_len = attn_full.shape[0]
    proj = dot(attn_full, qkv_full)
    width = proj.shape[1] // 3
    positions = jnp.arange(seq_len, dtype=jnp.int32)
    qkv_heads = jnp.stack(
        [
            rotate(proj[:, :width], positions, 1.0),
            rotate(proj[:, width : 2 * width], positions, 1.0),
            proj[:, 2 * width :],
        ],
        axis=1,
    ).astype(BF)
    head_outs, log_norms = attend_forward(qkv_heads)

    def out_blocks(inner, full):
        joined = jnp.swapaxes(full, 0, 1).reshape(full.shape[1], lax.axis_size("tp"), cols)
        return lambda t: dot(inner, lax.dynamic_index_in_dim(joined, t, 1, keepdims=False))

    def in_blocks(grads, full):
        split = full.reshape(lax.axis_size("tp"), cols, full.shape[1])
        return lambda t: contract_cols(
            grads, lax.dynamic_index_in_dim(split, t, 0, keepdims=False)
        )

    resid = input_float + scatter_rows(out_blocks(head_outs, out_full))
    rms_two = lax.rsqrt(row_total(jnp.sum(resid * resid, axis=-1)) / D + rms_epsilon)[:, None]
    normed_ffn = (resid * rms_two * ffn_scale).astype(BF)
    ffn_full = gather_rows(normed_ffn)
    cotan_full = gather_rows(cotangent)
    gate_up = dot(ffn_full, gu_full)
    units = gate_up.shape[1] // 2
    gate = gate_up[:, :units]
    up_value = gate_up[:, units:]
    sigma = jax.nn.sigmoid(gate)
    hidden = (gate * sigma * up_value).astype(BF)
    down_part = contract_rows(hidden, cotan_full).astype(BF)
    down_sum = owners(jnp.swapaxes(down_part.reshape(units, n_f, d_f), 0, 1))

    layer_output = (resid + scatter_rows(out_blocks(hidden, down_full))).astype(BF)
    down_rows = jnp.swapaxes(down_full, 0, 1).reshape(units, D)
    grad_hidden = contract_cols(cotan_full, down_rows)
    grad_gu = jnp.concatenate(
        [grad_hidden * up_value * sigma * (1.0 + gate * (1.0 - sigma)), grad_hidden * gate * sigma],
        axis=1,
    ).astype(BF)
    gu_part = contract_rows(ffn_full, grad_gu).astype(BF)
    gu_part = after(gu_part, down_sum)
    gu_sum = owners(gu_part.reshape(n_f, d_f, -1))
    grad_nffn = scatter_rows(in_blocks(grad_gu, gu_full))
    ffn_term = grad_nffn * ffn_scale
    ffn_dot = row_total(jnp.sum(ffn_term * resid, axis=-1))[:, None]
    grad_resid = cotangent.astype(F32) + rms_two * ffn_term - resid * rms_two**3 * ffn_dot / D
    ffn_gain_part = jnp.sum(grad_nffn * resid * rms_two, axis=0)
    grad_branch = grad_resid.astype(BF)
    branch_full = gather_rows(grad_branch)
    out_rows = jnp.swapaxes(out_full, 0, 1).reshape(out_full.shape[1], D)
    grad_heads = contract_cols(branch_full, out_rows).astype(BF)
    out_part = contract_rows(head_outs, branch_full).astype(BF)
    out_part = after(out_part, gu_sum)
    out_sum = owners(jnp.swapaxes(out_part.reshape(-1, n_f, d_f), 0, 1))
    query_grad, key_grad, value_grad = attend_backward(qkv_heads, log_norms, grad_heads)
    grad_proj = jnp.concatenate(
        [rotate(query_grad, positions, -1.0), rotate(key_grad, positions, -1.0), value_grad],
        axis=1,
    ).astype(BF)
    qkv_part = contract_rows(attn_full, grad_proj).astype(BF)
    qkv_sum = owners(qkv_part.reshape(n_f, d_f, -1))
    grad_nattn = scatter_rows(in_blocks(grad_proj, qkv_full))
    attn_term = grad_nattn * attn_scale
    attn_dot = row_total(jnp.sum(attn_term * input_float, axis=-1))[:, None]
    grad_input = grad_resid + rms_one * attn_term - input_float * rms_one**3 * attn_dot / D
    attn_gain_part = jnp.sum(grad_nattn * input_float * rms_one, axis=0)
    gain_grads = lax.psum((attn_gain_part, ffn_gain_part), ("fsdp", "ctx"))

    def in_grad(block, count):
        first, second = trade_ctx(block, 0)
        rows = first.shape[0]
        return jnp.concatenate(
            [first.reshape(rows, count, -1), second.reshape(rows, count, -1)], axis=2
        ).astype(F32)

    def out_grad(block):
        return jnp.concatenate(trade_ctx(block, 1), axis=0).astype(F32)

    return (
        layer_output,
        grad_input,
        gain_grads[0],
        in_grad(qkv_sum, 3),
        out_grad(out_sum),
        gain_grads[1],
        in_grad(gu_sum, 2),
        out_grad(down_sum),
    )


def solution(mesh):
    return jax.shard_map(
        body,
        mesh=mesh,
        in_specs=(
            P(("fsdp", "ctx"), "tp"),
            P("tp"),
            P("fsdp", None, "tp"),
            P("tp", "fsdp"),
            P("tp"),
            P("fsdp", None, "tp"),
            P("tp", "fsdp"),
            P(("fsdp", "ctx"), "tp"),
        ),
        out_specs=(
            P(("fsdp", "ctx"), "tp"),
            P(("fsdp", "ctx"), "tp"),
            P("tp"),
            P(("fsdp", "ctx"), None, "tp"),
            P("tp", ("fsdp", "ctx")),
            P("tp"),
            P(("fsdp", "ctx"), None, "tp"),
            P("tp", ("fsdp", "ctx")),
        ),
        check_vma=False,
    )
```

```python
import math

import jax
import jax.numpy as jnp
from jax import lax
from jax.experimental import pallas as pl
from jax.experimental.layout import Layout, with_layout_constraint
from jax.experimental.pallas import tpu as pltpu
from jax.sharding import PartitionSpec as P

D = 4096
HD = 128
BF = jnp.bfloat16
F32 = jnp.float32
rms_epsilon = 1e-05
NT = (((1,), (1,)), ((), ()))
LOG2E = 1.4426950408889634


def mm(left, right, dims=(((1,), (0,)), ((), ()))):
    return lax.dot_general(left, right, dims, preferred_element_type=F32)


def turn(values, cosine, sine):
    return values * cosine + pltpu.roll(values, HD // 2, 1) * sine


def rope_tables(seq_len):
    half_width = HD // 2
    inv_freq = jnp.exp(-math.log(10000.0) * jnp.arange(half_width, dtype=F32) * 2.0 / HD)
    angles = jnp.arange(seq_len, dtype=F32)[:, None] * inv_freq[None, :]
    cosine, sine = jnp.cos(angles), jnp.sin(angles)
    return jnp.concatenate([cosine, cosine], axis=1), jnp.concatenate([-sine, sine], axis=1)


def attend_forward(query_proj, key_proj, value_proj, cosine, sine):
    seq_len = query_proj.shape[0]
    heads = query_proj.shape[1] // HD
    block = min(512, seq_len)
    blocks = seq_len // block
    scale = LOG2E / math.sqrt(HD)

    def kernel(q_in, k_in, v_in, cos_q, sin_q, cos_k, sin_k, q_out, k_out, v_out, out, norm, vt):
        i = pl.program_id(1)

        @pl.when(i == 0)
        def _():
            for j in range(blocks):
                rows = pl.ds(j * block, block)
                k_out[rows, :] = turn(k_in[rows, :], cos_k[rows, :], sin_k[rows, :]).astype(BF)
                v_out[rows, :] = v_in[rows, :].astype(BF)
                vt[j] = v_in[rows, :].T.astype(BF)

        q_out[...] = turn(q_in[...], cos_q[...], sin_q[...]).astype(BF)
        query = q_out[...]

        def step(j, carry, diagonal):
            top, total, mixed = carry
            rows = pl.ds(pl.multiple_of(j * block, block), block)
            scores = mm(k_out[rows, :], query, NT) * scale
            if diagonal:
                key_at = lax.broadcasted_iota(jnp.int32, scores.shape, 0)
                query_at = lax.broadcasted_iota(jnp.int32, scores.shape, 1)
                scores = jnp.where(key_at <= query_at, scores, -1e30)
            new_top = jnp.maximum(top, jnp.max(scores, axis=0, keepdims=True))
            expo = jnp.exp2(scores - new_top)
            fade = jnp.exp2(top - new_top)
            total = total * fade + jnp.sum(expo, axis=0, keepdims=True)
            mixed = mixed * fade + mm(vt[j], expo.astype(BF))
            return new_top, total, mixed

        carry = (
            jnp.full((1, block), -1e30, F32),
            jnp.zeros((1, block), F32),
            jnp.zeros((HD, block), F32),
        )
        carry = lax.fori_loop(0, i, lambda j, c: step(j, c, False), carry)
        top, total, mixed = step(i, carry, True)
        out[...] = (mixed / total).T.astype(BF)
        norm[0] = top + jnp.log2(total)

    row = pl.BlockSpec((block, HD), lambda h, i: (i, h))
    col = pl.BlockSpec((seq_len, HD), lambda h, i: (0, h))
    pos = pl.BlockSpec((block, HD), lambda h, i: (i, 0))
    all_pos = pl.BlockSpec((seq_len, HD), lambda h, i: (0, 0))
    wide = jax.ShapeDtypeStruct((seq_len, heads * HD), BF)
    pairs = heads * seq_len * (seq_len + block) // 2
    return pl.pallas_call(
        kernel,
        grid=(heads, blocks),
        in_specs=[row, col, col, pos, pos, all_pos, all_pos],
        out_specs=[row, col, col, row, pl.BlockSpec((1, 1, block), lambda h, i: (h, 0, i))],
        out_shape=[wide, wide, wide, wide, jax.ShapeDtypeStruct((heads, 1, seq_len), F32)],
        scratch_shapes=[pltpu.VMEM((blocks, HD, block), BF)],
        compiler_params=pltpu.CompilerParams(vmem_limit_bytes=48 << 20),
        cost_estimate=pl.CostEstimate(
            flops=4 * pairs * HD,
            transcendentals=pairs,
            bytes_accessed=seq_len * heads * HD * (12 + 8),
        ),
    )(query_proj, key_proj, value_proj, cosine, sine, cosine, sine)


def attend_backward(queries, keys, values, outs, norms, grads, cosine, sine):
    seq_len = queries.shape[0]
    heads = queries.shape[1] // HD
    block = min(512, seq_len)
    blocks = seq_len // block
    root = 1.0 / math.sqrt(HD)
    scale = LOG2E * root

    def kernel(q, k, v, o, g, norm, cos_q, sin_q, cos_k, sin_k, dq, dk, dv, kt, dk_sum, dv_sum):
        i = pl.program_id(1)

        @pl.when(i == 0)
        def _():
            for j in range(blocks):
                rows = pl.ds(j * block, block)
                kt[j] = k[rows, :].astype(F32).T.astype(BF)
            dk_sum[...] = jnp.zeros_like(dk_sum)
            dv_sum[...] = jnp.zeros_like(dv_sum)

        query = q[...]
        grad = g[...]
        dots = (grad.astype(F32) * o[...].astype(F32)).T
        weighted = jnp.sum(dots, axis=0, keepdims=True)
        level = norm[0]

        def step(j, total, diagonal):
            rows = pl.ds(pl.multiple_of(j * block, block), block)
            scores = mm(k[rows, :], query, NT) * scale
            probs = jnp.exp2(scores - level)
            if diagonal:
                key_at = lax.broadcasted_iota(jnp.int32, scores.shape, 0)
                query_at = lax.broadcasted_iota(jnp.int32, scores.shape, 1)
                probs = jnp.where(key_at <= query_at, probs, 0.0)
            dv_sum[rows, :] += mm(probs.astype(BF), grad)
            d_probs = mm(v[rows, :], grad, NT)
            d_scores = (probs * (d_probs - weighted)).astype(BF)
            dk_sum[rows, :] += mm(d_scores, query)
            return total + mm(kt[j], d_scores)

        total = lax.fori_loop(
            0, i, lambda j, c: step(j, c, False), jnp.zeros((HD, block), F32)
        )
        total = step(i, total, True)
        dq[...] = turn(total.T * root, cos_q[...], -sin_q[...]).astype(BF)

        @pl.when(i == blocks - 1)
        def _():
            for j in range(blocks):
                rows = pl.ds(j * block, block)
                dk[rows, :] = turn(
                    dk_sum[rows, :] * root, cos_k[rows, :], -sin_k[rows, :]
                ).astype(BF)
                dv[rows, :] = dv_sum[rows, :].astype(BF)

    row = pl.BlockSpec((block, HD), lambda h, i: (i, h))
    col = pl.BlockSpec((seq_len, HD), lambda h, i: (0, h))
    pos = pl.BlockSpec((block, HD), lambda h, i: (i, 0))
    all_pos = pl.BlockSpec((seq_len, HD), lambda h, i: (0, 0))
    wide = jax.ShapeDtypeStruct((seq_len, heads * HD), BF)
    pairs = heads * seq_len * (seq_len + block) // 2
    return pl.pallas_call(
        kernel,
        grid=(heads, blocks),
        in_specs=[row, col, col, row, row, pl.BlockSpec((1, 1, block), lambda h, i: (h, 0, i)),
                  pos, pos, all_pos, all_pos],
        out_specs=[row, col, col],
        out_shape=[wide, wide, wide],
        scratch_shapes=[
            pltpu.VMEM((blocks, HD, block), BF),
            pltpu.VMEM((seq_len, HD), F32),
            pltpu.VMEM((seq_len, HD), F32),
        ],
        compiler_params=pltpu.CompilerParams(vmem_limit_bytes=48 << 20),
        cost_estimate=pl.CostEstimate(
            flops=10 * pairs * HD,
            transcendentals=pairs,
            bytes_accessed=seq_len * heads * HD * 16,
        ),
    )(queries, keys, values, outs, grads, norms, cosine, sine, cosine, sine)


def row_total(values):
    return lax.psum(values, "tp")


def swap(values, axis, bit):
    step = 1 << bit
    return lax.ppermute(values, axis, [(i, i ^ step) for i in range(lax.axis_size(axis))])


def high_bits():
    return list(range(1, lax.axis_size("tp").bit_length() - 1))[::-1]


def gather_rows(values):
    rows, cols = values.shape
    half = rows // 2
    n_t, n_c = lax.axis_size("tp"), lax.axis_size("ctx")
    me_t, me_c = lax.axis_index("tp"), lax.axis_index("ctx")
    across = [("tp", b) for b in high_bits()]
    full = jnp.zeros((n_t, n_c * rows, cols), values.dtype)
    for part, plan in enumerate(([("ctx", 0)] + across, across + [("ctx", 0)])):
        held = {(0, 0): values[part * half : (part + 1) * half]}
        for axis, bit in plan + [("tp", 0)]:
            for (dc, dt), piece in list(held.items()):
                key = (1, dt) if axis == "ctx" else (dc, dt | (1 << bit))
                held[key] = swap(piece, axis, bit)
        for (dc, dt), piece in held.items():
            start = (me_t ^ dt, (me_c ^ dc) * rows + part * half, 0)
            full = lax.dynamic_update_slice(full, piece[None], start)
    return with_layout_constraint(full, Layout((0, 1, 2)))


def scatter_rows(block_of):
    n_t, n_c = lax.axis_size("tp"), lax.axis_size("ctx")
    me_t, me_c = lax.axis_index("tp"), lax.axis_index("ctx")
    sums = {}
    for dt in range(0, n_t, 2):
        got = swap(block_of(me_t ^ (dt + 1)).astype(BF), "tp", 0)
        sums[dt] = (block_of(me_t ^ dt) + got.astype(F32)).astype(BF)
    rows = sums[0].shape[0] // n_c
    cols = sums[0].shape[1]
    half = rows // 2
    across = [("tp", b) for b in high_bits()]
    done = []
    for part, plan in enumerate(([("ctx", 0)] + across, across + [("ctx", 0)])):
        held = {}
        for dt, total in sums.items():
            split = total.reshape(n_c, rows, cols)[:, part * half : (part + 1) * half]
            for dc in range(n_c):
                held[(dc, dt)] = lax.dynamic_index_in_dim(split, me_c ^ dc, 0, keepdims=False)
        for axis, bit in plan:
            left = {}
            for (dc, dt), piece in held.items():
                give = dc == 1 if axis == "ctx" else (dt >> bit) & 1
                if not give:
                    away = (1, dt) if axis == "ctx" else (dc, dt | (1 << bit))
                    got = swap(held[away].astype(BF), axis, bit)
                    left[(dc, dt)] = piece.astype(F32) + got.astype(F32)
            held = left
        done.append(held[(0, 0)])
    return jnp.concatenate(done, axis=0)


def ctx_half(weight, axis):
    size = weight.shape[axis] // lax.axis_size("ctx")
    return lax.dynamic_slice_in_dim(weight, lax.axis_index("ctx") * size, size, axis)


def after(value, token):
    value, _ = lax.optimization_barrier((value, token))
    return value


def owners(grad):
    return lax.psum_scatter(grad, "fsdp", scatter_dimension=0, tiled=False)


def spread(weight):
    return lax.all_gather(weight, "fsdp", axis=0, tiled=False)


def trade_ctx(block, axis):
    size = block.shape[axis] // lax.axis_size("ctx")
    me = lax.axis_index("ctx")
    own = lax.dynamic_slice_in_dim(block, me * size, size, axis)
    give = lax.dynamic_slice_in_dim(block, (1 - me) * size, size, axis)
    got = swap(give, "ctx", 0)
    return jnp.where(me == 0, own, got), jnp.where(me == 0, got, own)


def out_grad(block):
    return jnp.concatenate(trade_ctx(block, 1), axis=0).astype(F32)


def total_rows(values):
    values = values + swap(values, "ctx", 0)
    for bit in range(lax.axis_size("fsdp").bit_length() - 1):
        values = values + swap(values, "fsdp", bit)
    return values


def body(
    layer_input, attn_gain, qkv_weight, out_weight, ffn_gain, gate_up_weight, down_weight, cotangent
):
    n_f = lax.axis_size("fsdp")
    d_f = D // n_f
    qkv_parts = [spread(ctx_half(qkv_weight[:, i], 1)) for i in range(3)]
    out_full = spread(ctx_half(out_weight, 0))
    gu_full = spread(ctx_half(gate_up_weight, 2).reshape(d_f, -1))
    down_full = spread(ctx_half(down_weight, 0))

    def into(full, weight):
        return mm(full, weight, (((0, 2), (0, 1)), ((), ())))

    def back_out(full, weight):
        return mm(full, weight, (((0, 2), (0, 2)), ((), ())))

    def out_blocks(inner, weight):
        return lambda t: mm(inner, lax.dynamic_index_in_dim(weight, t, 0, keepdims=False))

    def in_blocks(grads, weight):
        return lambda t: mm(grads, lax.dynamic_index_in_dim(weight, t, 0, keepdims=False), NT)

    def in_part(full, grads):
        return mm(full, grads, (((1,), (0,)), ((), ()))).astype(BF)

    def out_part(inner, full):
        return jnp.stack(
            [mm(inner, full[t], (((0,), (0,)), ((), ()))).astype(BF) for t in range(n_f)]
        )

    input_float = layer_input.astype(F32)
    attn_scale = attn_gain.astype(F32)
    ffn_scale = ffn_gain.astype(F32)
    rms_one = lax.rsqrt(row_total(jnp.sum(input_float * input_float, axis=-1)) / D + rms_epsilon)[
        :, None
    ]
    normed_attn = (input_float * rms_one * attn_scale).astype(BF)
    attn_full = gather_rows(normed_attn)
    seq_len = attn_full.shape[1]
    cosine, sine = rope_tables(seq_len)
    cotan_full = gather_rows(after(cotangent, attn_full))
    proj = [into(attn_full, part) for part in qkv_parts]
    queries, keys, values, head_outs, norms = attend_forward(*proj, cosine, sine)
    resid = input_float + scatter_rows(out_blocks(head_outs, out_full))
    rms_two = lax.rsqrt(row_total(jnp.sum(resid * resid, axis=-1)) / D + rms_epsilon)[:, None]
    normed_ffn = (resid * rms_two * ffn_scale).astype(BF)
    ffn_full = gather_rows(normed_ffn)
    gate_up = into(ffn_full, gu_full)
    units = gate_up.shape[1] // 2
    gate = gate_up[:, :units]
    up_value = gate_up[:, units:]
    sigma = jax.nn.sigmoid(gate)
    hidden = (gate * sigma * up_value).astype(BF)
    down_part = out_part(hidden, cotan_full)
    down_sum = owners(down_part)
    down_full = after(down_full, down_part)
    grad_hidden = back_out(cotan_full, down_full)
    grad_gu = jnp.concatenate(
        [grad_hidden * up_value * sigma * (1.0 + gate * (1.0 - sigma)), grad_hidden * gate * sigma],
        axis=1,
    ).astype(BF)
    gu_part = in_part(ffn_full, grad_gu)
    gu_sum = owners(after(gu_part, down_sum))
    grad_nffn = after(scatter_rows(in_blocks(grad_gu, gu_full)), (gu_part, down_sum))
    ffn_term = grad_nffn * ffn_scale
    ffn_dot = row_total(jnp.sum(ffn_term * resid, axis=-1))[:, None]
    grad_resid = cotangent.astype(F32) + rms_two * ffn_term - resid * rms_two**3 * ffn_dot / D
    ffn_gain_part = jnp.sum(grad_nffn * resid * rms_two, axis=0)
    grad_branch = grad_resid.astype(BF)
    branch_full = gather_rows(grad_branch)
    grad_heads = back_out(branch_full, out_full).astype(BF)
    out_sum = owners(out_part(head_outs, branch_full))
    grad_proj = attend_backward(
        queries, keys, values, head_outs, norms, grad_heads, cosine, sine
    )
    qkv_part = [in_part(attn_full, grad) for grad in grad_proj]
    qkv_sum = [owners(part) for part in qkv_part]
    grad_nattn = scatter_rows(
        in_blocks(jnp.concatenate(grad_proj, axis=1), jnp.concatenate(qkv_parts, axis=2))
    )
    hidden = after(hidden, qkv_part)
    layer_output = (resid + scatter_rows(out_blocks(hidden, down_full))).astype(BF)
    attn_term = grad_nattn * attn_scale
    attn_dot = row_total(jnp.sum(attn_term * input_float, axis=-1))[:, None]
    grad_input = grad_resid + rms_one * attn_term - input_float * rms_one**3 * attn_dot / D
    attn_gain_part = jnp.sum(grad_nattn * input_float * rms_one, axis=0)
    gain_grads = total_rows(jnp.stack([attn_gain_part, ffn_gain_part]))

    down_grad = out_grad(down_sum)
    rows, other_rows = trade_ctx(gu_sum, 0)
    gu_grad = jnp.concatenate(
        [v.reshape(v.shape[0], 2, -1) for v in (rows, other_rows)], axis=2
    ).astype(F32)
    out_weight_grad = out_grad(out_sum)
    done = (down_grad, out_weight_grad, gu_grad, grad_input, layer_output, gain_grads)
    qkv_grad = []
    for part in qkv_sum:
        qkv_grad.append(jnp.concatenate(trade_ctx(after(part, done), 0), axis=1).astype(F32))
        done = done + (qkv_grad[-1],)
    qkv_grad = jnp.stack(qkv_grad, axis=1)

    return (
        layer_output,
        grad_input,
        gain_grads[0],
        qkv_grad,
        out_weight_grad,
        gain_grads[1],
        gu_grad,
        down_grad,
    )


def solution(mesh):
    return jax.shard_map(
        body,
        mesh=mesh,
        in_specs=(
            P(("fsdp", "ctx"), "tp"),
            P("tp"),
            P("fsdp", None, "tp"),
            P("tp", "fsdp"),
            P("tp"),
            P("fsdp", None, "tp"),
            P("tp", "fsdp"),
            P(("fsdp", "ctx"), "tp"),
        ),
        out_specs=(
            P(("fsdp", "ctx"), "tp"),
            P(("fsdp", "ctx"), "tp"),
            P("tp"),
            P(("fsdp", "ctx"), None, "tp"),
            P("tp", ("fsdp", "ctx")),
            P("tp"),
            P(("fsdp", "ctx"), None, "tp"),
            P("tp", ("fsdp", "ctx")),
        ),
        check_vma=False,
    )
```

```python
import math

import jax
import jax.numpy as jnp
from jax import lax
from jax.experimental import pallas as pl
from jax.experimental.layout import Layout, with_layout_constraint
from jax.experimental.pallas import tpu as pltpu
from jax.sharding import PartitionSpec as P

D = 4096
HD = 128
BF = jnp.bfloat16
F32 = jnp.float32
rms_epsilon = 1e-05
NT = (((1,), (1,)), ((), ()))
LOG2E = 1.4426950408889634


def mm(left, right, dims=(((1,), (0,)), ((), ()))):
    return lax.dot_general(left, right, dims, preferred_element_type=F32)


def turn(values, cosine, sine):
    return values * cosine + pltpu.roll(values, HD // 2, 1) * sine


def rope_tables(seq_len):
    half_width = HD // 2
    inv_freq = jnp.exp(-math.log(10000.0) * jnp.arange(half_width, dtype=F32) * 2.0 / HD)
    angles = jnp.arange(seq_len, dtype=F32)[:, None] * inv_freq[None, :]
    cosine, sine = jnp.cos(angles), jnp.sin(angles)
    return jnp.concatenate([cosine, cosine], axis=1), jnp.concatenate([-sine, sine], axis=1)


def attend_forward(query_proj, key_proj, value_proj, cosine, sine):
    seq_len = query_proj.shape[0]
    heads = query_proj.shape[1] // HD
    block = min(512, seq_len)
    blocks = seq_len // block
    scale = LOG2E / math.sqrt(HD)

    def kernel(q_in, k_in, v_in, cos_q, sin_q, cos_k, sin_k, q_out, k_out, v_out, out, norm, vt):
        i = pl.program_id(1)

        @pl.when(i == 0)
        def _():
            for j in range(blocks):
                rows = pl.ds(j * block, block)
                k_out[rows, :] = turn(k_in[rows, :], cos_k[rows, :], sin_k[rows, :]).astype(BF)
                v_out[rows, :] = v_in[rows, :].astype(BF)
                vt[j] = v_in[rows, :].T.astype(BF)

        q_out[...] = turn(q_in[...], cos_q[...], sin_q[...]).astype(BF)
        query = q_out[...]

        def step(j, carry, diagonal):
            top, total, mixed = carry
            rows = pl.ds(pl.multiple_of(j * block, block), block)
            scores = mm(k_out[rows, :], query, NT) * scale
            if diagonal:
                key_at = lax.broadcasted_iota(jnp.int32, scores.shape, 0)
                query_at = lax.broadcasted_iota(jnp.int32, scores.shape, 1)
                scores = jnp.where(key_at <= query_at, scores, -1e30)
            new_top = jnp.maximum(top, jnp.max(scores, axis=0, keepdims=True))
            expo = jnp.exp2(scores - new_top)
            fade = jnp.exp2(top - new_top)
            total = total * fade + jnp.sum(expo, axis=0, keepdims=True)
            mixed = mixed * fade + mm(vt[j], expo.astype(BF))
            return new_top, total, mixed

        carry = (
            jnp.full((1, block), -1e30, F32),
            jnp.zeros((1, block), F32),
            jnp.zeros((HD, block), F32),
        )
        carry = lax.fori_loop(0, i, lambda j, c: step(j, c, False), carry)
        top, total, mixed = step(i, carry, True)
        out[...] = (mixed / total).T.astype(BF)
        norm[0] = top + jnp.log2(total)

    row = pl.BlockSpec((block, HD), lambda h, i: (i, h))
    col = pl.BlockSpec((seq_len, HD), lambda h, i: (0, h))
    pos = pl.BlockSpec((block, HD), lambda h, i: (i, 0))
    all_pos = pl.BlockSpec((seq_len, HD), lambda h, i: (0, 0))
    wide = jax.ShapeDtypeStruct((seq_len, heads * HD), BF)
    pairs = heads * seq_len * (seq_len + block) // 2
    return pl.pallas_call(
        kernel,
        grid=(heads, blocks),
        in_specs=[row, col, col, pos, pos, all_pos, all_pos],
        out_specs=[row, col, col, row, pl.BlockSpec((1, 1, block), lambda h, i: (h, 0, i))],
        out_shape=[wide, wide, wide, wide, jax.ShapeDtypeStruct((heads, 1, seq_len), F32)],
        scratch_shapes=[pltpu.VMEM((blocks, HD, block), BF)],
        compiler_params=pltpu.CompilerParams(vmem_limit_bytes=48 << 20),
        cost_estimate=pl.CostEstimate(
            flops=30 * pairs * HD,
            transcendentals=pairs,
            bytes_accessed=seq_len * heads * HD * (12 + 8),
        ),
    )(query_proj, key_proj, value_proj, cosine, sine, cosine, sine)


def attend_backward(queries, keys, values, outs, norms, grads, cosine, sine):
    seq_len = queries.shape[0]
    heads = queries.shape[1] // HD
    block = min(512, seq_len)
    blocks = seq_len // block
    root = 1.0 / math.sqrt(HD)
    scale = LOG2E * root

    def kernel(q, k, v, o, g, norm, cos_q, sin_q, cos_k, sin_k, dq, dk, dv, kt, dk_sum, dv_sum):
        i = pl.program_id(1)

        @pl.when(i == 0)
        def _():
            for j in range(blocks):
                rows = pl.ds(j * block, block)
                kt[j] = k[rows, :].astype(F32).T.astype(BF)
            dk_sum[...] = jnp.zeros_like(dk_sum)
            dv_sum[...] = jnp.zeros_like(dv_sum)

        query = q[...]
        grad = g[...]
        dots = (grad.astype(F32) * o[...].astype(F32)).T
        weighted = jnp.sum(dots, axis=0, keepdims=True)
        level = norm[0]

        def step(j, total, diagonal):
            rows = pl.ds(pl.multiple_of(j * block, block), block)
            scores = mm(k[rows, :], query, NT) * scale
            probs = jnp.exp2(scores - level)
            if diagonal:
                key_at = lax.broadcasted_iota(jnp.int32, scores.shape, 0)
                query_at = lax.broadcasted_iota(jnp.int32, scores.shape, 1)
                probs = jnp.where(key_at <= query_at, probs, 0.0)
            dv_sum[rows, :] += mm(probs.astype(BF), grad)
            d_probs = mm(v[rows, :], grad, NT)
            d_scores = (probs * (d_probs - weighted)).astype(BF)
            dk_sum[rows, :] += mm(d_scores, query)
            return total + mm(kt[j], d_scores)

        total = lax.fori_loop(
            0, i, lambda j, c: step(j, c, False), jnp.zeros((HD, block), F32)
        )
        total = step(i, total, True)
        dq[...] = turn(total.T * root, cos_q[...], -sin_q[...]).astype(BF)

        @pl.when(i == blocks - 1)
        def _():
            for j in range(blocks):
                rows = pl.ds(j * block, block)
                dk[rows, :] = turn(
                    dk_sum[rows, :] * root, cos_k[rows, :], -sin_k[rows, :]
                ).astype(BF)
                dv[rows, :] = dv_sum[rows, :].astype(BF)

    row = pl.BlockSpec((block, HD), lambda h, i: (i, h))
    col = pl.BlockSpec((seq_len, HD), lambda h, i: (0, h))
    pos = pl.BlockSpec((block, HD), lambda h, i: (i, 0))
    all_pos = pl.BlockSpec((seq_len, HD), lambda h, i: (0, 0))
    wide = jax.ShapeDtypeStruct((seq_len, heads * HD), BF)
    pairs = heads * seq_len * (seq_len + block) // 2
    return pl.pallas_call(
        kernel,
        grid=(heads, blocks),
        in_specs=[row, col, col, row, row, pl.BlockSpec((1, 1, block), lambda h, i: (h, 0, i)),
                  pos, pos, all_pos, all_pos],
        out_specs=[row, col, col],
        out_shape=[wide, wide, wide],
        scratch_shapes=[
            pltpu.VMEM((blocks, HD, block), BF),
            pltpu.VMEM((seq_len, HD), F32),
            pltpu.VMEM((seq_len, HD), F32),
        ],
        compiler_params=pltpu.CompilerParams(vmem_limit_bytes=48 << 20),
        cost_estimate=pl.CostEstimate(
            flops=38 * pairs * HD,
            transcendentals=pairs,
            bytes_accessed=seq_len * heads * HD * 16,
        ),
    )(queries, keys, values, outs, grads, norms, cosine, sine, cosine, sine)


def row_total(values):
    return lax.psum(values, "tp")


def flip(axis, bit):
    step = 1 << bit
    return [(i, i ^ step) for i in range(lax.axis_size(axis))]


def swap(values, axis, bit):
    return lax.ppermute(values, axis, flip(axis, bit))


def at_bit(axis, bit):
    return (lax.axis_index(axis) >> bit) & 1


def tp_high():
    return [("tp", b) for b in range(1, lax.axis_size("tp").bit_length() - 1)][::-1]


def cut(rows, count):
    step = -(-rows // (16 * count)) * 16
    edges = [min(i * step, rows) for i in range(count)] + [rows]
    return list(zip(edges[:-1], edges[1:]))


def turns(links):
    return [links[i:] + links[:i] for i in range(len(links))]


def pinned(values):
    return with_layout_constraint(values, Layout(tuple(range(values.ndim))))


def spot(shift):
    block = lax.axis_index("tp")
    row = lax.axis_index("ctx")
    for axis, bit in shift:
        if axis == "tp":
            block = block ^ (1 << bit)
        elif axis == "ctx":
            row = row ^ 1
    return block, row


def gather_rows(values):
    rows, cols = values.shape
    links = [("ctx", 0)] + tp_high()
    full = jnp.zeros((lax.axis_size("tp"), lax.axis_size("ctx") * rows, cols), values.dtype)
    orders = turns(links)
    for (low, high), order in zip(cut(rows, len(orders)), orders):
        held = {frozenset(): values[low:high]}
        for link in order + [("tp", 0)]:
            for shift, piece in list(held.items()):
                held[shift | {link}] = swap(piece, *link)
        for shift, piece in held.items():
            block, row = spot(shift)
            full = lax.dynamic_update_slice(full, piece[None], (block, row * rows + low, 0))
    return pinned(full)


def gather_pair(values, token=None):
    rows, cols = values.shape
    n_c = lax.axis_size("ctx")
    links = [("ctx", 0)] + tp_high() + [("fsdp", 0)]
    full = jnp.zeros((lax.axis_size("tp") // 2, 2 * n_c * rows, cols), values.dtype)
    orders = turns(links)
    for (low, high), order in zip(cut(rows, len(orders)), orders):
        held = {frozenset(): values[low:high]}
        for turn, link in enumerate(order):
            if turn == 1 and token is not None:
                held = dict(zip(held, after(list(held.values()), token)))
            for shift, piece in list(held.items()):
                held[shift | {link}] = swap(piece, *link)
        for shift, piece in held.items():
            block, row = spot(shift)
            plane = at_bit("fsdp", 0) ^ (("fsdp", 0) in shift)
            start = (block >> 1, (plane * n_c + row) * rows + low, 0)
            full = lax.dynamic_update_slice(full, piece[None], start)
    full = pinned(full)
    return full, pinned(swap(full, "tp", 0))


def lower(values):
    return values.astype(BF)


def scatter_sums(sums, links):
    high = tp_high()
    rows = sums[0].shape[-2]
    n_rows = sums[0].ndim - 2
    plan = [(link, i) for i, link in enumerate(high)]
    plan += [(link, len(high) + i) for i, link in enumerate(links)]
    orders = turns(plan)
    done = []
    for (low, top), order in zip(cut(rows, len(orders)), orders):
        part = jnp.stack([s[..., low:top, :] for s in sums])
        part = part.reshape((2,) * len(high) + part.shape[1:])
        for link, dim in order:
            me = at_bit(*link)
            give = lax.dynamic_index_in_dim(part, 1 - me, dim, keepdims=True)
            keep = lax.dynamic_index_in_dim(part, me, dim, keepdims=True)
            part = keep.astype(F32) + swap(lower(give), *link).astype(F32)
        done.append(part.reshape(part.shape[-2:]))
    return jnp.concatenate(done, axis=0)


def scatter_rows(block_of):
    n_c = lax.axis_size("ctx")
    core = at_bit("tp", 0)
    sums = []
    for i in range(lax.axis_size("tp") // 2):
        got = swap(lower(block_of(2 * i + 1 - core)), "tp", 0)
        total = lower(block_of(2 * i + core) + got.astype(F32))
        sums.append(total.reshape(n_c, -1, total.shape[-1]))
    return scatter_sums(sums, [("ctx", 0)])


def scatter_pair(own_block, other_block):
    n_c = lax.axis_size("ctx")
    sums = []
    for i in range(lax.axis_size("tp") // 2):
        got = swap(lower(other_block(i)), "tp", 0)
        total = lower(own_block(i) + got.astype(F32))
        sums.append(total.reshape(2, n_c, -1, total.shape[-1]))
    return scatter_sums(sums, [("fsdp", 0), ("ctx", 0)])


def share(weight, axis, index, count):
    size = weight.shape[axis] // count
    return lax.dynamic_slice_in_dim(weight, index * size, size, axis)


def after(value, token):
    value, _ = lax.optimization_barrier((value, token))
    return value


def owners(grad):
    return lax.psum_scatter(grad, "fsdp", scatter_dimension=0, tiled=False)


def spread(weight):
    return lax.all_gather(weight, "fsdp", axis=0, tiled=False)


def far_groups():
    count = lax.axis_size("fsdp")
    return [list(range(i, count, 2)) for i in range(2)]


def far_owners(grad):
    return lax.psum_scatter(
        grad, "fsdp", scatter_dimension=0, tiled=False, axis_index_groups=far_groups()
    )


def far_spread(weight):
    return lax.all_gather(weight, "fsdp", axis=0, tiled=False, axis_index_groups=far_groups())


def pair_share(block, axis, token, hold):
    n_c = lax.axis_size("ctx")
    place = lax.axis_index("ctx") * 2
    plane = at_bit("fsdp", 0)
    mine = share(block, axis, place + plane, 2 * n_c)
    near = swap(after(share(block, axis, place + 1 - plane, 2 * n_c), token), "fsdp", 0)
    near = after(near, hold)
    same = at_bit("tp", 0) == plane
    return jnp.where(same, mine, near), jnp.where(same, near, mine)


def pair_grad(own, other, axis):
    plane = at_bit("fsdp", 0)
    same = at_bit("tp", 0) == plane
    mine = jnp.where(same, own, other)
    near = swap(jnp.where(same, other, own), "fsdp", 0)
    pair = jnp.stack(
        [jnp.where(plane == 0, mine, near), jnp.where(plane == 0, near, mine)]
    )
    return [v[i] for v in trade_ctx(pair, axis + 1) for i in range(2)]


def trade_ctx(block, axis):
    n_c = lax.axis_size("ctx")
    me = lax.axis_index("ctx")
    own = share(block, axis, me, n_c)
    got = swap(share(block, axis, 1 - me, n_c), "ctx", 0)
    return jnp.where(me == 0, own, got), jnp.where(me == 0, got, own)


def total_rows(values):
    values = values + swap(values, "ctx", 0)
    for bit in range(lax.axis_size("fsdp").bit_length() - 1):
        values = values + swap(values, "fsdp", bit)
    return values


def into(full, weight):
    return mm(full, weight, (((0, 2), (0, 1)), ((), ())))


def back_out(full, weight):
    return mm(full, weight, (((0, 2), (0, 2)), ((), ())))


def in_part(full, grads):
    return lower(mm(full, grads, (((1,), (0,)), ((), ()))))


def out_part(inner, full):
    return jnp.stack(
        [lower(mm(inner, full[i], (((0,), (0,)), ((), ())))) for i in range(full.shape[0])]
    )


def body(
    layer_input, attn_gain, qkv_weight, out_weight, ffn_gain, gate_up_weight, down_weight, cotangent
):
    n_c = lax.axis_size("ctx")
    me_c = lax.axis_index("ctx")
    qkv_parts = [spread(share(qkv_weight[:, i], 1, me_c, n_c)) for i in range(3)]
    out_full = spread(share(out_weight, 0, me_c, n_c))

    def out_blocks(inner, weight):
        return lambda t: mm(inner, lax.dynamic_index_in_dim(weight, t, 0, keepdims=False))

    def in_blocks(grads, weight):
        return lambda t: mm(grads, lax.dynamic_index_in_dim(weight, t, 0, keepdims=False), NT)

    input_float = layer_input.astype(F32)
    attn_scale = attn_gain.astype(F32)
    ffn_scale = ffn_gain.astype(F32)
    rms_one = lax.rsqrt(row_total(jnp.sum(input_float * input_float, axis=-1)) / D + rms_epsilon)[
        :, None
    ]
    normed_attn = lower(input_float * rms_one * attn_scale)
    attn_full = gather_rows(normed_attn)
    seq_len = attn_full.shape[1]
    cosine, sine = rope_tables(seq_len)
    proj = [into(attn_full, part) for part in qkv_parts]
    cotan_full = gather_pair(after(cotangent, attn_full))
    proj = after(proj, cotan_full)
    queries, keys, values, head_outs, norms = attend_forward(*proj, cosine, sine)
    gu_share = pair_share(gate_up_weight, 2, tuple(proj), head_outs)
    gu_wide = far_spread(jnp.stack(gu_share))
    down_share = jnp.stack(pair_share(down_weight, 0, gu_share, gu_share))
    down_full = far_spread(down_share)
    gu_pair = [gu_wide[:, i].reshape(gu_wide.shape[0], gu_wide.shape[2], -1) for i in range(2)]
    resid = input_float + scatter_rows(out_blocks(head_outs, out_full))
    resid = after(resid, down_share)
    rms_two = lax.rsqrt(row_total(jnp.sum(resid * resid, axis=-1)) / D + rms_epsilon)[:, None]
    normed_ffn = lower(resid * rms_two * ffn_scale)
    ffn_full = gather_pair(normed_ffn, gu_wide)
    gate_up = into(ffn_full[0], gu_pair[0]) + into(ffn_full[1], gu_pair[1])
    units = gate_up.shape[1] // 2
    gate = gate_up[:, :units]
    up_value = gate_up[:, units:]
    sigma = jax.nn.sigmoid(gate)
    hidden = lower(gate * sigma * up_value)
    down_part = [out_part(hidden, full) for full in cotan_full]
    down_sum = [far_owners(part) for part in down_part]
    down_full = after(down_full, down_part)
    down_pair = [down_full[:, i] for i in range(2)]
    grad_hidden = back_out(cotan_full[0], down_pair[0]) + back_out(cotan_full[1], down_pair[1])
    grad_gu = lower(
        jnp.concatenate(
            [
                grad_hidden * up_value * sigma * (1.0 + gate * (1.0 - sigma)),
                grad_hidden * gate * sigma,
            ],
            axis=1,
        )
    )
    gu_part = [in_part(full, grad_gu) for full in ffn_full]
    gu_sum = [far_owners(after(part, down_sum)) for part in gu_part]
    grad_nffn = scatter_pair(
        lambda i: mm(grad_gu, gu_pair[0][i], NT), lambda i: mm(grad_gu, gu_pair[1][i], NT)
    )
    grad_nffn = after(grad_nffn, gu_part)
    ffn_term = grad_nffn * ffn_scale
    ffn_dot = row_total(jnp.sum(ffn_term * resid, axis=-1))[:, None]
    grad_resid = cotangent.astype(F32) + rms_two * ffn_term - resid * rms_two**3 * ffn_dot / D
    ffn_gain_part = jnp.sum(grad_nffn * resid * rms_two, axis=0)
    grad_branch = lower(grad_resid)
    branch_full = gather_rows(grad_branch)
    grad_heads = lower(back_out(branch_full, out_full))
    out_sum = owners(out_part(head_outs, branch_full))
    grad_proj = attend_backward(
        queries, keys, values, head_outs, norms, grad_heads, cosine, sine
    )
    qkv_part = [in_part(attn_full, grad) for grad in grad_proj]
    qkv_sum = [owners(part) for part in qkv_part]
    grad_nattn = scatter_rows(
        in_blocks(jnp.concatenate(grad_proj, axis=1), jnp.concatenate(qkv_parts, axis=2))
    )
    hidden = after(hidden, qkv_part)
    ffn_out = scatter_pair(
        lambda i: mm(hidden, down_pair[0][i]), lambda i: mm(hidden, down_pair[1][i])
    )
    layer_output = lower(resid + ffn_out)
    attn_term = grad_nattn * attn_scale
    attn_dot = row_total(jnp.sum(attn_term * input_float, axis=-1))[:, None]
    grad_input = grad_resid + rms_one * attn_term - input_float * rms_one**3 * attn_dot / D
    attn_gain_part = jnp.sum(grad_nattn * input_float * rms_one, axis=0)
    gain_grads = total_rows(jnp.stack([attn_gain_part, ffn_gain_part]))

    down_grad = jnp.concatenate(pair_grad(*down_sum, 1), axis=0).astype(F32)
    gu_grad = jnp.concatenate(
        [v.reshape(v.shape[0], 2, -1) for v in pair_grad(*gu_sum, 0)], axis=2
    ).astype(F32)
    out_weight_grad = jnp.concatenate(trade_ctx(out_sum, 1), axis=0).astype(F32)
    done = (down_grad, out_weight_grad, gu_grad, grad_input, layer_output, gain_grads)
    qkv_grad = []
    for part in qkv_sum:
        qkv_grad.append(jnp.concatenate(trade_ctx(after(part, done), 0), axis=1).astype(F32))
        done = done + (qkv_grad[-1],)
    qkv_grad = jnp.stack(qkv_grad, axis=1)

    return (
        layer_output,
        grad_input,
        gain_grads[0],
        qkv_grad,
        out_weight_grad,
        gain_grads[1],
        gu_grad,
        down_grad,
    )


def solution(mesh):
    return jax.shard_map(
        body,
        mesh=mesh,
        in_specs=(
            P(("fsdp", "ctx"), "tp"),
            P("tp"),
            P("fsdp", None, "tp"),
            P("tp", "fsdp"),
            P("tp"),
            P("fsdp", None, "tp"),
            P("tp", "fsdp"),
            P(("fsdp", "ctx"), "tp"),
        ),
        out_specs=(
            P(("fsdp", "ctx"), "tp"),
            P(("fsdp", "ctx"), "tp"),
            P("tp"),
            P(("fsdp", "ctx"), None, "tp"),
            P("tp", ("fsdp", "ctx")),
            P("tp"),
            P(("fsdp", "ctx"), None, "tp"),
            P("tp", ("fsdp", "ctx")),
        ),
        check_vma=False,
    )
```

```python
import math

import jax
import jax.numpy as jnp
from jax import lax
from jax.experimental import pallas as pl
from jax.experimental.layout import Layout, with_layout_constraint
from jax.experimental.pallas import tpu as pltpu
from jax.sharding import PartitionSpec as P

D = 4096
HD = 128
BF = jnp.bfloat16
F32 = jnp.float32
rms_epsilon = 1e-05
NT = (((1,), (1,)), ((), ()))
LOG2E = 1.4426950408889634


def mm(left, right, dims=(((1,), (0,)), ((), ()))):
    return lax.dot_general(left, right, dims, preferred_element_type=F32)


def turn(values, cosine, sine):
    return values * cosine + pltpu.roll(values, HD // 2, 1) * sine


def rope_tables(seq_len):
    half_width = HD // 2
    inv_freq = jnp.exp(-math.log(10000.0) * jnp.arange(half_width, dtype=F32) * 2.0 / HD)
    angles = jnp.arange(seq_len, dtype=F32)[:, None] * inv_freq[None, :]
    cosine, sine = jnp.cos(angles), jnp.sin(angles)
    return jnp.concatenate([cosine, cosine], axis=1), jnp.concatenate([-sine, sine], axis=1)


def attend_forward(query_proj, key_proj, value_proj, cosine, sine):
    seq_len = query_proj.shape[0]
    heads = query_proj.shape[1] // HD
    block = min(512, seq_len)
    blocks = seq_len // block
    scale = LOG2E / math.sqrt(HD)

    def kernel(q_in, k_in, v_in, cos_q, sin_q, cos_k, sin_k, q_out, k_out, v_out, out, norm, vt):
        i = pl.program_id(1)

        @pl.when(i == 0)
        def _():
            for j in range(blocks):
                rows = pl.ds(j * block, block)
                k_out[rows, :] = turn(k_in[rows, :], cos_k[rows, :], sin_k[rows, :]).astype(BF)
                v_out[rows, :] = v_in[rows, :].astype(BF)
                vt[j] = v_in[rows, :].T.astype(BF)

        q_out[...] = turn(q_in[...], cos_q[...], sin_q[...]).astype(BF)
        query = q_out[...]

        def step(j, carry, diagonal):
            top, total, mixed = carry
            rows = pl.ds(pl.multiple_of(j * block, block), block)
            scores = mm(k_out[rows, :], query, NT) * scale
            if diagonal:
                key_at = lax.broadcasted_iota(jnp.int32, scores.shape, 0)
                query_at = lax.broadcasted_iota(jnp.int32, scores.shape, 1)
                scores = jnp.where(key_at <= query_at, scores, -1e30)
            new_top = jnp.maximum(top, jnp.max(scores, axis=0, keepdims=True))
            expo = jnp.exp2(scores - new_top)
            fade = jnp.exp2(top - new_top)
            total = total * fade + jnp.sum(expo, axis=0, keepdims=True)
            mixed = mixed * fade + mm(vt[j], expo.astype(BF))
            return new_top, total, mixed

        carry = (
            jnp.full((1, block), -1e30, F32),
            jnp.zeros((1, block), F32),
            jnp.zeros((HD, block), F32),
        )
        carry = lax.fori_loop(0, i, lambda j, c: step(j, c, False), carry)
        top, total, mixed = step(i, carry, True)
        out[...] = (mixed / total).T.astype(BF)
        norm[0] = top + jnp.log2(total)

    row = pl.BlockSpec((block, HD), lambda h, i: (i, h))
    col = pl.BlockSpec((seq_len, HD), lambda h, i: (0, h))
    pos = pl.BlockSpec((block, HD), lambda h, i: (i, 0))
    all_pos = pl.BlockSpec((seq_len, HD), lambda h, i: (0, 0))
    wide = jax.ShapeDtypeStruct((seq_len, heads * HD), BF)
    pairs = heads * seq_len * (seq_len + block) // 2
    return pl.pallas_call(
        kernel,
        grid=(heads, blocks),
        in_specs=[row, col, col, pos, pos, all_pos, all_pos],
        out_specs=[row, col, col, row, pl.BlockSpec((1, 1, block), lambda h, i: (h, 0, i))],
        out_shape=[wide, wide, wide, wide, jax.ShapeDtypeStruct((heads, 1, seq_len), F32)],
        scratch_shapes=[pltpu.VMEM((blocks, HD, block), BF)],
        compiler_params=pltpu.CompilerParams(vmem_limit_bytes=48 << 20),
        cost_estimate=pl.CostEstimate(
            flops=30 * pairs * HD,
            transcendentals=pairs,
            bytes_accessed=seq_len * heads * HD * (12 + 8),
        ),
    )(query_proj, key_proj, value_proj, cosine, sine, cosine, sine)


def attend_backward(queries, keys, values, outs, norms, grads, cosine, sine):
    seq_len = queries.shape[0]
    heads = queries.shape[1] // HD
    block = min(512, seq_len)
    blocks = seq_len // block
    root = 1.0 / math.sqrt(HD)
    scale = LOG2E * root

    def kernel(q, k, v, o, g, norm, cos_q, sin_q, cos_k, sin_k, dq, dk, dv, kt, dk_sum, dv_sum):
        i = pl.program_id(1)

        @pl.when(i == 0)
        def _():
            for j in range(blocks):
                rows = pl.ds(j * block, block)
                kt[j] = k[rows, :].astype(F32).T.astype(BF)
            dk_sum[...] = jnp.zeros_like(dk_sum)
            dv_sum[...] = jnp.zeros_like(dv_sum)

        query = q[...]
        grad = g[...]
        dots = (grad.astype(F32) * o[...].astype(F32)).T
        weighted = jnp.sum(dots, axis=0, keepdims=True)
        level = norm[0]

        def step(j, total, diagonal):
            rows = pl.ds(pl.multiple_of(j * block, block), block)
            scores = mm(k[rows, :], query, NT) * scale
            probs = jnp.exp2(scores - level)
            if diagonal:
                key_at = lax.broadcasted_iota(jnp.int32, scores.shape, 0)
                query_at = lax.broadcasted_iota(jnp.int32, scores.shape, 1)
                probs = jnp.where(key_at <= query_at, probs, 0.0)
            dv_sum[rows, :] += mm(probs.astype(BF), grad)
            d_probs = mm(v[rows, :], grad, NT)
            d_scores = (probs * (d_probs - weighted)).astype(BF)
            dk_sum[rows, :] += mm(d_scores, query)
            return total + mm(kt[j], d_scores)

        total = lax.fori_loop(
            0, i, lambda j, c: step(j, c, False), jnp.zeros((HD, block), F32)
        )
        total = step(i, total, True)
        dq[...] = turn(total.T * root, cos_q[...], -sin_q[...]).astype(BF)

        @pl.when(i == blocks - 1)
        def _():
            for j in range(blocks):
                rows = pl.ds(j * block, block)
                dk[rows, :] = turn(
                    dk_sum[rows, :] * root, cos_k[rows, :], -sin_k[rows, :]
                ).astype(BF)
                dv[rows, :] = dv_sum[rows, :].astype(BF)

    row = pl.BlockSpec((block, HD), lambda h, i: (i, h))
    col = pl.BlockSpec((seq_len, HD), lambda h, i: (0, h))
    pos = pl.BlockSpec((block, HD), lambda h, i: (i, 0))
    all_pos = pl.BlockSpec((seq_len, HD), lambda h, i: (0, 0))
    wide = jax.ShapeDtypeStruct((seq_len, heads * HD), BF)
    pairs = heads * seq_len * (seq_len + block) // 2
    return pl.pallas_call(
        kernel,
        grid=(heads, blocks),
        in_specs=[row, col, col, row, row, pl.BlockSpec((1, 1, block), lambda h, i: (h, 0, i)),
                  pos, pos, all_pos, all_pos],
        out_specs=[row, col, col],
        out_shape=[wide, wide, wide],
        scratch_shapes=[
            pltpu.VMEM((blocks, HD, block), BF),
            pltpu.VMEM((seq_len, HD), F32),
            pltpu.VMEM((seq_len, HD), F32),
        ],
        compiler_params=pltpu.CompilerParams(vmem_limit_bytes=48 << 20),
        cost_estimate=pl.CostEstimate(
            flops=38 * pairs * HD,
            transcendentals=pairs,
            bytes_accessed=seq_len * heads * HD * 16,
        ),
    )(queries, keys, values, outs, grads, norms, cosine, sine, cosine, sine)


def row_total(values):
    return lax.psum(values, "tp")


def swap(values, axis, bit):
    step = 1 << bit
    return lax.ppermute(values, axis, [(i, i ^ step) for i in range(lax.axis_size(axis))])


def high_bits():
    return list(range(1, lax.axis_size("tp").bit_length() - 1))[::-1]


def gather_rows(values):
    rows, cols = values.shape
    half = rows // 2
    n_t, n_c = lax.axis_size("tp"), lax.axis_size("ctx")
    me_t, me_c = lax.axis_index("tp"), lax.axis_index("ctx")
    across = [("tp", b) for b in high_bits()]
    full = jnp.zeros((n_t, n_c * rows, cols), values.dtype)
    for part, plan in enumerate(([("ctx", 0)] + across, across + [("ctx", 0)])):
        held = {(0, 0): values[part * half : (part + 1) * half]}
        for axis, bit in plan + [("tp", 0)]:
            for (dc, dt), piece in list(held.items()):
                key = (1, dt) if axis == "ctx" else (dc, dt | (1 << bit))
                held[key] = swap(piece, axis, bit)
        for (dc, dt), piece in held.items():
            start = (me_t ^ dt, (me_c ^ dc) * rows + part * half, 0)
            full = lax.dynamic_update_slice(full, piece[None], start)
    return with_layout_constraint(full, Layout((0, 1, 2)))


def scatter_rows(block_of):
    n_t, n_c = lax.axis_size("tp"), lax.axis_size("ctx")
    me_t, me_c = lax.axis_index("tp"), lax.axis_index("ctx")
    sums = {}
    for dt in range(0, n_t, 2):
        got = swap(block_of(me_t ^ (dt + 1)).astype(BF), "tp", 0)
        sums[dt] = (block_of(me_t ^ dt) + got.astype(F32)).astype(BF)
    rows = sums[0].shape[0] // n_c
    cols = sums[0].shape[1]
    half = rows // 2
    across = [("tp", b) for b in high_bits()]
    done = []
    for part, plan in enumerate(([("ctx", 0)] + across, across + [("ctx", 0)])):
        held = {}
        for dt, total in sums.items():
            split = total.reshape(n_c, rows, cols)[:, part * half : (part + 1) * half]
            for dc in range(n_c):
                held[(dc, dt)] = lax.dynamic_index_in_dim(split, me_c ^ dc, 0, keepdims=False)
        for axis, bit in plan:
            left = {}
            for (dc, dt), piece in held.items():
                give = dc == 1 if axis == "ctx" else (dt >> bit) & 1
                if not give:
                    away = (1, dt) if axis == "ctx" else (dc, dt | (1 << bit))
                    got = swap(held[away].astype(BF), axis, bit)
                    left[(dc, dt)] = piece.astype(F32) + got.astype(F32)
            held = left
        done.append(held[(0, 0)])
    return jnp.concatenate(done, axis=0)


def ctx_half(weight, axis):
    size = weight.shape[axis] // lax.axis_size("ctx")
    return lax.dynamic_slice_in_dim(weight, lax.axis_index("ctx") * size, size, axis)


def part_of(weight, axis, index):
    size = weight.shape[axis] // (2 * lax.axis_size("ctx"))
    start = (2 * lax.axis_index("ctx") + index) * size
    return lax.dynamic_slice_in_dim(weight, start, size, axis)


def after(value, token):
    value, _ = lax.optimization_barrier((value, token))
    return value


def owners(grad):
    return lax.psum_scatter(grad, "fsdp", scatter_dimension=0, tiled=False)


def line_owners(grad):
    count = lax.axis_size("fsdp")
    me = lax.axis_index("fsdp")

    def part(owner):
        owner = jnp.clip(owner, 0, count - 1)
        return lax.dynamic_index_in_dim(grad, owner, 0, keepdims=False)

    def joined(mine, got):
        return mine if got is None else (mine.astype(F32) + got.astype(F32)).astype(BF)

    steps = []
    up = down = None
    for step in range(count - 1):
        gap = count - 1 - step
        up = joined(part(me + gap), up)
        up = lax.ppermute(up, "fsdp", [(i, i + 1) for i in range(step + 1)])
        down = joined(part(me - gap), down)
        down = lax.ppermute(down, "fsdp", [(i, i - 1) for i in range(gap, count)])
        steps.append((up, down))
    return steps, part(me).astype(F32) + up.astype(F32) + down.astype(F32)


def spread(weight):
    return lax.all_gather(weight, "fsdp", axis=0, tiled=False)


def trade_ctx(block, axis):
    size = block.shape[axis] // lax.axis_size("ctx")
    me = lax.axis_index("ctx")
    own = lax.dynamic_slice_in_dim(block, me * size, size, axis)
    give = lax.dynamic_slice_in_dim(block, (1 - me) * size, size, axis)
    got = swap(give, "ctx", 0)
    return jnp.where(me == 0, own, got), jnp.where(me == 0, got, own)


def by_ctx(halves):
    return [half[i] for i in range(lax.axis_size("ctx")) for half in halves]


def out_grad(block):
    return jnp.concatenate(trade_ctx(block, 1), axis=0).astype(F32)


def total_rows(values):
    values = values + swap(values, "ctx", 0)
    for bit in range(lax.axis_size("fsdp").bit_length() - 1):
        values = values + swap(values, "fsdp", bit)
    return values


def body(
    layer_input, attn_gain, qkv_weight, out_weight, ffn_gain, gate_up_weight, down_weight, cotangent
):
    n_f = lax.axis_size("fsdp")
    d_f = D // n_f
    qkv_full = spread(ctx_half(jnp.swapaxes(qkv_weight, 0, 1), 2))
    qkv_parts = [qkv_full[:, i] for i in range(3)]
    out_full = spread(ctx_half(out_weight, 0))
    gu_full = [spread(part_of(gate_up_weight, 2, i).reshape(d_f, -1)) for i in range(2)]
    down_full = [spread(part_of(down_weight, 0, i)) for i in range(2)]

    def into(full, weight):
        return mm(full, weight, (((0, 2), (0, 1)), ((), ())))

    def back_out(full, weight):
        return mm(full, weight, (((0, 2), (0, 2)), ((), ())))

    def out_blocks(inner, weight):
        return lambda t: mm(inner, lax.dynamic_index_in_dim(weight, t, 0, keepdims=False))

    def in_blocks(grads, weight):
        return lambda t: mm(grads, lax.dynamic_index_in_dim(weight, t, 0, keepdims=False), NT)

    def in_part(full, grads):
        return mm(full, grads, (((1,), (0,)), ((), ()))).astype(BF)

    def out_part(inner, full):
        return jnp.stack(
            [mm(inner, full[t], (((0,), (0,)), ((), ()))).astype(BF) for t in range(n_f)]
        )

    input_float = layer_input.astype(F32)
    attn_scale = attn_gain.astype(F32)
    ffn_scale = ffn_gain.astype(F32)
    rms_one = lax.rsqrt(row_total(jnp.sum(input_float * input_float, axis=-1)) / D + rms_epsilon)[
        :, None
    ]
    normed_attn = (input_float * rms_one * attn_scale).astype(BF)
    attn_full = gather_rows(normed_attn)
    seq_len = attn_full.shape[1]
    cosine, sine = rope_tables(seq_len)
    cotan_full = gather_rows(after(cotangent, attn_full))
    proj = after([into(attn_full, part) for part in qkv_parts], cotan_full)
    queries, keys, values, head_outs, norms = attend_forward(*proj, cosine, sine)
    resid = input_float + scatter_rows(out_blocks(head_outs, out_full))
    rms_two = lax.rsqrt(row_total(jnp.sum(resid * resid, axis=-1)) / D + rms_epsilon)[:, None]
    normed_ffn = (resid * rms_two * ffn_scale).astype(BF)
    ffn_full = gather_rows(normed_ffn)

    def ffn_hidden(tokens, weight):
        gate_up = into(tokens, weight)
        units = gate_up.shape[1] // 2
        gate = gate_up[:, :units]
        up_value = gate_up[:, units:]
        sigma = jax.nn.sigmoid(gate)
        return gate, up_value, sigma, (gate * sigma * up_value).astype(BF)

    def ffn_grads(cotan, weight, gate, up_value, sigma):
        grad_hidden = back_out(cotan, weight)
        return jnp.concatenate(
            [
                grad_hidden * up_value * sigma * (1.0 + gate * (1.0 - sigma)),
                grad_hidden * gate * sigma,
            ],
            axis=1,
        ).astype(BF)

    *inner, hidden_a = ffn_hidden(ffn_full, gu_full[0])
    down_part_a = out_part(hidden_a, cotan_full)
    down_steps, down_sum_a = line_owners(down_part_a)
    weight = after(down_full[0], down_part_a)
    grad_gu_a = ffn_grads(cotan_full, weight, *inner)
    gu_part_a = in_part(ffn_full, grad_gu_a)
    gu_steps, gu_sum_a = line_owners(gu_part_a)
    tokens = after(ffn_full, (gu_part_a, gu_steps[0], down_steps[-1]))
    *inner, hidden_b = ffn_hidden(tokens, gu_full[1])
    down_part_b = out_part(hidden_b, cotan_full)
    down_sum_b = owners(down_part_b)
    weight = after(down_full[1], (down_part_b, gu_steps[-1]))
    grad_gu_b = ffn_grads(cotan_full, weight, *inner)
    gu_part_b = in_part(ffn_full, grad_gu_b)
    gu_sum_b = owners(gu_part_b)
    blocks = [in_blocks(grad_gu_a, gu_full[0]), in_blocks(grad_gu_b, gu_full[1])]
    grad_nffn = after(scatter_rows(lambda t: blocks[0](t) + blocks[1](t)), gu_part_b)
    ffn_term = grad_nffn * ffn_scale
    ffn_dot = row_total(jnp.sum(ffn_term * resid, axis=-1))[:, None]
    grad_resid = cotangent.astype(F32) + rms_two * ffn_term - resid * rms_two**3 * ffn_dot / D
    ffn_gain_part = jnp.sum(grad_nffn * resid * rms_two, axis=0)
    grad_branch = grad_resid.astype(BF)
    branch_full = gather_rows(grad_branch)
    grad_heads = back_out(branch_full, out_full).astype(BF)
    out_sum = owners(out_part(head_outs, branch_full))
    grad_proj = attend_backward(
        queries, keys, values, head_outs, norms, grad_heads, cosine, sine
    )
    qkv_part = [
        in_part(attn_full, jnp.concatenate(grad_proj[1:], axis=1)),
        in_part(attn_full, grad_proj[0]),
    ]
    qkv_sum = [owners(part) for part in qkv_part]
    grad_nattn = scatter_rows(
        in_blocks(jnp.concatenate(grad_proj, axis=1), jnp.concatenate(qkv_parts, axis=2))
    )
    hidden_a, hidden_b = after((hidden_a, hidden_b), qkv_part)
    outs = [out_blocks(hidden_a, down_full[0]), out_blocks(hidden_b, down_full[1])]
    layer_output = (resid + scatter_rows(lambda t: outs[0](t) + outs[1](t))).astype(BF)
    attn_term = grad_nattn * attn_scale
    attn_dot = row_total(jnp.sum(attn_term * input_float, axis=-1))[:, None]
    grad_input = grad_resid + rms_one * attn_term - input_float * rms_one**3 * attn_dot / D
    attn_gain_part = jnp.sum(grad_nattn * input_float * rms_one, axis=0)
    gain_grads = total_rows(jnp.stack([attn_gain_part, ffn_gain_part]))

    down_grad = by_ctx([trade_ctx(v, 1) for v in (down_sum_a.astype(BF), down_sum_b)])
    down_grad = jnp.concatenate(down_grad, axis=0).astype(F32)
    gu_grad = by_ctx([trade_ctx(v, 0) for v in (gu_sum_a.astype(BF), gu_sum_b)])
    gu_grad = jnp.concatenate([v.reshape(v.shape[0], 2, -1) for v in gu_grad], axis=2).astype(F32)
    out_weight_grad = out_grad(out_sum)
    done = (down_grad, out_weight_grad, gu_grad, grad_input, layer_output, gain_grads)
    qkv_grad = []
    for part in qkv_sum:
        first, second = trade_ctx(after(part, done), 0)
        wide = queries.shape[1]
        for i in range(0, first.shape[1], wide):
            both = [first[:, i : i + wide], second[:, i : i + wide]]
            qkv_grad.append(jnp.concatenate(both, axis=1).astype(F32))
        done = done + (qkv_grad[-1],)
    qkv_grad = jnp.stack([qkv_grad[2], qkv_grad[0], qkv_grad[1]], axis=1)

    return (
        layer_output,
        grad_input,
        gain_grads[0],
        qkv_grad,
        out_weight_grad,
        gain_grads[1],
        gu_grad,
        down_grad,
    )


def solution(mesh):
    return jax.shard_map(
        body,
        mesh=mesh,
        in_specs=(
            P(("fsdp", "ctx"), "tp"),
            P("tp"),
            P("fsdp", None, "tp"),
            P("tp", "fsdp"),
            P("tp"),
            P("fsdp", None, "tp"),
            P("tp", "fsdp"),
            P(("fsdp", "ctx"), "tp"),
        ),
        out_specs=(
            P(("fsdp", "ctx"), "tp"),
            P(("fsdp", "ctx"), "tp"),
            P("tp"),
            P(("fsdp", "ctx"), None, "tp"),
            P("tp", ("fsdp", "ctx")),
            P("tp"),
            P(("fsdp", "ctx"), None, "tp"),
            P("tp", ("fsdp", "ctx")),
        ),
        check_vma=False,
    )
```

```python
import math

import jax
import jax.numpy as jnp
from jax import lax
from jax.experimental import pallas as pl
from jax.experimental.layout import Layout, with_layout_constraint
from jax.experimental.pallas import tpu as pltpu
from jax.sharding import PartitionSpec as P

D = 4096
HD = 128
BF = jnp.bfloat16
F32 = jnp.float32
rms_epsilon = 1e-05
NT = (((1,), (1,)), ((), ()))
LOG2E = 1.4426950408889634


def mm(left, right, dims=(((1,), (0,)), ((), ()))):
    return lax.dot_general(left, right, dims, preferred_element_type=F32)


def turn(values, cosine, sine):
    return values * cosine + pltpu.roll(values, HD // 2, 1) * sine


def rope_tables(seq_len):
    half_width = HD // 2
    inv_freq = jnp.exp(-math.log(10000.0) * jnp.arange(half_width, dtype=F32) * 2.0 / HD)
    angles = jnp.arange(seq_len, dtype=F32)[:, None] * inv_freq[None, :]
    cosine, sine = jnp.cos(angles), jnp.sin(angles)
    return jnp.concatenate([cosine, cosine], axis=1), jnp.concatenate([-sine, sine], axis=1)


def attend_forward(query_proj, key_proj, value_proj, cosine, sine):
    seq_len = query_proj.shape[0]
    heads = query_proj.shape[1] // HD
    block = min(512, seq_len)
    blocks = seq_len // block
    scale = LOG2E / math.sqrt(HD)

    def kernel(q_in, k_in, v_in, cos_q, sin_q, cos_k, sin_k, q_out, k_out, v_out, out, norm, vt):
        i = pl.program_id(1)

        @pl.when(i == 0)
        def _():
            for j in range(blocks):
                rows = pl.ds(j * block, block)
                k_out[rows, :] = turn(k_in[rows, :], cos_k[rows, :], sin_k[rows, :]).astype(BF)
                v_out[rows, :] = v_in[rows, :].astype(BF)
                vt[j] = v_in[rows, :].T.astype(BF)

        q_out[...] = turn(q_in[...], cos_q[...], sin_q[...]).astype(BF)
        query = q_out[...]

        def step(j, carry, diagonal):
            top, total, mixed = carry
            rows = pl.ds(pl.multiple_of(j * block, block), block)
            scores = mm(k_out[rows, :], query, NT) * scale
            if diagonal:
                key_at = lax.broadcasted_iota(jnp.int32, scores.shape, 0)
                query_at = lax.broadcasted_iota(jnp.int32, scores.shape, 1)
                scores = jnp.where(key_at <= query_at, scores, -1e30)
            new_top = jnp.maximum(top, jnp.max(scores, axis=0, keepdims=True))
            expo = jnp.exp2(scores - new_top)
            fade = jnp.exp2(top - new_top)
            total = total * fade + jnp.sum(expo, axis=0, keepdims=True)
            mixed = mixed * fade + mm(vt[j], expo.astype(BF))
            return new_top, total, mixed

        carry = (
            jnp.full((1, block), -1e30, F32),
            jnp.zeros((1, block), F32),
            jnp.zeros((HD, block), F32),
        )
        carry = lax.fori_loop(0, i, lambda j, c: step(j, c, False), carry)
        top, total, mixed = step(i, carry, True)
        out[...] = (mixed / total).T.astype(BF)
        norm[0] = top + jnp.log2(total)

    row = pl.BlockSpec((block, HD), lambda h, i: (i, h))
    col = pl.BlockSpec((seq_len, HD), lambda h, i: (0, h))
    pos = pl.BlockSpec((block, HD), lambda h, i: (i, 0))
    all_pos = pl.BlockSpec((seq_len, HD), lambda h, i: (0, 0))
    wide = jax.ShapeDtypeStruct((seq_len, heads * HD), BF)
    pairs = heads * seq_len * (seq_len + block) // 2
    return pl.pallas_call(
        kernel,
        grid=(heads, blocks),
        in_specs=[row, col, col, pos, pos, all_pos, all_pos],
        out_specs=[row, col, col, row, pl.BlockSpec((1, 1, block), lambda h, i: (h, 0, i))],
        out_shape=[wide, wide, wide, wide, jax.ShapeDtypeStruct((heads, 1, seq_len), F32)],
        scratch_shapes=[pltpu.VMEM((blocks, HD, block), BF)],
        compiler_params=pltpu.CompilerParams(vmem_limit_bytes=48 << 20),
        cost_estimate=pl.CostEstimate(
            flops=30 * pairs * HD,
            transcendentals=pairs,
            bytes_accessed=seq_len * heads * HD * (12 + 8),
        ),
    )(query_proj, key_proj, value_proj, cosine, sine, cosine, sine)


def attend_backward(queries, keys, values, outs, norms, grads, cosine, sine):
    seq_len = queries.shape[0]
    heads = queries.shape[1] // HD
    block = min(512, seq_len)
    blocks = seq_len // block
    root = 1.0 / math.sqrt(HD)
    scale = LOG2E * root

    def kernel(q, k, v, o, g, norm, cos_q, sin_q, cos_k, sin_k, dq, dk, dv, kt, dk_sum, dv_sum):
        i = pl.program_id(1)

        @pl.when(i == 0)
        def _():
            for j in range(blocks):
                rows = pl.ds(j * block, block)
                kt[j] = k[rows, :].astype(F32).T.astype(BF)
            dk_sum[...] = jnp.zeros_like(dk_sum)
            dv_sum[...] = jnp.zeros_like(dv_sum)

        query = q[...]
        grad = g[...]
        dots = (grad.astype(F32) * o[...].astype(F32)).T
        weighted = jnp.sum(dots, axis=0, keepdims=True)
        level = norm[0]

        def step(j, total, diagonal):
            rows = pl.ds(pl.multiple_of(j * block, block), block)
            scores = mm(k[rows, :], query, NT) * scale
            probs = jnp.exp2(scores - level)
            if diagonal:
                key_at = lax.broadcasted_iota(jnp.int32, scores.shape, 0)
                query_at = lax.broadcasted_iota(jnp.int32, scores.shape, 1)
                probs = jnp.where(key_at <= query_at, probs, 0.0)
            dv_sum[rows, :] += mm(probs.astype(BF), grad)
            d_probs = mm(v[rows, :], grad, NT)
            d_scores = (probs * (d_probs - weighted)).astype(BF)
            dk_sum[rows, :] += mm(d_scores, query)
            return total + mm(kt[j], d_scores)

        total = lax.fori_loop(
            0, i, lambda j, c: step(j, c, False), jnp.zeros((HD, block), F32)
        )
        total = step(i, total, True)
        dq[...] = turn(total.T * root, cos_q[...], -sin_q[...]).astype(BF)

        @pl.when(i == blocks - 1)
        def _():
            for j in range(blocks):
                rows = pl.ds(j * block, block)
                dk[rows, :] = turn(
                    dk_sum[rows, :] * root, cos_k[rows, :], -sin_k[rows, :]
                ).astype(BF)
                dv[rows, :] = dv_sum[rows, :].astype(BF)

    row = pl.BlockSpec((block, HD), lambda h, i: (i, h))
    col = pl.BlockSpec((seq_len, HD), lambda h, i: (0, h))
    pos = pl.BlockSpec((block, HD), lambda h, i: (i, 0))
    all_pos = pl.BlockSpec((seq_len, HD), lambda h, i: (0, 0))
    wide = jax.ShapeDtypeStruct((seq_len, heads * HD), BF)
    pairs = heads * seq_len * (seq_len + block) // 2
    return pl.pallas_call(
        kernel,
        grid=(heads, blocks),
        in_specs=[row, col, col, row, row, pl.BlockSpec((1, 1, block), lambda h, i: (h, 0, i)),
                  pos, pos, all_pos, all_pos],
        out_specs=[row, col, col],
        out_shape=[wide, wide, wide],
        scratch_shapes=[
            pltpu.VMEM((blocks, HD, block), BF),
            pltpu.VMEM((seq_len, HD), F32),
            pltpu.VMEM((seq_len, HD), F32),
        ],
        compiler_params=pltpu.CompilerParams(vmem_limit_bytes=48 << 20),
        cost_estimate=pl.CostEstimate(
            flops=38 * pairs * HD,
            transcendentals=pairs,
            bytes_accessed=seq_len * heads * HD * 16,
        ),
    )(queries, keys, values, outs, grads, norms, cosine, sine, cosine, sine)


def row_total(values):
    return lax.psum(values, "tp")


def swap(values, axis, bit):
    step = 1 << bit
    return lax.ppermute(values, axis, [(i, i ^ step) for i in range(lax.axis_size(axis))])


def high_bits():
    return list(range(1, lax.axis_size("tp").bit_length() - 1))[::-1]


def gather_rows(values):
    rows, cols = values.shape
    half = rows // 2
    n_t, n_c = lax.axis_size("tp"), lax.axis_size("ctx")
    me_t, me_c = lax.axis_index("tp"), lax.axis_index("ctx")
    across = [("tp", b) for b in high_bits()]
    full = jnp.zeros((n_t, n_c * rows, cols), values.dtype)
    for part, plan in enumerate(([("ctx", 0)] + across, across + [("ctx", 0)])):
        held = {(0, 0): values[part * half : (part + 1) * half]}
        for axis, bit in plan + [("tp", 0)]:
            for (dc, dt), piece in list(held.items()):
                key = (1, dt) if axis == "ctx" else (dc, dt | (1 << bit))
                held[key] = swap(piece, axis, bit)
        for (dc, dt), piece in held.items():
            start = (me_t ^ dt, (me_c ^ dc) * rows + part * half, 0)
            full = lax.dynamic_update_slice(full, piece[None], start)
    return with_layout_constraint(full, Layout((0, 1, 2)))


def gather_pair(values):
    return gather_rows(values), gather_rows(near(values))


def scatter_rows(block_of):
    n_t, n_c = lax.axis_size("tp"), lax.axis_size("ctx")
    me_t, me_c = lax.axis_index("tp"), lax.axis_index("ctx")
    sums = {}
    for dt in range(0, n_t, 2):
        got = swap(block_of(me_t ^ (dt + 1)).astype(BF), "tp", 0)
        sums[dt] = (block_of(me_t ^ dt) + got.astype(F32)).astype(BF)
    rows = sums[0].shape[0] // n_c
    cols = sums[0].shape[1]
    half = rows // 2
    across = [("tp", b) for b in high_bits()]
    done = []
    for part, plan in enumerate(([("ctx", 0)] + across, across + [("ctx", 0)])):
        held = {}
        for dt, total in sums.items():
            split = total.reshape(n_c, rows, cols)[:, part * half : (part + 1) * half]
            for dc in range(n_c):
                held[(dc, dt)] = lax.dynamic_index_in_dim(split, me_c ^ dc, 0, keepdims=False)
        for axis, bit in plan:
            left = {}
            for (dc, dt), piece in held.items():
                give = dc == 1 if axis == "ctx" else (dt >> bit) & 1
                if not give:
                    away = (1, dt) if axis == "ctx" else (dc, dt | (1 << bit))
                    got = swap(held[away].astype(BF), axis, bit)
                    left[(dc, dt)] = piece.astype(F32) + got.astype(F32)
            held = left
        done.append(held[(0, 0)])
    return jnp.concatenate(done, axis=0)


def ctx_half(weight, axis):
    size = weight.shape[axis] // lax.axis_size("ctx")
    return lax.dynamic_slice_in_dim(weight, lax.axis_index("ctx") * size, size, axis)


def after(value, token):
    value, _ = lax.optimization_barrier((value, token))
    return value


def owners(grad):
    return lax.psum_scatter(grad, "fsdp", scatter_dimension=0, tiled=False)


def far_groups():
    count = lax.axis_size("fsdp")
    return [list(range(i, count, 2)) for i in range(2)]


def far_owners(grad):
    grad = grad.reshape((-1, 2) + grad.shape[1:])
    return lax.psum_scatter(
        grad, "fsdp", scatter_dimension=0, tiled=False, axis_index_groups=far_groups()
    )


def far_spread(weight):
    full = lax.all_gather(
        weight, "fsdp", axis=0, tiled=False, axis_index_groups=far_groups()
    )
    return full.reshape((-1,) + full.shape[2:])


def plane():
    return lax.axis_index("fsdp") & 1


def near(values):
    return swap(values, "fsdp", 0)


def in_pair(mine, other):
    return jnp.where(plane() == 0, mine, other), jnp.where(plane() == 0, other, mine)


def pair_share(block, axis, token, hold):
    count = 2 * lax.axis_size("ctx")
    size = block.shape[axis] // count
    place = lax.axis_index("ctx") * 2

    def columns(index):
        return lax.dynamic_slice_in_dim(block, (place + index) * size, size, axis)

    other = near(after(columns(1 - plane()), token))
    return jnp.stack(in_pair(columns(plane()), after(other, hold)))


def pair_grad(block, axis):
    mine = lax.dynamic_index_in_dim(block, plane(), 0, keepdims=False)
    give = lax.dynamic_index_in_dim(block, 1 - plane(), 0, keepdims=False)
    both = trade_ctx(jnp.stack(in_pair(mine, near(give))), axis + 1)
    return [v[i] for v in both for i in range(2)]


def spread(weight):
    return lax.all_gather(weight, "fsdp", axis=0, tiled=False)


def trade_ctx(block, axis):
    size = block.shape[axis] // lax.axis_size("ctx")
    me = lax.axis_index("ctx")
    own = lax.dynamic_slice_in_dim(block, me * size, size, axis)
    give = lax.dynamic_slice_in_dim(block, (1 - me) * size, size, axis)
    got = swap(give, "ctx", 0)
    return jnp.where(me == 0, own, got), jnp.where(me == 0, got, own)


def out_grad(block):
    return jnp.concatenate(trade_ctx(block, 1), axis=0).astype(F32)


def total_rows(values):
    values = values + swap(values, "ctx", 0)
    for bit in range(lax.axis_size("fsdp").bit_length() - 1):
        values = values + swap(values, "fsdp", bit)
    return values


def body(
    layer_input, attn_gain, qkv_weight, out_weight, ffn_gain, gate_up_weight, down_weight, cotangent
):
    n_f = lax.axis_size("fsdp")
    d_f = D // n_f
    qkv_full = spread(ctx_half(jnp.swapaxes(qkv_weight, 0, 1), 2))
    qkv_parts = [qkv_full[:, i] for i in range(3)]
    out_full = spread(ctx_half(out_weight, 0))

    def into(full, weight):
        return mm(full, weight, (((0, 2), (0, 1)), ((), ())))

    def back_out(full, weight):
        return mm(full, weight, (((0, 2), (0, 2)), ((), ())))

    def out_blocks(inner, weight):
        return lambda t: mm(inner, lax.dynamic_index_in_dim(weight, t, 0, keepdims=False))

    def in_blocks(grads, weight):
        return lambda t: mm(grads, lax.dynamic_index_in_dim(weight, t, 0, keepdims=False), NT)

    def in_sum(full, grads):
        return mm(full, grads, (((1,), (0,)), ((), ())))

    def in_part(full, grads):
        return in_sum(full, grads).astype(BF)

    def out_part(inner, full):
        def block(t):
            return sum(mm(v, f[t], (((0,), (0,)), ((), ()))) for v, f in zip(inner, full))

        return jnp.stack([block(t).astype(BF) for t in range(n_f)])

    input_float = layer_input.astype(F32)
    attn_scale = attn_gain.astype(F32)
    ffn_scale = ffn_gain.astype(F32)
    rms_one = lax.rsqrt(row_total(jnp.sum(input_float * input_float, axis=-1)) / D + rms_epsilon)[
        :, None
    ]
    normed_attn = (input_float * rms_one * attn_scale).astype(BF)
    attn_full = gather_rows(normed_attn)
    seq_len = attn_full.shape[1]
    cosine, sine = rope_tables(seq_len)
    cotans = gather_pair(after(cotangent, attn_full))
    proj = after([into(attn_full, part) for part in qkv_parts], cotans[0])
    queries, keys, values, head_outs, norms = attend_forward(*proj, cosine, sine)
    gu_share = pair_share(gate_up_weight, 2, tuple(proj), head_outs)
    gu_full = far_spread(gu_share.reshape(2, d_f, -1))
    down_share = pair_share(down_weight, 0, gu_share, gu_share)
    down_full = far_spread(down_share)
    resid = input_float + scatter_rows(out_blocks(head_outs, out_full))
    rms_two = lax.rsqrt(row_total(jnp.sum(resid * resid, axis=-1)) / D + rms_epsilon)[:, None]
    normed_ffn = (resid * rms_two * ffn_scale).astype(BF)
    tokens = gather_pair(normed_ffn)
    inner = []
    for part in tokens:
        gate_up = into(part, gu_full)
        units = gate_up.shape[1] // 2
        gate = gate_up[:, :units]
        up_value = gate_up[:, units:]
        sigma = jax.nn.sigmoid(gate)
        inner.append((gate, up_value, sigma, (gate * sigma * up_value).astype(BF)))
    hidden = [v[3] for v in inner]
    down_part = out_part(hidden, cotans)
    down_sum = far_owners(down_part)
    down_full = after(down_full, down_part)
    grad_gu = []
    for cotan, (gate, up_value, sigma, _) in zip(cotans, inner):
        grad_hidden = back_out(cotan, down_full)
        grad_gu.append(
            jnp.concatenate(
                [
                    grad_hidden * up_value * sigma * (1.0 + gate * (1.0 - sigma)),
                    grad_hidden * gate * sigma,
                ],
                axis=1,
            ).astype(BF)
        )
    grad_near = scatter_rows(in_blocks(grad_gu[1], gu_full))
    gu_part = (in_sum(tokens[0], grad_gu[0]) + in_sum(tokens[1], grad_gu[1])).astype(BF)
    gu_sum = far_owners(gu_part)
    grad_own = scatter_rows(in_blocks(grad_gu[0], gu_full))
    grad_nffn = after(grad_own, gu_part) + near(grad_near.astype(BF)).astype(F32)
    ffn_term = grad_nffn * ffn_scale
    ffn_dot = row_total(jnp.sum(ffn_term * resid, axis=-1))[:, None]
    grad_resid = cotangent.astype(F32) + rms_two * ffn_term - resid * rms_two**3 * ffn_dot / D
    ffn_gain_part = jnp.sum(grad_nffn * resid * rms_two, axis=0)
    grad_branch = grad_resid.astype(BF)
    branch_full = gather_rows(grad_branch)
    grad_heads = back_out(branch_full, out_full).astype(BF)
    out_sum = owners(out_part([head_outs], [branch_full]))
    grad_proj = attend_backward(
        queries, keys, values, head_outs, norms, grad_heads, cosine, sine
    )
    qkv_part = [
        in_part(attn_full, jnp.concatenate(grad_proj[1:], axis=1)),
        in_part(attn_full, grad_proj[0]),
    ]
    qkv_sum = [owners(part) for part in qkv_part]
    grad_nattn = scatter_rows(
        in_blocks(jnp.concatenate(grad_proj, axis=1), jnp.concatenate(qkv_parts, axis=2))
    )
    hidden = after(hidden, qkv_part)
    out_near = scatter_rows(out_blocks(hidden[1], down_full))
    out_own = scatter_rows(out_blocks(hidden[0], down_full))
    layer_output = (resid + out_own + near(out_near.astype(BF)).astype(F32)).astype(BF)
    attn_term = grad_nattn * attn_scale
    attn_dot = row_total(jnp.sum(attn_term * input_float, axis=-1))[:, None]
    grad_input = grad_resid + rms_one * attn_term - input_float * rms_one**3 * attn_dot / D
    attn_gain_part = jnp.sum(grad_nattn * input_float * rms_one, axis=0)
    gain_grads = total_rows(jnp.stack([attn_gain_part, ffn_gain_part]))

    down_grad = jnp.concatenate(pair_grad(down_sum, 1), axis=0).astype(F32)
    gu_grad = jnp.concatenate(
        [v.reshape(v.shape[0], 2, -1) for v in pair_grad(gu_sum, 0)], axis=2
    ).astype(F32)
    out_weight_grad = out_grad(out_sum)
    done = (down_grad, out_weight_grad, gu_grad, grad_input, layer_output, gain_grads)
    qkv_grad = []
    for part in qkv_sum:
        first, second = trade_ctx(after(part, done), 0)
        wide = queries.shape[1]
        for i in range(0, first.shape[1], wide):
            both = [first[:, i : i + wide], second[:, i : i + wide]]
            qkv_grad.append(jnp.concatenate(both, axis=1).astype(F32))
        done = done + (qkv_grad[-1],)
    qkv_grad = jnp.stack([qkv_grad[2], qkv_grad[0], qkv_grad[1]], axis=1)

    return (
        layer_output,
        grad_input,
        gain_grads[0],
        qkv_grad,
        out_weight_grad,
        gain_grads[1],
        gu_grad,
        down_grad,
    )


def solution(mesh):
    return jax.shard_map(
        body,
        mesh=mesh,
        in_specs=(
            P(("fsdp", "ctx"), "tp"),
            P("tp"),
            P("fsdp", None, "tp"),
            P("tp", "fsdp"),
            P("tp"),
            P("fsdp", None, "tp"),
            P("tp", "fsdp"),
            P(("fsdp", "ctx"), "tp"),
        ),
        out_specs=(
            P(("fsdp", "ctx"), "tp"),
            P(("fsdp", "ctx"), "tp"),
            P("tp"),
            P(("fsdp", "ctx"), None, "tp"),
            P("tp", ("fsdp", "ctx")),
            P("tp"),
            P(("fsdp", "ctx"), None, "tp"),
            P("tp", ("fsdp", "ctx")),
        ),
        check_vma=False,
    )
```

```python
import math

import jax
import jax.numpy as jnp
from jax import lax
from jax.experimental import pallas as pl
from jax.experimental.layout import Layout, with_layout_constraint
from jax.experimental.pallas import tpu as pltpu
from jax.sharding import PartitionSpec as P

D = 4096
HD = 128
BF = jnp.bfloat16
F32 = jnp.float32
rms_epsilon = 1e-05
NT = (((1,), (1,)), ((), ()))
LOG2E = 1.4426950408889634


def mm(left, right, dims=(((1,), (0,)), ((), ()))):
    return lax.dot_general(left, right, dims, preferred_element_type=F32)


def turn(values, cosine, sine):
    return values * cosine + pltpu.roll(values, HD // 2, 1) * sine


def rope_tables(seq_len):
    half_width = HD // 2
    inv_freq = jnp.exp(-math.log(10000.0) * jnp.arange(half_width, dtype=F32) * 2.0 / HD)
    angles = jnp.arange(seq_len, dtype=F32)[:, None] * inv_freq[None, :]
    cosine, sine = jnp.cos(angles), jnp.sin(angles)
    return jnp.concatenate([cosine, cosine], axis=1), jnp.concatenate([-sine, sine], axis=1)


def attend_forward(query_proj, key_proj, value_proj, cosine, sine):
    seq_len = query_proj.shape[0]
    heads = query_proj.shape[1] // HD
    block = min(512, seq_len)
    blocks = seq_len // block
    scale = LOG2E / math.sqrt(HD)

    def kernel(q_in, k_in, v_in, cos_q, sin_q, cos_k, sin_k, q_out, k_out, v_out, out, norm, vt):
        i = pl.program_id(1)

        @pl.when(i == 0)
        def _():
            for j in range(blocks):
                rows = pl.ds(j * block, block)
                k_out[rows, :] = turn(k_in[rows, :], cos_k[rows, :], sin_k[rows, :]).astype(BF)
                v_out[rows, :] = v_in[rows, :].astype(BF)
                vt[j] = v_in[rows, :].T.astype(BF)

        q_out[...] = turn(q_in[...], cos_q[...], sin_q[...]).astype(BF)
        query = q_out[...]

        def step(j, carry, diagonal):
            top, total, mixed = carry
            rows = pl.ds(pl.multiple_of(j * block, block), block)
            scores = mm(k_out[rows, :], query, NT) * scale
            if diagonal:
                key_at = lax.broadcasted_iota(jnp.int32, scores.shape, 0)
                query_at = lax.broadcasted_iota(jnp.int32, scores.shape, 1)
                scores = jnp.where(key_at <= query_at, scores, -1e30)
            new_top = jnp.maximum(top, jnp.max(scores, axis=0, keepdims=True))
            expo = jnp.exp2(scores - new_top)
            fade = jnp.exp2(top - new_top)
            total = total * fade + jnp.sum(expo, axis=0, keepdims=True)
            mixed = mixed * fade + mm(vt[j], expo.astype(BF))
            return new_top, total, mixed

        carry = (
            jnp.full((1, block), -1e30, F32),
            jnp.zeros((1, block), F32),
            jnp.zeros((HD, block), F32),
        )
        carry = lax.fori_loop(0, i, lambda j, c: step(j, c, False), carry)
        top, total, mixed = step(i, carry, True)
        out[...] = (mixed / total).T.astype(BF)
        norm[0] = top + jnp.log2(total)

    row = pl.BlockSpec((block, HD), lambda h, i: (i, h))
    col = pl.BlockSpec((seq_len, HD), lambda h, i: (0, h))
    pos = pl.BlockSpec((block, HD), lambda h, i: (i, 0))
    all_pos = pl.BlockSpec((seq_len, HD), lambda h, i: (0, 0))
    wide = jax.ShapeDtypeStruct((seq_len, heads * HD), BF)
    pairs = heads * seq_len * (seq_len + block) // 2
    return pl.pallas_call(
        kernel,
        grid=(heads, blocks),
        in_specs=[row, col, col, pos, pos, all_pos, all_pos],
        out_specs=[row, col, col, row, pl.BlockSpec((1, 1, block), lambda h, i: (h, 0, i))],
        out_shape=[wide, wide, wide, wide, jax.ShapeDtypeStruct((heads, 1, seq_len), F32)],
        scratch_shapes=[pltpu.VMEM((blocks, HD, block), BF)],
        compiler_params=pltpu.CompilerParams(vmem_limit_bytes=48 << 20),
        cost_estimate=pl.CostEstimate(
            flops=30 * pairs * HD,
            transcendentals=pairs,
            bytes_accessed=seq_len * heads * HD * (12 + 8),
        ),
    )(query_proj, key_proj, value_proj, cosine, sine, cosine, sine)


def attend_backward(queries, keys, values, outs, norms, grads, cosine, sine):
    seq_len = queries.shape[0]
    heads = queries.shape[1] // HD
    block = min(512, seq_len)
    blocks = seq_len // block
    root = 1.0 / math.sqrt(HD)
    scale = LOG2E * root

    def kernel(q, k, v, o, g, norm, cos_q, sin_q, cos_k, sin_k, dq, dk, dv, kt, dk_sum, dv_sum):
        i = pl.program_id(1)

        @pl.when(i == 0)
        def _():
            for j in range(blocks):
                rows = pl.ds(j * block, block)
                kt[j] = k[rows, :].astype(F32).T.astype(BF)
            dk_sum[...] = jnp.zeros_like(dk_sum)
            dv_sum[...] = jnp.zeros_like(dv_sum)

        query = q[...]
        grad = g[...]
        dots = (grad.astype(F32) * o[...].astype(F32)).T
        weighted = jnp.sum(dots, axis=0, keepdims=True)
        level = norm[0]

        def step(j, total, diagonal):
            rows = pl.ds(pl.multiple_of(j * block, block), block)
            scores = mm(k[rows, :], query, NT) * scale
            probs = jnp.exp2(scores - level)
            if diagonal:
                key_at = lax.broadcasted_iota(jnp.int32, scores.shape, 0)
                query_at = lax.broadcasted_iota(jnp.int32, scores.shape, 1)
                probs = jnp.where(key_at <= query_at, probs, 0.0)
            dv_sum[rows, :] += mm(probs.astype(BF), grad)
            d_probs = mm(v[rows, :], grad, NT)
            d_scores = (probs * (d_probs - weighted)).astype(BF)
            dk_sum[rows, :] += mm(d_scores, query)
            return total + mm(kt[j], d_scores)

        total = lax.fori_loop(
            0, i, lambda j, c: step(j, c, False), jnp.zeros((HD, block), F32)
        )
        total = step(i, total, True)
        dq[...] = turn(total.T * root, cos_q[...], -sin_q[...]).astype(BF)

        @pl.when(i == blocks - 1)
        def _():
            for j in range(blocks):
                rows = pl.ds(j * block, block)
                dk[rows, :] = turn(
                    dk_sum[rows, :] * root, cos_k[rows, :], -sin_k[rows, :]
                ).astype(BF)
                dv[rows, :] = dv_sum[rows, :].astype(BF)

    row = pl.BlockSpec((block, HD), lambda h, i: (i, h))
    col = pl.BlockSpec((seq_len, HD), lambda h, i: (0, h))
    pos = pl.BlockSpec((block, HD), lambda h, i: (i, 0))
    all_pos = pl.BlockSpec((seq_len, HD), lambda h, i: (0, 0))
    wide = jax.ShapeDtypeStruct((seq_len, heads * HD), BF)
    pairs = heads * seq_len * (seq_len + block) // 2
    return pl.pallas_call(
        kernel,
        grid=(heads, blocks),
        in_specs=[row, col, col, row, row, pl.BlockSpec((1, 1, block), lambda h, i: (h, 0, i)),
                  pos, pos, all_pos, all_pos],
        out_specs=[row, col, col],
        out_shape=[wide, wide, wide],
        scratch_shapes=[
            pltpu.VMEM((blocks, HD, block), BF),
            pltpu.VMEM((seq_len, HD), F32),
            pltpu.VMEM((seq_len, HD), F32),
        ],
        compiler_params=pltpu.CompilerParams(vmem_limit_bytes=48 << 20),
        cost_estimate=pl.CostEstimate(
            flops=38 * pairs * HD,
            transcendentals=pairs,
            bytes_accessed=seq_len * heads * HD * 16,
        ),
    )(queries, keys, values, outs, grads, norms, cosine, sine, cosine, sine)


def row_total(values):
    return lax.psum(values, "tp")


def swap(values, axis, bit):
    step = 1 << bit
    return lax.ppermute(values, axis, [(i, i ^ step) for i in range(lax.axis_size(axis))])


def high_bits():
    return list(range(1, lax.axis_size("tp").bit_length() - 1))[::-1]


def gather_rows(values, arrived=None):
    rows, cols = values.shape
    half = rows // 2
    n_t, n_c = lax.axis_size("tp"), lax.axis_size("ctx")
    me_t, me_c = lax.axis_index("tp"), lax.axis_index("ctx")
    across = [("tp", b) for b in high_bits()]
    full = jnp.zeros((n_t, n_c * rows, cols), values.dtype)
    for part, plan in enumerate(([("ctx", 0)] + across, across + [("ctx", 0)])):
        held = {(0, 0): values[part * half : (part + 1) * half]}
        for axis, bit in plan + [("tp", 0)]:
            for (dc, dt), piece in list(held.items()):
                key = (1, dt) if axis == "ctx" else (dc, dt | (1 << bit))
                held[key] = swap(piece, axis, bit)
            if arrived is not None and len(held) == 2:
                arrived.append(held[key])
        for (dc, dt), piece in held.items():
            start = (me_t ^ dt, (me_c ^ dc) * rows + part * half, 0)
            full = lax.dynamic_update_slice(full, piece[None], start)
    return with_layout_constraint(full, Layout((0, 1, 2)))


def core_sums(block_of):
    n_t = lax.axis_size("tp")
    me_t = lax.axis_index("tp")
    sums = {}
    for dt in range(0, n_t, 2):
        got = swap(block_of(me_t ^ (dt + 1)).astype(BF), "tp", 0)
        sums[dt] = (block_of(me_t ^ dt) + got.astype(F32)).astype(BF)
    return sums


def scatter_sums(sums):
    n_c = lax.axis_size("ctx")
    me_c = lax.axis_index("ctx")
    rows = sums[0].shape[0] // n_c
    cols = sums[0].shape[1]
    half = rows // 2
    across = [("tp", b) for b in high_bits()]
    done = []
    for part, plan in enumerate(([("ctx", 0)] + across, across + [("ctx", 0)])):
        held = {}
        for dt, total in sums.items():
            split = total.reshape(n_c, rows, cols)[:, part * half : (part + 1) * half]
            for dc in range(n_c):
                held[(dc, dt)] = lax.dynamic_index_in_dim(split, me_c ^ dc, 0, keepdims=False)
        for axis, bit in plan:
            left = {}
            for (dc, dt), piece in held.items():
                give = dc == 1 if axis == "ctx" else (dt >> bit) & 1
                if not give:
                    away = (1, dt) if axis == "ctx" else (dc, dt | (1 << bit))
                    got = swap(held[away].astype(BF), axis, bit)
                    left[(dc, dt)] = piece.astype(F32) + got.astype(F32)
            held = left
        done.append(held[(0, 0)])
    return jnp.concatenate(done, axis=0)


def scatter_rows(block_of):
    return scatter_sums(core_sums(block_of))


def ctx_half(weight, axis):
    size = weight.shape[axis] // lax.axis_size("ctx")
    return lax.dynamic_slice_in_dim(weight, lax.axis_index("ctx") * size, size, axis)


def after(value, token):
    value, _ = lax.optimization_barrier((value, token))
    return value


def owners(grad):
    return lax.psum_scatter(grad, "fsdp", scatter_dimension=0, tiled=False)


def far_groups():
    count = lax.axis_size("fsdp")
    return [list(range(i, count, 2)) for i in range(2)]


def far_owners(grad):
    grad = grad.reshape((-1, 2) + grad.shape[1:])
    return lax.psum_scatter(
        grad, "fsdp", scatter_dimension=0, tiled=False, axis_index_groups=far_groups()
    )


def far_spread(weight):
    full = lax.all_gather(
        weight, "fsdp", axis=0, tiled=False, axis_index_groups=far_groups()
    )
    return full.reshape((-1,) + full.shape[2:])


def plane():
    return lax.axis_index("fsdp") & 1


def near(values):
    return swap(values, "fsdp", 0)


def in_pair(mine, other):
    return jnp.where(plane() == 0, mine, other), jnp.where(plane() == 0, other, mine)


def pair_share(block, axis, token, hold):
    count = 2 * lax.axis_size("ctx")
    size = block.shape[axis] // count
    place = lax.axis_index("ctx") * 2

    def columns(index):
        return lax.dynamic_slice_in_dim(block, (place + index) * size, size, axis)

    other = near(after(columns(1 - plane()), token))
    return jnp.stack(in_pair(columns(plane()), after(other, hold)))


def pair_grad(block, axis):
    mine = lax.dynamic_index_in_dim(block, plane(), 0, keepdims=False)
    give = lax.dynamic_index_in_dim(block, 1 - plane(), 0, keepdims=False)
    both = trade_ctx(jnp.stack(in_pair(mine, near(give))), axis + 1)
    return [v[i] for v in both for i in range(2)]


def spread(weight):
    return lax.all_gather(weight, "fsdp", axis=0, tiled=False)


def trade_ctx(block, axis):
    size = block.shape[axis] // lax.axis_size("ctx")
    me = lax.axis_index("ctx")
    own = lax.dynamic_slice_in_dim(block, me * size, size, axis)
    give = lax.dynamic_slice_in_dim(block, (1 - me) * size, size, axis)
    got = swap(give, "ctx", 0)
    return jnp.where(me == 0, own, got), jnp.where(me == 0, got, own)


def out_grad(block):
    return jnp.concatenate(trade_ctx(block, 1), axis=0).astype(F32)


def total_rows(values):
    values = values + swap(values, "ctx", 0)
    for bit in range(lax.axis_size("fsdp").bit_length() - 1):
        values = values + swap(values, "fsdp", bit)
    return values


def body(
    layer_input, attn_gain, qkv_weight, out_weight, ffn_gain, gate_up_weight, down_weight, cotangent
):
    n_f = lax.axis_size("fsdp")
    d_f = D // n_f
    qkv_full = spread(ctx_half(jnp.swapaxes(qkv_weight, 0, 1), 2))
    qkv_parts = [qkv_full[:, i] for i in range(3)]
    out_full = spread(ctx_half(out_weight, 0))

    def into(full, weight):
        return mm(full, weight, (((0, 2), (0, 1)), ((), ())))

    def back_out(full, weight):
        return mm(full, weight, (((0, 2), (0, 2)), ((), ())))

    def out_blocks(inner, weight):
        return lambda t: mm(inner, lax.dynamic_index_in_dim(weight, t, 0, keepdims=False))

    def in_blocks(grads, weight):
        return lambda t: mm(grads, lax.dynamic_index_in_dim(weight, t, 0, keepdims=False), NT)

    def in_sum(full, grads):
        return mm(full, grads, (((1,), (0,)), ((), ())))

    def in_part(full, grads):
        return in_sum(full, grads).astype(BF)

    def out_part(inner, full):
        def block(t):
            return sum(mm(v, f[t], (((0,), (0,)), ((), ()))) for v, f in zip(inner, full))

        return jnp.stack([block(t).astype(BF) for t in range(n_f)])

    input_float = layer_input.astype(F32)
    attn_scale = attn_gain.astype(F32)
    ffn_scale = ffn_gain.astype(F32)
    rms_one = lax.rsqrt(row_total(jnp.sum(input_float * input_float, axis=-1)) / D + rms_epsilon)[
        :, None
    ]
    normed_attn = (input_float * rms_one * attn_scale).astype(BF)
    attn_full = gather_rows(normed_attn)
    seq_len = attn_full.shape[1]
    cosine, sine = rope_tables(seq_len)
    cotans = [gather_rows(after(cotangent, attn_full))]
    proj = after([into(attn_full, part) for part in qkv_parts], cotans[0])
    queries, keys, values, head_outs, norms = attend_forward(*proj, cosine, sine)
    sums = core_sums(out_blocks(head_outs, out_full))
    gu_share = pair_share(gate_up_weight, 2, tuple(proj), tuple(sums.values()))
    gu_full = far_spread(gu_share.reshape(2, d_f, -1))
    down_share = pair_share(down_weight, 0, gu_share, gu_share)
    resid = after(input_float + scatter_sums(sums), down_share)
    rms_two = lax.rsqrt(row_total(jnp.sum(resid * resid, axis=-1)) / D + rms_epsilon)[:, None]
    normed_ffn = (resid * rms_two * ffn_scale).astype(BF)
    down_full = far_spread(down_share)
    tokens = [gather_rows(normed_ffn), gather_rows(near(normed_ffn))]
    cotans.append(gather_rows(after(near(after(cotangent, tokens[0])), tokens[1])))
    inner = []
    for part in tokens:
        gate_up = into(part, gu_full)
        units = gate_up.shape[1] // 2
        gate = gate_up[:, :units]
        up_value = gate_up[:, units:]
        sigma = jax.nn.sigmoid(gate)
        inner.append((gate, up_value, sigma, (gate * sigma * up_value).astype(BF)))
    hidden = [v[3] for v in inner]
    down_part = out_part(hidden, cotans)
    down_sum = far_owners(down_part)
    down_full = after(down_full, down_part)
    grad_gu = []
    for cotan, (gate, up_value, sigma, _) in zip(cotans, inner):
        grad_hidden = back_out(cotan, down_full)
        grad_gu.append(
            jnp.concatenate(
                [
                    grad_hidden * up_value * sigma * (1.0 + gate * (1.0 - sigma)),
                    grad_hidden * gate * sigma,
                ],
                axis=1,
            ).astype(BF)
        )
    sums_near = core_sums(in_blocks(grad_gu[1], gu_full))
    sums_own = core_sums(in_blocks(after(grad_gu[0], tuple(sums_near.values())), gu_full))
    grad_gu = after(grad_gu, tuple(sums_own.values()))
    gu_part = [
        sum(in_sum(t, g[:, i * units : (i + 1) * units]) for t, g in zip(tokens, grad_gu))
        for i in range(2)
    ]
    gu_part = [part.astype(BF) for part in gu_part]
    gu_sum = [far_owners(after(part, down_sum)) for part in gu_part]
    grad_nffn = scatter_sums(sums_own) + near(scatter_sums(sums_near).astype(BF)).astype(F32)
    grad_nffn = after(grad_nffn, gu_part)
    ffn_term = grad_nffn * ffn_scale
    ffn_dot = row_total(jnp.sum(ffn_term * resid, axis=-1))[:, None]
    grad_resid = cotangent.astype(F32) + rms_two * ffn_term - resid * rms_two**3 * ffn_dot / D
    ffn_gain_part = jnp.sum(grad_nffn * resid * rms_two, axis=0)
    grad_branch = grad_resid.astype(BF)
    arrived = []
    branch_full = gather_rows(grad_branch, arrived)
    hidden = after(hidden, arrived)
    sums_near = core_sums(out_blocks(hidden[1], down_full))
    sums_own = core_sums(out_blocks(hidden[0], down_full))
    down_grad = jnp.concatenate(pair_grad(down_sum, 1), axis=0).astype(F32)
    grad_heads = back_out(branch_full, out_full).astype(BF)
    grad_heads = after(grad_heads, (sums_near, sums_own, down_grad))
    ffn_out = scatter_sums(sums_own) + near(scatter_sums(sums_near).astype(BF)).astype(F32)
    layer_output = (resid + ffn_out).astype(BF)
    gate_grad = pair_grad(gu_sum[0], 0)
    out_sum = owners(out_part([head_outs], [branch_full]))
    grad_proj = attend_backward(
        queries, keys, values, head_outs, norms, grad_heads, cosine, sine
    )
    qkv_part = [
        in_part(attn_full, jnp.concatenate(grad_proj[1:], axis=1)),
        in_part(attn_full, grad_proj[0]),
    ]
    qkv_sum = [owners(part) for part in qkv_part]
    grad_proj = after(grad_proj, (layer_output, gate_grad))
    grad_nattn = scatter_rows(
        in_blocks(jnp.concatenate(grad_proj, axis=1), jnp.concatenate(qkv_parts, axis=2))
    )
    attn_term = grad_nattn * attn_scale
    attn_dot = row_total(jnp.sum(attn_term * input_float, axis=-1))[:, None]
    grad_input = grad_resid + rms_one * attn_term - input_float * rms_one**3 * attn_dot / D
    attn_gain_part = jnp.sum(grad_nattn * input_float * rms_one, axis=0)
    gain_grads = total_rows(jnp.stack([attn_gain_part, ffn_gain_part]))

    gu_grad = jnp.stack(
        [jnp.concatenate(v, axis=1) for v in (gate_grad, pair_grad(gu_sum[1], 0))], axis=1
    ).astype(F32)
    out_weight_grad = out_grad(out_sum)
    done = (down_grad, out_weight_grad, gu_grad, grad_input, layer_output, gain_grads)
    qkv_grad = []
    for part in qkv_sum:
        first, second = trade_ctx(after(part, done), 0)
        wide = queries.shape[1]
        for i in range(0, first.shape[1], wide):
            both = [first[:, i : i + wide], second[:, i : i + wide]]
            qkv_grad.append(jnp.concatenate(both, axis=1).astype(F32))
        done = done + (qkv_grad[-1],)
    qkv_grad = jnp.stack([qkv_grad[2], qkv_grad[0], qkv_grad[1]], axis=1)

    return (
        layer_output,
        grad_input,
        gain_grads[0],
        qkv_grad,
        out_weight_grad,
        gain_grads[1],
        gu_grad,
        down_grad,
    )


def solution(mesh):
    return jax.shard_map(
        body,
        mesh=mesh,
        in_specs=(
            P(("fsdp", "ctx"), "tp"),
            P("tp"),
            P("fsdp", None, "tp"),
            P("tp", "fsdp"),
            P("tp"),
            P("fsdp", None, "tp"),
            P("tp", "fsdp"),
            P(("fsdp", "ctx"), "tp"),
        ),
        out_specs=(
            P(("fsdp", "ctx"), "tp"),
            P(("fsdp", "ctx"), "tp"),
            P("tp"),
            P(("fsdp", "ctx"), None, "tp"),
            P("tp", ("fsdp", "ctx")),
            P("tp"),
            P(("fsdp", "ctx"), None, "tp"),
            P("tp", ("fsdp", "ctx")),
        ),
        check_vma=False,
    )
```

```python
import math

import jax
import jax.numpy as jnp
from jax import lax
from jax.experimental import pallas as pl
from jax.experimental.layout import Layout, with_layout_constraint
from jax.experimental.pallas import tpu as pltpu
from jax.sharding import PartitionSpec as P

D = 4096
HD = 128
BF = jnp.bfloat16
F32 = jnp.float32
rms_epsilon = 1e-05
NT = (((1,), (1,)), ((), ()))
LOG2E = 1.4426950408889634


def mm(left, right, dims=(((1,), (0,)), ((), ()))):
    return lax.dot_general(left, right, dims, preferred_element_type=F32)


def turn(values, cosine, sine):
    return values * cosine + pltpu.roll(values, HD // 2, 1) * sine


def rope_tables(seq_len):
    half_width = HD // 2
    inv_freq = jnp.exp(-math.log(10000.0) * jnp.arange(half_width, dtype=F32) * 2.0 / HD)
    angles = jnp.arange(seq_len, dtype=F32)[:, None] * inv_freq[None, :]
    cosine, sine = jnp.cos(angles), jnp.sin(angles)
    return jnp.concatenate([cosine, cosine], axis=1), jnp.concatenate([-sine, sine], axis=1)


def attend_forward(query_proj, key_proj, value_proj, cosine, sine):
    seq_len = query_proj.shape[0]
    heads = query_proj.shape[1] // HD
    block = min(512, seq_len)
    blocks = seq_len // block
    scale = LOG2E / math.sqrt(HD)

    def kernel(q_in, k_in, v_in, cos_q, sin_q, cos_k, sin_k, q_out, k_out, v_out, out, norm, vt):
        i = pl.program_id(1)

        @pl.when(i == 0)
        def _():
            for j in range(blocks):
                rows = pl.ds(j * block, block)
                k_out[rows, :] = turn(k_in[rows, :], cos_k[rows, :], sin_k[rows, :]).astype(BF)
                v_out[rows, :] = v_in[rows, :].astype(BF)
                vt[j] = v_in[rows, :].T.astype(BF)

        q_out[...] = turn(q_in[...], cos_q[...], sin_q[...]).astype(BF)
        query = q_out[...]

        def step(j, carry, diagonal):
            top, total, mixed = carry
            rows = pl.ds(pl.multiple_of(j * block, block), block)
            scores = mm(k_out[rows, :], query, NT) * scale
            if diagonal:
                key_at = lax.broadcasted_iota(jnp.int32, scores.shape, 0)
                query_at = lax.broadcasted_iota(jnp.int32, scores.shape, 1)
                scores = jnp.where(key_at <= query_at, scores, -1e30)
            new_top = jnp.maximum(top, jnp.max(scores, axis=0, keepdims=True))
            expo = jnp.exp2(scores - new_top)
            fade = jnp.exp2(top - new_top)
            total = total * fade + jnp.sum(expo, axis=0, keepdims=True)
            mixed = mixed * fade + mm(vt[j], expo.astype(BF))
            return new_top, total, mixed

        carry = (
            jnp.full((1, block), -1e30, F32),
            jnp.zeros((1, block), F32),
            jnp.zeros((HD, block), F32),
        )
        carry = lax.fori_loop(0, i, lambda j, c: step(j, c, False), carry)
        top, total, mixed = step(i, carry, True)
        out[...] = (mixed / total).T.astype(BF)
        norm[0] = top + jnp.log2(total)

    row = pl.BlockSpec((block, HD), lambda h, i: (i, h))
    col = pl.BlockSpec((seq_len, HD), lambda h, i: (0, h))
    pos = pl.BlockSpec((block, HD), lambda h, i: (i, 0))
    all_pos = pl.BlockSpec((seq_len, HD), lambda h, i: (0, 0))
    wide = jax.ShapeDtypeStruct((seq_len, heads * HD), BF)
    pairs = heads * seq_len * (seq_len + block) // 2
    return pl.pallas_call(
        kernel,
        grid=(heads, blocks),
        in_specs=[row, col, col, pos, pos, all_pos, all_pos],
        out_specs=[row, col, col, row, pl.BlockSpec((1, 1, block), lambda h, i: (h, 0, i))],
        out_shape=[wide, wide, wide, wide, jax.ShapeDtypeStruct((heads, 1, seq_len), F32)],
        scratch_shapes=[pltpu.VMEM((blocks, HD, block), BF)],
        compiler_params=pltpu.CompilerParams(vmem_limit_bytes=48 << 20),
        cost_estimate=pl.CostEstimate(
            flops=4 * pairs * HD,
            transcendentals=pairs,
            bytes_accessed=seq_len * heads * HD * (12 + 8),
        ),
    )(query_proj, key_proj, value_proj, cosine, sine, cosine, sine)


def attend_backward(queries, keys, values, outs, norms, grads, cosine, sine):
    seq_len = queries.shape[0]
    heads = queries.shape[1] // HD
    block = min(512, seq_len)
    blocks = seq_len // block
    root = 1.0 / math.sqrt(HD)
    scale = LOG2E * root

    def kernel(q, k, v, o, g, norm, cos_q, sin_q, cos_k, sin_k, dq, dk, dv, kt, dk_sum, dv_sum):
        i = pl.program_id(1)

        @pl.when(i == 0)
        def _():
            for j in range(blocks):
                rows = pl.ds(j * block, block)
                kt[j] = k[rows, :].astype(F32).T.astype(BF)
            dk_sum[...] = jnp.zeros_like(dk_sum)
            dv_sum[...] = jnp.zeros_like(dv_sum)

        query = q[...]
        grad = g[...]
        dots = (grad.astype(F32) * o[...].astype(F32)).T
        weighted = jnp.sum(dots, axis=0, keepdims=True)
        level = norm[0]

        def step(j, total, diagonal):
            rows = pl.ds(pl.multiple_of(j * block, block), block)
            scores = mm(k[rows, :], query, NT) * scale
            probs = jnp.exp2(scores - level)
            if diagonal:
                key_at = lax.broadcasted_iota(jnp.int32, scores.shape, 0)
                query_at = lax.broadcasted_iota(jnp.int32, scores.shape, 1)
                probs = jnp.where(key_at <= query_at, probs, 0.0)
            dv_sum[rows, :] += mm(probs.astype(BF), grad)
            d_probs = mm(v[rows, :], grad, NT)
            d_scores = (probs * (d_probs - weighted)).astype(BF)
            dk_sum[rows, :] += mm(d_scores, query)
            return total + mm(kt[j], d_scores)

        total = lax.fori_loop(
            0, i, lambda j, c: step(j, c, False), jnp.zeros((HD, block), F32)
        )
        total = step(i, total, True)
        dq[...] = turn(total.T * root, cos_q[...], -sin_q[...]).astype(BF)

        @pl.when(i == blocks - 1)
        def _():
            for j in range(blocks):
                rows = pl.ds(j * block, block)
                dk[rows, :] = turn(
                    dk_sum[rows, :] * root, cos_k[rows, :], -sin_k[rows, :]
                ).astype(BF)
                dv[rows, :] = dv_sum[rows, :].astype(BF)

    row = pl.BlockSpec((block, HD), lambda h, i: (i, h))
    col = pl.BlockSpec((seq_len, HD), lambda h, i: (0, h))
    pos = pl.BlockSpec((block, HD), lambda h, i: (i, 0))
    all_pos = pl.BlockSpec((seq_len, HD), lambda h, i: (0, 0))
    wide = jax.ShapeDtypeStruct((seq_len, heads * HD), BF)
    pairs = heads * seq_len * (seq_len + block) // 2
    return pl.pallas_call(
        kernel,
        grid=(heads, blocks),
        in_specs=[row, col, col, row, row, pl.BlockSpec((1, 1, block), lambda h, i: (h, 0, i)),
                  pos, pos, all_pos, all_pos],
        out_specs=[row, col, col],
        out_shape=[wide, wide, wide],
        scratch_shapes=[
            pltpu.VMEM((blocks, HD, block), BF),
            pltpu.VMEM((seq_len, HD), F32),
            pltpu.VMEM((seq_len, HD), F32),
        ],
        compiler_params=pltpu.CompilerParams(vmem_limit_bytes=48 << 20),
        cost_estimate=pl.CostEstimate(
            flops=10 * pairs * HD,
            transcendentals=pairs,
            bytes_accessed=seq_len * heads * HD * 16,
        ),
    )(queries, keys, values, outs, grads, norms, cosine, sine, cosine, sine)


def row_total(values):
    return lax.psum(values, "tp")


def swap(values, axis, bit):
    step = 1 << bit
    return lax.ppermute(values, axis, [(i, i ^ step) for i in range(lax.axis_size(axis))])


def high_bits():
    return list(range(1, lax.axis_size("tp").bit_length() - 1))[::-1]


def gather_rows(values):
    rows, cols = values.shape
    half = rows // 2
    n_t, n_c = lax.axis_size("tp"), lax.axis_size("ctx")
    me_t, me_c = lax.axis_index("tp"), lax.axis_index("ctx")
    across = [("tp", b) for b in high_bits()]
    full = jnp.zeros((n_t, n_c * rows, cols), values.dtype)
    for part, plan in enumerate(([("ctx", 0)] + across, across + [("ctx", 0)])):
        held = {(0, 0): values[part * half : (part + 1) * half]}
        for axis, bit in plan + [("tp", 0)]:
            for (dc, dt), piece in list(held.items()):
                key = (1, dt) if axis == "ctx" else (dc, dt | (1 << bit))
                held[key] = swap(piece, axis, bit)
        for (dc, dt), piece in held.items():
            start = (me_t ^ dt, (me_c ^ dc) * rows + part * half, 0)
            full = lax.dynamic_update_slice(full, piece[None], start)
    return with_layout_constraint(full, Layout((0, 1, 2)))


def scatter_rows(block_of):
    n_t, n_c = lax.axis_size("tp"), lax.axis_size("ctx")
    me_t, me_c = lax.axis_index("tp"), lax.axis_index("ctx")
    sums = {}
    for dt in range(0, n_t, 2):
        got = swap(block_of(me_t ^ (dt + 1)).astype(BF), "tp", 0)
        sums[dt] = (block_of(me_t ^ dt) + got.astype(F32)).astype(BF)
    rows = sums[0].shape[0] // n_c
    cols = sums[0].shape[1]
    half = rows // 2
    across = [("tp", b) for b in high_bits()]
    done = []
    for part, plan in enumerate(([("ctx", 0)] + across, across + [("ctx", 0)])):
        held = {}
        for dt, total in sums.items():
            split = total.reshape(n_c, rows, cols)[:, part * half : (part + 1) * half]
            for dc in range(n_c):
                held[(dc, dt)] = lax.dynamic_index_in_dim(split, me_c ^ dc, 0, keepdims=False)
        for axis, bit in plan:
            left = {}
            for (dc, dt), piece in held.items():
                give = dc == 1 if axis == "ctx" else (dt >> bit) & 1
                if not give:
                    away = (1, dt) if axis == "ctx" else (dc, dt | (1 << bit))
                    got = swap(held[away].astype(BF), axis, bit)
                    left[(dc, dt)] = piece.astype(F32) + got.astype(F32)
            held = left
        done.append(held[(0, 0)])
    return jnp.concatenate(done, axis=0)


def ctx_half(weight, axis):
    size = weight.shape[axis] // lax.axis_size("ctx")
    return lax.dynamic_slice_in_dim(weight, lax.axis_index("ctx") * size, size, axis)


def after(value, token):
    value, _ = lax.optimization_barrier((value, token))
    return value


def owners(grad):
    return lax.psum_scatter(grad, "fsdp", scatter_dimension=0, tiled=False)


def spread(weight):
    return lax.all_gather(weight, "fsdp", axis=0, tiled=False)


def trade_ctx(block, axis):
    size = block.shape[axis] // lax.axis_size("ctx")
    me = lax.axis_index("ctx")
    own = lax.dynamic_slice_in_dim(block, me * size, size, axis)
    give = lax.dynamic_slice_in_dim(block, (1 - me) * size, size, axis)
    got = swap(give, "ctx", 0)
    return jnp.where(me == 0, own, got), jnp.where(me == 0, got, own)


def out_grad(block):
    return jnp.concatenate(trade_ctx(block, 1), axis=0).astype(F32)


def total_rows(values):
    values = values + swap(values, "ctx", 0)
    for bit in range(lax.axis_size("fsdp").bit_length() - 1):
        values = values + swap(values, "fsdp", bit)
    return values


def body(
    layer_input, attn_gain, qkv_weight, out_weight, ffn_gain, gate_up_weight, down_weight, cotangent
):
    n_f = lax.axis_size("fsdp")
    d_f = D // n_f
    qkv_full = spread(ctx_half(jnp.swapaxes(qkv_weight, 0, 1), 2))
    qkv_parts = [qkv_full[:, i] for i in range(3)]
    out_full = spread(ctx_half(out_weight, 0))
    gu_full = spread(ctx_half(gate_up_weight, 2).reshape(d_f, -1))
    down_full = spread(ctx_half(down_weight, 0))

    def into(full, weight):
        return mm(full, weight, (((0, 2), (0, 1)), ((), ())))

    def back_out(full, weight):
        return mm(full, weight, (((0, 2), (0, 2)), ((), ())))

    def out_blocks(inner, weight):
        return lambda t: mm(inner, lax.dynamic_index_in_dim(weight, t, 0, keepdims=False))

    def in_blocks(grads, weight):
        return lambda t: mm(grads, lax.dynamic_index_in_dim(weight, t, 0, keepdims=False), NT)

    def in_part(full, grads):
        return mm(full, grads, (((1,), (0,)), ((), ()))).astype(BF)

    def out_part(inner, full):
        return jnp.stack(
            [mm(inner, full[t], (((0,), (0,)), ((), ()))).astype(BF) for t in range(n_f)]
        )

    input_float = layer_input.astype(F32)
    attn_scale = attn_gain.astype(F32)
    ffn_scale = ffn_gain.astype(F32)
    rms_one = lax.rsqrt(row_total(jnp.sum(input_float * input_float, axis=-1)) / D + rms_epsilon)[
        :, None
    ]
    normed_attn = (input_float * rms_one * attn_scale).astype(BF)
    attn_full = gather_rows(normed_attn)
    seq_len = attn_full.shape[1]
    cosine, sine = rope_tables(seq_len)
    cotan_full = gather_rows(after(cotangent, attn_full))
    proj = [into(attn_full, part) for part in qkv_parts]
    queries, keys, values, head_outs, norms = attend_forward(*proj, cosine, sine)
    resid = input_float + scatter_rows(out_blocks(head_outs, out_full))
    rms_two = lax.rsqrt(row_total(jnp.sum(resid * resid, axis=-1)) / D + rms_epsilon)[:, None]
    normed_ffn = (resid * rms_two * ffn_scale).astype(BF)
    ffn_full = gather_rows(normed_ffn)
    gate_up = into(ffn_full, gu_full)
    units = gate_up.shape[1] // 2
    gate = gate_up[:, :units]
    up_value = gate_up[:, units:]
    sigma = jax.nn.sigmoid(gate)
    hidden = (gate * sigma * up_value).astype(BF)
    down_part = out_part(hidden, cotan_full)
    down_sum = owners(down_part)
    down_full = after(down_full, down_part)
    grad_hidden = back_out(cotan_full, down_full)
    grad_gu = jnp.concatenate(
        [grad_hidden * up_value * sigma * (1.0 + gate * (1.0 - sigma)), grad_hidden * gate * sigma],
        axis=1,
    ).astype(BF)
    gu_part = in_part(ffn_full, grad_gu)
    gu_sum = owners(after(gu_part, down_sum))
    grad_nffn = after(scatter_rows(in_blocks(grad_gu, gu_full)), (gu_part, down_sum))
    ffn_term = grad_nffn * ffn_scale
    ffn_dot = row_total(jnp.sum(ffn_term * resid, axis=-1))[:, None]
    grad_resid = cotangent.astype(F32) + rms_two * ffn_term - resid * rms_two**3 * ffn_dot / D
    ffn_gain_part = jnp.sum(grad_nffn * resid * rms_two, axis=0)
    grad_branch = grad_resid.astype(BF)
    branch_full = gather_rows(grad_branch)
    grad_heads = back_out(branch_full, out_full).astype(BF)
    out_sum = owners(out_part(head_outs, branch_full))
    grad_proj = attend_backward(
        queries, keys, values, head_outs, norms, grad_heads, cosine, sine
    )
    qkv_part = [
        in_part(attn_full, jnp.concatenate(grad_proj[1:], axis=1)),
        in_part(attn_full, grad_proj[0]),
    ]
    qkv_sum = [owners(part) for part in qkv_part]
    grad_nattn = scatter_rows(
        in_blocks(jnp.concatenate(grad_proj, axis=1), jnp.concatenate(qkv_parts, axis=2))
    )
    hidden = after(hidden, qkv_part)
    layer_output = (resid + scatter_rows(out_blocks(hidden, down_full))).astype(BF)
    attn_term = grad_nattn * attn_scale
    attn_dot = row_total(jnp.sum(attn_term * input_float, axis=-1))[:, None]
    grad_input = grad_resid + rms_one * attn_term - input_float * rms_one**3 * attn_dot / D
    attn_gain_part = jnp.sum(grad_nattn * input_float * rms_one, axis=0)
    gain_grads = total_rows(jnp.stack([attn_gain_part, ffn_gain_part]))

    down_grad = out_grad(down_sum)
    rows, other_rows = trade_ctx(gu_sum, 0)
    gu_grad = jnp.concatenate(
        [v.reshape(v.shape[0], 2, -1) for v in (rows, other_rows)], axis=2
    ).astype(F32)
    out_weight_grad = out_grad(out_sum)
    done = (down_grad, out_weight_grad, gu_grad, grad_input, layer_output, gain_grads)
    qkv_grad = []
    for part in qkv_sum:
        first, second = trade_ctx(after(part, done), 0)
        wide = queries.shape[1]
        for i in range(0, first.shape[1], wide):
            both = [first[:, i : i + wide], second[:, i : i + wide]]
            qkv_grad.append(jnp.concatenate(both, axis=1).astype(F32))
        done = done + (qkv_grad[-1],)
    qkv_grad = jnp.stack([qkv_grad[2], qkv_grad[0], qkv_grad[1]], axis=1)

    return (
        layer_output,
        grad_input,
        gain_grads[0],
        qkv_grad,
        out_weight_grad,
        gain_grads[1],
        gu_grad,
        down_grad,
    )


def solution(mesh):
    return jax.shard_map(
        body,
        mesh=mesh,
        in_specs=(
            P(("fsdp", "ctx"), "tp"),
            P("tp"),
            P("fsdp", None, "tp"),
            P("tp", "fsdp"),
            P("tp"),
            P("fsdp", None, "tp"),
            P("tp", "fsdp"),
            P(("fsdp", "ctx"), "tp"),
        ),
        out_specs=(
            P(("fsdp", "ctx"), "tp"),
            P(("fsdp", "ctx"), "tp"),
            P("tp"),
            P(("fsdp", "ctx"), None, "tp"),
            P("tp", ("fsdp", "ctx")),
            P("tp"),
            P(("fsdp", "ctx"), None, "tp"),
            P("tp", ("fsdp", "ctx")),
        ),
        check_vma=False,
    )
```

```python
import math

import jax
import jax.numpy as jnp
from jax import lax
from jax.experimental import pallas as pl
from jax.experimental.layout import Layout, with_layout_constraint
from jax.experimental.pallas import tpu as pltpu
from jax.sharding import PartitionSpec as P

D = 4096
HD = 128
BF = jnp.bfloat16
F32 = jnp.float32
rms_epsilon = 1e-05
NT = (((1,), (1,)), ((), ()))
LOG2E = 1.4426950408889634


def mm(left, right, dims=(((1,), (0,)), ((), ()))):
    return lax.dot_general(left, right, dims, preferred_element_type=F32)


def turn(values, cosine, sine):
    return values * cosine + pltpu.roll(values, HD // 2, 1) * sine


def rope_tables(seq_len):
    half_width = HD // 2
    inv_freq = jnp.exp(-math.log(10000.0) * jnp.arange(half_width, dtype=F32) * 2.0 / HD)
    angles = jnp.arange(seq_len, dtype=F32)[:, None] * inv_freq[None, :]
    cosine, sine = jnp.cos(angles), jnp.sin(angles)
    return jnp.concatenate([cosine, cosine], axis=1), jnp.concatenate([-sine, sine], axis=1)


def attend_forward(query_proj, key_proj, value_proj, cosine, sine):
    seq_len = query_proj.shape[0]
    heads = query_proj.shape[1] // HD
    block = min(512, seq_len)
    blocks = seq_len // block
    scale = LOG2E / math.sqrt(HD)

    def kernel(q_in, k_in, v_in, cos_q, sin_q, cos_k, sin_k, q_out, k_out, v_out, out, norm, vt):
        i = pl.program_id(1)

        @pl.when(i == 0)
        def _():
            for j in range(blocks):
                rows = pl.ds(j * block, block)
                k_out[rows, :] = turn(k_in[rows, :], cos_k[rows, :], sin_k[rows, :]).astype(BF)
                v_out[rows, :] = v_in[rows, :].astype(BF)
                vt[j] = v_in[rows, :].T.astype(BF)

        q_out[...] = turn(q_in[...], cos_q[...], sin_q[...]).astype(BF)
        query = q_out[...]

        def step(j, carry, diagonal):
            top, total, mixed = carry
            rows = pl.ds(pl.multiple_of(j * block, block), block)
            scores = mm(k_out[rows, :], query, NT) * scale
            if diagonal:
                key_at = lax.broadcasted_iota(jnp.int32, scores.shape, 0)
                query_at = lax.broadcasted_iota(jnp.int32, scores.shape, 1)
                scores = jnp.where(key_at <= query_at, scores, -1e30)
            new_top = jnp.maximum(top, jnp.max(scores, axis=0, keepdims=True))
            expo = jnp.exp2(scores - new_top)
            fade = jnp.exp2(top - new_top)
            total = total * fade + jnp.sum(expo, axis=0, keepdims=True)
            mixed = mixed * fade + mm(vt[j], expo.astype(BF))
            return new_top, total, mixed

        carry = (
            jnp.full((1, block), -1e30, F32),
            jnp.zeros((1, block), F32),
            jnp.zeros((HD, block), F32),
        )
        carry = lax.fori_loop(0, i, lambda j, c: step(j, c, False), carry)
        top, total, mixed = step(i, carry, True)
        out[...] = (mixed / total).T.astype(BF)
        norm[0] = top + jnp.log2(total)

    row = pl.BlockSpec((block, HD), lambda h, i: (i, h))
    col = pl.BlockSpec((seq_len, HD), lambda h, i: (0, h))
    pos = pl.BlockSpec((block, HD), lambda h, i: (i, 0))
    all_pos = pl.BlockSpec((seq_len, HD), lambda h, i: (0, 0))
    wide = jax.ShapeDtypeStruct((seq_len, heads * HD), BF)
    pairs = heads * seq_len * (seq_len + block) // 2
    return pl.pallas_call(
        kernel,
        grid=(heads, blocks),
        in_specs=[row, col, col, pos, pos, all_pos, all_pos],
        out_specs=[row, col, col, row, pl.BlockSpec((1, 1, block), lambda h, i: (h, 0, i))],
        out_shape=[wide, wide, wide, wide, jax.ShapeDtypeStruct((heads, 1, seq_len), F32)],
        scratch_shapes=[pltpu.VMEM((blocks, HD, block), BF)],
        compiler_params=pltpu.CompilerParams(vmem_limit_bytes=48 << 20),
        cost_estimate=pl.CostEstimate(
            flops=30 * pairs * HD,
            transcendentals=pairs,
            bytes_accessed=seq_len * heads * HD * (12 + 8),
        ),
    )(query_proj, key_proj, value_proj, cosine, sine, cosine, sine)


def attend_backward(queries, keys, values, outs, norms, grads, cosine, sine):
    seq_len = queries.shape[0]
    heads = queries.shape[1] // HD
    block = min(512, seq_len)
    blocks = seq_len // block
    root = 1.0 / math.sqrt(HD)
    scale = LOG2E * root

    def kernel(q, k, v, o, g, norm, cos_q, sin_q, cos_k, sin_k, dq, dk, dv, kt, dk_sum, dv_sum):
        i = pl.program_id(1)

        @pl.when(i == 0)
        def _():
            for j in range(blocks):
                rows = pl.ds(j * block, block)
                kt[j] = k[rows, :].astype(F32).T.astype(BF)
            dk_sum[...] = jnp.zeros_like(dk_sum)
            dv_sum[...] = jnp.zeros_like(dv_sum)

        query = q[...]
        grad = g[...]
        dots = (grad.astype(F32) * o[...].astype(F32)).T
        weighted = jnp.sum(dots, axis=0, keepdims=True)
        level = norm[0]

        def step(j, total, diagonal):
            rows = pl.ds(pl.multiple_of(j * block, block), block)
            scores = mm(k[rows, :], query, NT) * scale
            probs = jnp.exp2(scores - level)
            if diagonal:
                key_at = lax.broadcasted_iota(jnp.int32, scores.shape, 0)
                query_at = lax.broadcasted_iota(jnp.int32, scores.shape, 1)
                probs = jnp.where(key_at <= query_at, probs, 0.0)
            dv_sum[rows, :] += mm(probs.astype(BF), grad)
            d_probs = mm(v[rows, :], grad, NT)
            d_scores = (probs * (d_probs - weighted)).astype(BF)
            dk_sum[rows, :] += mm(d_scores, query)
            return total + mm(kt[j], d_scores)

        total = lax.fori_loop(
            0, i, lambda j, c: step(j, c, False), jnp.zeros((HD, block), F32)
        )
        total = step(i, total, True)
        dq[...] = turn(total.T * root, cos_q[...], -sin_q[...]).astype(BF)

        @pl.when(i == blocks - 1)
        def _():
            for j in range(blocks):
                rows = pl.ds(j * block, block)
                dk[rows, :] = turn(
                    dk_sum[rows, :] * root, cos_k[rows, :], -sin_k[rows, :]
                ).astype(BF)
                dv[rows, :] = dv_sum[rows, :].astype(BF)

    row = pl.BlockSpec((block, HD), lambda h, i: (i, h))
    col = pl.BlockSpec((seq_len, HD), lambda h, i: (0, h))
    pos = pl.BlockSpec((block, HD), lambda h, i: (i, 0))
    all_pos = pl.BlockSpec((seq_len, HD), lambda h, i: (0, 0))
    wide = jax.ShapeDtypeStruct((seq_len, heads * HD), BF)
    pairs = heads * seq_len * (seq_len + block) // 2
    return pl.pallas_call(
        kernel,
        grid=(heads, blocks),
        in_specs=[row, col, col, row, row, pl.BlockSpec((1, 1, block), lambda h, i: (h, 0, i)),
                  pos, pos, all_pos, all_pos],
        out_specs=[row, col, col],
        out_shape=[wide, wide, wide],
        scratch_shapes=[
            pltpu.VMEM((blocks, HD, block), BF),
            pltpu.VMEM((seq_len, HD), F32),
            pltpu.VMEM((seq_len, HD), F32),
        ],
        compiler_params=pltpu.CompilerParams(vmem_limit_bytes=48 << 20),
        cost_estimate=pl.CostEstimate(
            flops=38 * pairs * HD,
            transcendentals=pairs,
            bytes_accessed=seq_len * heads * HD * 16,
        ),
    )(queries, keys, values, outs, grads, norms, cosine, sine, cosine, sine)


def row_total(values):
    return lax.psum(values, "tp")


def swap(values, axis, bit):
    step = 1 << bit
    return lax.ppermute(values, axis, [(i, i ^ step) for i in range(lax.axis_size(axis))])


def high_bits():
    return list(range(1, lax.axis_size("tp").bit_length() - 1))[::-1]


def gather_rows(values, arrived=None):
    rows, cols = values.shape
    half = rows // 2
    n_t, n_c = lax.axis_size("tp"), lax.axis_size("ctx")
    me_t, me_c = lax.axis_index("tp"), lax.axis_index("ctx")
    across = [("tp", b) for b in high_bits()]
    full = jnp.zeros((n_t, n_c * rows, cols), values.dtype)
    for part, plan in enumerate(([("ctx", 0)] + across, across + [("ctx", 0)])):
        held = {(0, 0): values[part * half : (part + 1) * half]}
        for axis, bit in plan + [("tp", 0)]:
            for (dc, dt), piece in list(held.items()):
                key = (1, dt) if axis == "ctx" else (dc, dt | (1 << bit))
                held[key] = swap(piece, axis, bit)
            if arrived is not None and len(held) == 2:
                arrived.append(held[key])
        for (dc, dt), piece in held.items():
            start = (me_t ^ dt, (me_c ^ dc) * rows + part * half, 0)
            full = lax.dynamic_update_slice(full, piece[None], start)
    return with_layout_constraint(full, Layout((0, 1, 2)))


def core_sums(block_of):
    n_t = lax.axis_size("tp")
    me_t = lax.axis_index("tp")
    sums = {}
    for dt in range(0, n_t, 2):
        got = swap(block_of(me_t ^ (dt + 1)).astype(BF), "tp", 0)
        sums[dt] = (block_of(me_t ^ dt) + got.astype(F32)).astype(BF)
    return sums


def scatter_sums(sums):
    n_c = lax.axis_size("ctx")
    me_c = lax.axis_index("ctx")
    rows = sums[0].shape[0] // n_c
    cols = sums[0].shape[1]
    half = rows // 2
    across = [("tp", b) for b in high_bits()]
    done = []
    for part, plan in enumerate(([("ctx", 0)] + across, across + [("ctx", 0)])):
        held = {}
        for dt, total in sums.items():
            split = total.reshape(n_c, rows, cols)[:, part * half : (part + 1) * half]
            for dc in range(n_c):
                held[(dc, dt)] = lax.dynamic_index_in_dim(split, me_c ^ dc, 0, keepdims=False)
        for axis, bit in plan:
            left = {}
            for (dc, dt), piece in held.items():
                give = dc == 1 if axis == "ctx" else (dt >> bit) & 1
                if not give:
                    away = (1, dt) if axis == "ctx" else (dc, dt | (1 << bit))
                    got = swap(held[away].astype(BF), axis, bit)
                    left[(dc, dt)] = piece.astype(F32) + got.astype(F32)
            held = left
        done.append(held[(0, 0)])
    return jnp.concatenate(done, axis=0)


def scatter_rows(block_of):
    return scatter_sums(core_sums(block_of))


def ctx_half(weight, axis):
    size = weight.shape[axis] // lax.axis_size("ctx")
    return lax.dynamic_slice_in_dim(weight, lax.axis_index("ctx") * size, size, axis)


def after(value, token):
    value, _ = lax.optimization_barrier((value, token))
    return value


def owners(grad):
    return lax.psum_scatter(grad, "fsdp", scatter_dimension=0, tiled=False)


def far_groups():
    count = lax.axis_size("fsdp")
    return [list(range(i, count, 2)) for i in range(2)]


def far_owners(grad):
    grad = grad.reshape((-1, 2) + grad.shape[1:])
    return lax.psum_scatter(
        grad, "fsdp", scatter_dimension=0, tiled=False, axis_index_groups=far_groups()
    )


def far_spread(weight):
    full = lax.all_gather(
        weight, "fsdp", axis=0, tiled=False, axis_index_groups=far_groups()
    )
    return full.reshape((-1,) + full.shape[2:])


def plane():
    return lax.axis_index("fsdp") & 1


def near(values):
    return swap(values, "fsdp", 0)


def in_pair(mine, other):
    return jnp.where(plane() == 0, mine, other), jnp.where(plane() == 0, other, mine)


def pair_share(block, axis):
    count = 2 * lax.axis_size("ctx")
    size = block.shape[axis] // count
    place = lax.axis_index("ctx") * 2

    def columns(index):
        return lax.dynamic_slice_in_dim(block, (place + index) * size, size, axis)

    return jnp.stack(in_pair(columns(plane()), near(columns(1 - plane()))))


def pair_grad(block, axis):
    mine = lax.dynamic_index_in_dim(block, plane(), 0, keepdims=False)
    give = lax.dynamic_index_in_dim(block, 1 - plane(), 0, keepdims=False)
    both = trade_ctx(jnp.stack(in_pair(mine, near(give))), axis + 1)
    return [v[i] for v in both for i in range(2)]


def spread(weight):
    return lax.all_gather(weight, "fsdp", axis=0, tiled=False)


def trade_ctx(block, axis):
    size = block.shape[axis] // lax.axis_size("ctx")
    me = lax.axis_index("ctx")
    own = lax.dynamic_slice_in_dim(block, me * size, size, axis)
    give = lax.dynamic_slice_in_dim(block, (1 - me) * size, size, axis)
    got = swap(give, "ctx", 0)
    return jnp.where(me == 0, own, got), jnp.where(me == 0, got, own)


def out_grad(block):
    return jnp.concatenate(trade_ctx(block, 1), axis=0).astype(F32)


def total_rows(values):
    values = values + swap(values, "ctx", 0)
    for bit in range(lax.axis_size("fsdp").bit_length() - 1):
        values = values + swap(values, "fsdp", bit)
    return values


def body(
    layer_input, attn_gain, qkv_weight, out_weight, ffn_gain, gate_up_weight, down_weight, cotangent
):
    n_f = lax.axis_size("fsdp")
    d_f = D // n_f
    qkv_full = spread(ctx_half(jnp.swapaxes(qkv_weight, 0, 1), 2))
    qkv_parts = [qkv_full[:, i] for i in range(3)]
    out_full = spread(ctx_half(out_weight, 0))

    def into(full, weight):
        return mm(full, weight, (((0, 2), (0, 1)), ((), ())))

    def back_out(full, weight):
        return mm(full, weight, (((0, 2), (0, 2)), ((), ())))

    def out_blocks(inner, weight):
        return lambda t: mm(inner, lax.dynamic_index_in_dim(weight, t, 0, keepdims=False))

    def in_blocks(grads, weight):
        return lambda t: mm(grads, lax.dynamic_index_in_dim(weight, t, 0, keepdims=False), NT)

    def in_sum(full, grads):
        return mm(full, grads, (((1,), (0,)), ((), ())))

    def in_part(full, grads):
        return in_sum(full, grads).astype(BF)

    def out_part(inner, full):
        def block(t):
            return sum(mm(v, f[t], (((0,), (0,)), ((), ()))) for v, f in zip(inner, full))

        return jnp.stack([block(t).astype(BF) for t in range(n_f)])

    shares = (pair_share(gate_up_weight, 2).reshape(2, d_f, -1), pair_share(down_weight, 0))
    gu_full = far_spread(shares[0])
    down_full = far_spread(shares[1])
    input_float = layer_input.astype(F32)
    attn_scale = attn_gain.astype(F32)
    ffn_scale = ffn_gain.astype(F32)
    rms_one = lax.rsqrt(row_total(jnp.sum(input_float * input_float, axis=-1)) / D + rms_epsilon)[
        :, None
    ]
    normed_attn = (input_float * rms_one * attn_scale).astype(BF)
    attn_full = gather_rows(normed_attn)
    seq_len = attn_full.shape[1]
    cosine, sine = rope_tables(seq_len)
    cotans = [gather_rows(after(cotangent, attn_full))]
    full = after(attn_full, (cotans[0], shares))
    proj = [into(full, part) for part in qkv_parts]
    queries, keys, values, head_outs, norms = attend_forward(*proj, cosine, sine)
    sums = core_sums(out_blocks(head_outs, out_full))
    resid = input_float + scatter_sums(sums)
    rms_two = lax.rsqrt(row_total(jnp.sum(resid * resid, axis=-1)) / D + rms_epsilon)[:, None]
    normed_ffn = (resid * rms_two * ffn_scale).astype(BF)
    tokens = [gather_rows(normed_ffn), gather_rows(near(normed_ffn))]
    gate_ups = [into(part, gu_full) for part in tokens]
    cotans.append(gather_rows(after(near(after(cotangent, normed_ffn)), gate_ups[0])))
    inner = []
    for gate_up in gate_ups:
        units = gate_up.shape[1] // 2
        gate = gate_up[:, :units]
        up_value = gate_up[:, units:]
        sigma = jax.nn.sigmoid(gate)
        inner.append((gate, up_value, sigma, (gate * sigma * up_value).astype(BF)))
    hidden = [v[3] for v in inner]
    down_part = out_part(hidden, cotans)
    down_sum = far_owners(down_part)
    down_full = after(down_full, down_part)
    grad_gu = []
    for cotan, (gate, up_value, sigma, _) in zip(cotans, inner):
        grad_hidden = back_out(cotan, down_full)
        grad_gu.append(
            jnp.concatenate(
                [
                    grad_hidden * up_value * sigma * (1.0 + gate * (1.0 - sigma)),
                    grad_hidden * gate * sigma,
                ],
                axis=1,
            ).astype(BF)
        )
    sums_near = core_sums(in_blocks(grad_gu[1], gu_full))
    sums_own = core_sums(in_blocks(after(grad_gu[0], tuple(sums_near.values())), gu_full))
    grad_gu = after(grad_gu, tuple(sums_own.values()))
    gu_part = [
        sum(in_sum(t, g[:, i * units : (i + 1) * units]) for t, g in zip(tokens, grad_gu))
        for i in range(2)
    ]
    gu_part = [part.astype(BF) for part in gu_part]
    gu_sum = [far_owners(after(part, down_sum)) for part in gu_part]
    grad_nffn = scatter_sums(sums_own) + near(scatter_sums(sums_near).astype(BF)).astype(F32)
    grad_nffn = after(grad_nffn, gu_part)
    ffn_term = grad_nffn * ffn_scale
    ffn_dot = row_total(jnp.sum(ffn_term * resid, axis=-1))[:, None]
    grad_resid = cotangent.astype(F32) + rms_two * ffn_term - resid * rms_two**3 * ffn_dot / D
    ffn_gain_part = jnp.sum(grad_nffn * resid * rms_two, axis=0)
    grad_branch = grad_resid.astype(BF)
    arrived = []
    branch_full = gather_rows(grad_branch, arrived)
    hidden = after(hidden, arrived)
    sums_near = core_sums(out_blocks(hidden[1], down_full))
    sums_own = core_sums(out_blocks(hidden[0], down_full))
    down_grad = jnp.concatenate(pair_grad(down_sum, 1), axis=0).astype(F32)
    grad_heads = back_out(branch_full, out_full).astype(BF)
    grad_heads = after(grad_heads, (sums_near, sums_own, down_grad))
    ffn_out = scatter_sums(sums_own) + near(scatter_sums(sums_near).astype(BF)).astype(F32)
    layer_output = (resid + ffn_out).astype(BF)
    gate_grad = pair_grad(gu_sum[0], 0)
    out_sum = owners(out_part([head_outs], [branch_full]))
    grad_proj = attend_backward(
        queries, keys, values, head_outs, norms, grad_heads, cosine, sine
    )
    joined = jnp.concatenate(grad_proj, axis=1)
    qkv_part = in_part(attn_full, joined)
    qkv_sum = owners(qkv_part)
    joined = after(joined, (layer_output, gate_grad, qkv_part))
    grad_nattn = scatter_rows(in_blocks(joined, jnp.concatenate(qkv_parts, axis=2)))
    attn_term = grad_nattn * attn_scale
    attn_dot = row_total(jnp.sum(attn_term * input_float, axis=-1))[:, None]
    grad_input = grad_resid + rms_one * attn_term - input_float * rms_one**3 * attn_dot / D
    attn_gain_part = jnp.sum(grad_nattn * input_float * rms_one, axis=0)
    gain_grads = total_rows(jnp.stack([attn_gain_part, ffn_gain_part]))

    gu_grad = jnp.stack(
        [jnp.concatenate(v, axis=1) for v in (gate_grad, pair_grad(gu_sum[1], 0))], axis=1
    ).astype(F32)
    out_weight_grad = out_grad(out_sum)
    done = (down_grad, out_weight_grad, gu_grad, grad_input, layer_output, gain_grads)
    halves = trade_ctx(after(qkv_sum, done), 0)
    wide = queries.shape[1]
    qkv_grad = jnp.stack(
        [
            jnp.concatenate([v[:, i * wide : (i + 1) * wide] for v in halves], axis=1)
            for i in range(3)
        ],
        axis=1,
    ).astype(F32)

    return (
        layer_output,
        grad_input,
        gain_grads[0],
        qkv_grad,
        out_weight_grad,
        gain_grads[1],
        gu_grad,
        down_grad,
    )


def solution(mesh):
    return jax.shard_map(
        body,
        mesh=mesh,
        in_specs=(
            P(("fsdp", "ctx"), "tp"),
            P("tp"),
            P("fsdp", None, "tp"),
            P("tp", "fsdp"),
            P("tp"),
            P("fsdp", None, "tp"),
            P("tp", "fsdp"),
            P(("fsdp", "ctx"), "tp"),
        ),
        out_specs=(
            P(("fsdp", "ctx"), "tp"),
            P(("fsdp", "ctx"), "tp"),
            P("tp"),
            P(("fsdp", "ctx"), None, "tp"),
            P("tp", ("fsdp", "ctx")),
            P("tp"),
            P(("fsdp", "ctx"), None, "tp"),
            P("tp", ("fsdp", "ctx")),
        ),
        check_vma=False,
    )
```

```python
import math

import jax
import jax.numpy as jnp
from jax import lax
from jax.experimental import pallas as pl
from jax.experimental.layout import Layout, with_layout_constraint
from jax.experimental.pallas import tpu as pltpu
from jax.sharding import PartitionSpec as P

D = 4096
HD = 128
BF = jnp.bfloat16
F32 = jnp.float32
rms_epsilon = 1e-05
NT = (((1,), (1,)), ((), ()))
LOG2E = 1.4426950408889634


def mm(left, right, dims=(((1,), (0,)), ((), ()))):
    return lax.dot_general(left, right, dims, preferred_element_type=F32)


def turn(values, cosine, sine):
    return values * cosine + pltpu.roll(values, HD // 2, 1) * sine


def rope_tables(seq_len):
    half_width = HD // 2
    inv_freq = jnp.exp(-math.log(10000.0) * jnp.arange(half_width, dtype=F32) * 2.0 / HD)
    angles = jnp.arange(seq_len, dtype=F32)[:, None] * inv_freq[None, :]
    cosine, sine = jnp.cos(angles), jnp.sin(angles)
    return jnp.concatenate([cosine, cosine], axis=1), jnp.concatenate([-sine, sine], axis=1)


def attend_forward(query_proj, key_proj, value_proj, cosine, sine):
    seq_len = query_proj.shape[0]
    heads = query_proj.shape[1] // HD
    block = min(512, seq_len)
    blocks = seq_len // block
    scale = LOG2E / math.sqrt(HD)

    def kernel(q_in, k_in, v_in, cos_q, sin_q, cos_k, sin_k, q_out, k_out, v_out, out, norm, vt):
        i = pl.program_id(1)

        @pl.when(i == 0)
        def _():
            for j in range(blocks):
                rows = pl.ds(j * block, block)
                k_out[rows, :] = turn(k_in[rows, :], cos_k[rows, :], sin_k[rows, :]).astype(BF)
                v_out[rows, :] = v_in[rows, :].astype(BF)
                vt[j] = v_in[rows, :].T.astype(BF)

        q_out[...] = turn(q_in[...], cos_q[...], sin_q[...]).astype(BF)
        query = q_out[...]

        def step(j, carry, diagonal):
            top, total, mixed = carry
            rows = pl.ds(pl.multiple_of(j * block, block), block)
            scores = mm(k_out[rows, :], query, NT) * scale
            if diagonal:
                key_at = lax.broadcasted_iota(jnp.int32, scores.shape, 0)
                query_at = lax.broadcasted_iota(jnp.int32, scores.shape, 1)
                scores = jnp.where(key_at <= query_at, scores, -1e30)
            new_top = jnp.maximum(top, jnp.max(scores, axis=0, keepdims=True))
            expo = jnp.exp2(scores - new_top)
            fade = jnp.exp2(top - new_top)
            total = total * fade + jnp.sum(expo, axis=0, keepdims=True)
            mixed = mixed * fade + mm(vt[j], expo.astype(BF))
            return new_top, total, mixed

        carry = (
            jnp.full((1, block), -1e30, F32),
            jnp.zeros((1, block), F32),
            jnp.zeros((HD, block), F32),
        )
        carry = lax.fori_loop(0, i, lambda j, c: step(j, c, False), carry)
        top, total, mixed = step(i, carry, True)
        out[...] = (mixed / total).T.astype(BF)
        norm[0] = top + jnp.log2(total)

    row = pl.BlockSpec((block, HD), lambda h, i: (i, h))
    col = pl.BlockSpec((seq_len, HD), lambda h, i: (0, h))
    pos = pl.BlockSpec((block, HD), lambda h, i: (i, 0))
    all_pos = pl.BlockSpec((seq_len, HD), lambda h, i: (0, 0))
    wide = jax.ShapeDtypeStruct((seq_len, heads * HD), BF)
    pairs = heads * seq_len * (seq_len + block) // 2
    return pl.pallas_call(
        kernel,
        grid=(heads, blocks),
        in_specs=[row, col, col, pos, pos, all_pos, all_pos],
        out_specs=[row, col, col, row, pl.BlockSpec((1, 1, block), lambda h, i: (h, 0, i))],
        out_shape=[wide, wide, wide, wide, jax.ShapeDtypeStruct((heads, 1, seq_len), F32)],
        scratch_shapes=[pltpu.VMEM((blocks, HD, block), BF)],
        compiler_params=pltpu.CompilerParams(vmem_limit_bytes=48 << 20),
        cost_estimate=pl.CostEstimate(
            flops=4 * pairs * HD,
            transcendentals=pairs,
            bytes_accessed=seq_len * heads * HD * (12 + 8),
        ),
    )(query_proj, key_proj, value_proj, cosine, sine, cosine, sine)


def attend_backward(queries, keys, values, outs, norms, grads, cosine, sine):
    seq_len = queries.shape[0]
    heads = queries.shape[1] // HD
    block = min(512, seq_len)
    blocks = seq_len // block
    root = 1.0 / math.sqrt(HD)
    scale = LOG2E * root

    def kernel(q, k, v, o, g, norm, cos_q, sin_q, cos_k, sin_k, dq, dk, dv, kt, dk_sum, dv_sum):
        i = pl.program_id(1)

        @pl.when(i == 0)
        def _():
            for j in range(blocks):
                rows = pl.ds(j * block, block)
                kt[j] = k[rows, :].astype(F32).T.astype(BF)
            dk_sum[...] = jnp.zeros_like(dk_sum)
            dv_sum[...] = jnp.zeros_like(dv_sum)

        query = q[...]
        grad = g[...]
        dots = (grad.astype(F32) * o[...].astype(F32)).T
        weighted = jnp.sum(dots, axis=0, keepdims=True)
        level = norm[0]

        def step(j, total, diagonal):
            rows = pl.ds(pl.multiple_of(j * block, block), block)
            scores = mm(k[rows, :], query, NT) * scale
            probs = jnp.exp2(scores - level)
            if diagonal:
                key_at = lax.broadcasted_iota(jnp.int32, scores.shape, 0)
                query_at = lax.broadcasted_iota(jnp.int32, scores.shape, 1)
                probs = jnp.where(key_at <= query_at, probs, 0.0)
            dv_sum[rows, :] += mm(probs.astype(BF), grad)
            d_probs = mm(v[rows, :], grad, NT)
            d_scores = (probs * (d_probs - weighted)).astype(BF)
            dk_sum[rows, :] += mm(d_scores, query)
            return total + mm(kt[j], d_scores)

        total = lax.fori_loop(
            0, i, lambda j, c: step(j, c, False), jnp.zeros((HD, block), F32)
        )
        total = step(i, total, True)
        dq[...] = turn(total.T * root, cos_q[...], -sin_q[...]).astype(BF)

        @pl.when(i == blocks - 1)
        def _():
            for j in range(blocks):
                rows = pl.ds(j * block, block)
                dk[rows, :] = turn(
                    dk_sum[rows, :] * root, cos_k[rows, :], -sin_k[rows, :]
                ).astype(BF)
                dv[rows, :] = dv_sum[rows, :].astype(BF)

    row = pl.BlockSpec((block, HD), lambda h, i: (i, h))
    col = pl.BlockSpec((seq_len, HD), lambda h, i: (0, h))
    pos = pl.BlockSpec((block, HD), lambda h, i: (i, 0))
    all_pos = pl.BlockSpec((seq_len, HD), lambda h, i: (0, 0))
    wide = jax.ShapeDtypeStruct((seq_len, heads * HD), BF)
    pairs = heads * seq_len * (seq_len + block) // 2
    return pl.pallas_call(
        kernel,
        grid=(heads, blocks),
        in_specs=[row, col, col, row, row, pl.BlockSpec((1, 1, block), lambda h, i: (h, 0, i)),
                  pos, pos, all_pos, all_pos],
        out_specs=[row, col, col],
        out_shape=[wide, wide, wide],
        scratch_shapes=[
            pltpu.VMEM((blocks, HD, block), BF),
            pltpu.VMEM((seq_len, HD), F32),
            pltpu.VMEM((seq_len, HD), F32),
        ],
        compiler_params=pltpu.CompilerParams(vmem_limit_bytes=48 << 20),
        cost_estimate=pl.CostEstimate(
            flops=10 * pairs * HD,
            transcendentals=pairs,
            bytes_accessed=seq_len * heads * HD * 16,
        ),
    )(queries, keys, values, outs, grads, norms, cosine, sine, cosine, sine)


def row_total(values):
    return lax.psum(values, "tp")


def swap(values, axis, bit):
    step = 1 << bit
    return lax.ppermute(values, axis, [(i, i ^ step) for i in range(lax.axis_size(axis))])


def high_bits():
    return list(range(1, lax.axis_size("tp").bit_length() - 1))[::-1]


def gather_rows(values):
    rows, cols = values.shape
    half = rows // 2
    n_t, n_c = lax.axis_size("tp"), lax.axis_size("ctx")
    me_t, me_c = lax.axis_index("tp"), lax.axis_index("ctx")
    across = [("tp", b) for b in high_bits()]
    full = jnp.zeros((n_t, n_c * rows, cols), values.dtype)
    for part, plan in enumerate(([("ctx", 0)] + across, across + [("ctx", 0)])):
        held = {(0, 0): values[part * half : (part + 1) * half]}
        for axis, bit in plan + [("tp", 0)]:
            for (dc, dt), piece in list(held.items()):
                key = (1, dt) if axis == "ctx" else (dc, dt | (1 << bit))
                held[key] = swap(piece, axis, bit)
        for (dc, dt), piece in held.items():
            start = (me_t ^ dt, (me_c ^ dc) * rows + part * half, 0)
            full = lax.dynamic_update_slice(full, piece[None], start)
    return with_layout_constraint(full, Layout((0, 1, 2)))


def scatter_rows(block_of):
    n_t, n_c = lax.axis_size("tp"), lax.axis_size("ctx")
    me_t, me_c = lax.axis_index("tp"), lax.axis_index("ctx")
    sums = {}
    for dt in range(0, n_t, 2):
        got = swap(block_of(me_t ^ (dt + 1)).astype(BF), "tp", 0)
        sums[dt] = (block_of(me_t ^ dt) + got.astype(F32)).astype(BF)
    rows = sums[0].shape[0] // n_c
    cols = sums[0].shape[1]
    half = rows // 2
    across = [("tp", b) for b in high_bits()]
    done = []
    for part, plan in enumerate(([("ctx", 0)] + across, across + [("ctx", 0)])):
        held = {}
        for dt, total in sums.items():
            split = total.reshape(n_c, rows, cols)[:, part * half : (part + 1) * half]
            for dc in range(n_c):
                held[(dc, dt)] = lax.dynamic_index_in_dim(split, me_c ^ dc, 0, keepdims=False)
        for axis, bit in plan:
            left = {}
            for (dc, dt), piece in held.items():
                give = dc == 1 if axis == "ctx" else (dt >> bit) & 1
                if not give:
                    away = (1, dt) if axis == "ctx" else (dc, dt | (1 << bit))
                    got = swap(held[away].astype(BF), axis, bit)
                    left[(dc, dt)] = piece.astype(F32) + got.astype(F32)
            held = left
        done.append(held[(0, 0)])
    return jnp.concatenate(done, axis=0)


def ctx_half(weight, axis):
    size = weight.shape[axis] // lax.axis_size("ctx")
    return lax.dynamic_slice_in_dim(weight, lax.axis_index("ctx") * size, size, axis)


def after(value, token):
    value, _ = lax.optimization_barrier((value, token))
    return value


def owners(grad):
    return lax.psum_scatter(grad, "fsdp", scatter_dimension=0, tiled=False)


def spread(weight):
    return lax.all_gather(weight, "fsdp", axis=0, tiled=False)


def trade_ctx(block, axis):
    size = block.shape[axis] // lax.axis_size("ctx")
    me = lax.axis_index("ctx")
    own = lax.dynamic_slice_in_dim(block, me * size, size, axis)
    give = lax.dynamic_slice_in_dim(block, (1 - me) * size, size, axis)
    got = swap(give, "ctx", 0)
    return jnp.where(me == 0, own, got), jnp.where(me == 0, got, own)


def out_grad(block):
    return jnp.concatenate(trade_ctx(block, 1), axis=0).astype(F32)


def total_rows(values):
    values = values + swap(values, "ctx", 0)
    for bit in range(lax.axis_size("fsdp").bit_length() - 1):
        values = values + swap(values, "fsdp", bit)
    return values


def body(
    layer_input, attn_gain, qkv_weight, out_weight, ffn_gain, gate_up_weight, down_weight, cotangent
):
    n_f = lax.axis_size("fsdp")
    d_f = D // n_f
    qkv_full = spread(ctx_half(jnp.swapaxes(qkv_weight, 0, 1), 2))
    qkv_parts = [qkv_full[:, i] for i in range(3)]
    out_full = spread(ctx_half(out_weight, 0))
    gu_full = spread(ctx_half(gate_up_weight, 2).reshape(d_f, -1))
    down_full = spread(ctx_half(down_weight, 0))

    def into(full, weight):
        return mm(full, weight, (((0, 2), (0, 1)), ((), ())))

    def back_out(full, weight):
        return mm(full, weight, (((0, 2), (0, 2)), ((), ())))

    def out_blocks(inner, weight):
        return lambda t: mm(inner, lax.dynamic_index_in_dim(weight, t, 0, keepdims=False))

    def in_blocks(grads, weight):
        return lambda t: mm(grads, lax.dynamic_index_in_dim(weight, t, 0, keepdims=False), NT)

    def in_part(full, grads):
        return mm(full, grads, (((1,), (0,)), ((), ()))).astype(BF)

    def out_part(inner, full):
        return jnp.stack(
            [mm(inner, full[t], (((0,), (0,)), ((), ()))).astype(BF) for t in range(n_f)]
        )

    input_float = layer_input.astype(F32)
    attn_scale = attn_gain.astype(F32)
    ffn_scale = ffn_gain.astype(F32)
    rms_one = lax.rsqrt(row_total(jnp.sum(input_float * input_float, axis=-1)) / D + rms_epsilon)[
        :, None
    ]
    normed_attn = (input_float * rms_one * attn_scale).astype(BF)
    attn_full = gather_rows(normed_attn)
    seq_len = attn_full.shape[1]
    cosine, sine = rope_tables(seq_len)
    cotan_full = gather_rows(after(cotangent, attn_full))
    proj = [into(attn_full, part) for part in qkv_parts]
    queries, keys, values, head_outs, norms = attend_forward(*proj, cosine, sine)
    resid = input_float + scatter_rows(out_blocks(head_outs, out_full))
    rms_two = lax.rsqrt(row_total(jnp.sum(resid * resid, axis=-1)) / D + rms_epsilon)[:, None]
    normed_ffn = (resid * rms_two * ffn_scale).astype(BF)
    ffn_full = gather_rows(normed_ffn)
    gate_up = into(ffn_full, gu_full)
    units = gate_up.shape[1] // 2
    gate = gate_up[:, :units]
    up_value = gate_up[:, units:]
    sigma = jax.nn.sigmoid(gate)
    hidden = (gate * sigma * up_value).astype(BF)
    down_part = out_part(hidden, cotan_full)
    down_sum = owners(down_part)
    down_full = after(down_full, down_part)
    grad_hidden = back_out(cotan_full, down_full)
    grad_gu = jnp.concatenate(
        [grad_hidden * up_value * sigma * (1.0 + gate * (1.0 - sigma)), grad_hidden * gate * sigma],
        axis=1,
    ).astype(BF)
    gu_part = in_part(ffn_full, grad_gu)
    gu_sum = owners(after(gu_part, down_sum))
    grad_nffn = after(scatter_rows(in_blocks(grad_gu, gu_full)), (gu_part, down_sum))
    ffn_term = grad_nffn * ffn_scale
    ffn_dot = row_total(jnp.sum(ffn_term * resid, axis=-1))[:, None]
    grad_resid = cotangent.astype(F32) + rms_two * ffn_term - resid * rms_two**3 * ffn_dot / D
    ffn_gain_part = jnp.sum(grad_nffn * resid * rms_two, axis=0)
    grad_branch = grad_resid.astype(BF)
    branch_full = gather_rows(grad_branch)
    grad_heads = back_out(branch_full, out_full).astype(BF)
    grad_proj = attend_backward(
        queries, keys, values, head_outs, norms, grad_heads, cosine, sine
    )
    joined = jnp.concatenate(grad_proj, axis=1)
    qkv_part = in_part(attn_full, joined)
    qkv_sum = [owners(qkv_part)]
    grad_nattn = scatter_rows(in_blocks(joined, jnp.concatenate(qkv_parts, axis=2)))
    out_sum = owners(out_part(after(head_outs, qkv_part), branch_full))
    hidden = after(hidden, qkv_part)
    layer_output = (resid + scatter_rows(out_blocks(hidden, down_full))).astype(BF)
    attn_term = grad_nattn * attn_scale
    attn_dot = row_total(jnp.sum(attn_term * input_float, axis=-1))[:, None]
    grad_input = grad_resid + rms_one * attn_term - input_float * rms_one**3 * attn_dot / D
    attn_gain_part = jnp.sum(grad_nattn * input_float * rms_one, axis=0)
    gain_grads = total_rows(jnp.stack([attn_gain_part, ffn_gain_part]))

    down_grad = out_grad(down_sum)
    rows, other_rows = trade_ctx(gu_sum, 0)
    gu_grad = jnp.concatenate(
        [v.reshape(v.shape[0], 2, -1) for v in (rows, other_rows)], axis=2
    ).astype(F32)
    done = (down_grad, gu_grad, grad_input, layer_output, gain_grads)
    qkv_grad = []
    for part in qkv_sum:
        first, second = trade_ctx(after(part, done), 0)
        wide = queries.shape[1]
        for i in range(0, first.shape[1], wide):
            both = [first[:, i : i + wide], second[:, i : i + wide]]
            qkv_grad.append(jnp.concatenate(both, axis=1).astype(F32))
        done = done + (qkv_grad[-1],)
    qkv_grad = jnp.stack(qkv_grad, axis=1)
    out_weight_grad = out_grad(after(out_sum, done))

    return (
        layer_output,
        grad_input,
        gain_grads[0],
        qkv_grad,
        out_weight_grad,
        gain_grads[1],
        gu_grad,
        down_grad,
    )


def solution(mesh):
    return jax.shard_map(
        body,
        mesh=mesh,
        in_specs=(
            P(("fsdp", "ctx"), "tp"),
            P("tp"),
            P("fsdp", None, "tp"),
            P("tp", "fsdp"),
            P("tp"),
            P("fsdp", None, "tp"),
            P("tp", "fsdp"),
            P(("fsdp", "ctx"), "tp"),
        ),
        out_specs=(
            P(("fsdp", "ctx"), "tp"),
            P(("fsdp", "ctx"), "tp"),
            P("tp"),
            P(("fsdp", "ctx"), None, "tp"),
            P("tp", ("fsdp", "ctx")),
            P("tp"),
            P(("fsdp", "ctx"), None, "tp"),
            P("tp", ("fsdp", "ctx")),
        ),
        check_vma=False,
    )
```

```python
import math

import jax
import jax.numpy as jnp
from jax import lax
from jax.experimental import pallas as pl
from jax.experimental.layout import Layout, with_layout_constraint
from jax.experimental.pallas import tpu as pltpu
from jax.sharding import PartitionSpec as P

D = 4096
HD = 128
BF = jnp.bfloat16
F32 = jnp.float32
rms_epsilon = 1e-05
NT = (((1,), (1,)), ((), ()))
LOG2E = 1.4426950408889634


def mm(left, right, dims=(((1,), (0,)), ((), ()))):
    return lax.dot_general(left, right, dims, preferred_element_type=F32)


def turn(values, cosine, sine):
    return values * cosine + pltpu.roll(values, HD // 2, 1) * sine


def rope_tables(seq_len):
    half_width = HD // 2
    inv_freq = jnp.exp(-math.log(10000.0) * jnp.arange(half_width, dtype=F32) * 2.0 / HD)
    angles = jnp.arange(seq_len, dtype=F32)[:, None] * inv_freq[None, :]
    cosine, sine = jnp.cos(angles), jnp.sin(angles)
    return jnp.concatenate([cosine, cosine], axis=1), jnp.concatenate([-sine, sine], axis=1)


def attend_forward(query_proj, key_proj, value_proj, cosine, sine):
    seq_len = query_proj.shape[0]
    heads = query_proj.shape[1] // HD
    block = min(512, seq_len)
    blocks = seq_len // block
    scale = LOG2E / math.sqrt(HD)

    def kernel(q_in, k_in, v_in, cos_q, sin_q, cos_k, sin_k, q_out, k_out, v_out, out, norm, vt):
        i = pl.program_id(1)

        @pl.when(i == 0)
        def _():
            for j in range(blocks):
                rows = pl.ds(j * block, block)
                k_out[rows, :] = turn(k_in[rows, :], cos_k[rows, :], sin_k[rows, :]).astype(BF)
                v_out[rows, :] = v_in[rows, :].astype(BF)
                vt[j] = v_in[rows, :].T.astype(BF)

        q_out[...] = turn(q_in[...], cos_q[...], sin_q[...]).astype(BF)
        query = q_out[...]

        def step(j, carry, diagonal):
            top, total, mixed = carry
            rows = pl.ds(pl.multiple_of(j * block, block), block)
            scores = mm(k_out[rows, :], query, NT) * scale
            if diagonal:
                key_at = lax.broadcasted_iota(jnp.int32, scores.shape, 0)
                query_at = lax.broadcasted_iota(jnp.int32, scores.shape, 1)
                scores = jnp.where(key_at <= query_at, scores, -1e30)
            new_top = jnp.maximum(top, jnp.max(scores, axis=0, keepdims=True))
            expo = jnp.exp2(scores - new_top)
            fade = jnp.exp2(top - new_top)
            total = total * fade + jnp.sum(expo, axis=0, keepdims=True)
            mixed = mixed * fade + mm(vt[j], expo.astype(BF))
            return new_top, total, mixed

        carry = (
            jnp.full((1, block), -1e30, F32),
            jnp.zeros((1, block), F32),
            jnp.zeros((HD, block), F32),
        )
        carry = lax.fori_loop(0, i, lambda j, c: step(j, c, False), carry)
        top, total, mixed = step(i, carry, True)
        out[...] = (mixed / total).T.astype(BF)
        norm[0] = top + jnp.log2(total)

    row = pl.BlockSpec((block, HD), lambda h, i: (i, h))
    col = pl.BlockSpec((seq_len, HD), lambda h, i: (0, h))
    pos = pl.BlockSpec((block, HD), lambda h, i: (i, 0))
    all_pos = pl.BlockSpec((seq_len, HD), lambda h, i: (0, 0))
    wide = jax.ShapeDtypeStruct((seq_len, heads * HD), BF)
    pairs = heads * seq_len * (seq_len + block) // 2
    return pl.pallas_call(
        kernel,
        grid=(heads, blocks),
        in_specs=[row, col, col, pos, pos, all_pos, all_pos],
        out_specs=[row, col, col, row, pl.BlockSpec((1, 1, block), lambda h, i: (h, 0, i))],
        out_shape=[wide, wide, wide, wide, jax.ShapeDtypeStruct((heads, 1, seq_len), F32)],
        scratch_shapes=[pltpu.VMEM((blocks, HD, block), BF)],
        compiler_params=pltpu.CompilerParams(vmem_limit_bytes=48 << 20),
        cost_estimate=pl.CostEstimate(
            flops=4 * pairs * HD,
            transcendentals=pairs,
            bytes_accessed=seq_len * heads * HD * (12 + 8),
        ),
    )(query_proj, key_proj, value_proj, cosine, sine, cosine, sine)


def attend_backward(queries, keys, values, outs, norms, grads, cosine, sine):
    seq_len = queries.shape[0]
    heads = queries.shape[1] // HD
    block = min(512, seq_len)
    blocks = seq_len // block
    root = 1.0 / math.sqrt(HD)
    scale = LOG2E * root

    def kernel(q, k, v, o, g, norm, cos_q, sin_q, cos_k, sin_k, dq, dk, dv, kt, dk_sum, dv_sum):
        i = pl.program_id(1)

        @pl.when(i == 0)
        def _():
            for j in range(blocks):
                rows = pl.ds(j * block, block)
                kt[j] = k[rows, :].astype(F32).T.astype(BF)
            dk_sum[...] = jnp.zeros_like(dk_sum)
            dv_sum[...] = jnp.zeros_like(dv_sum)

        query = q[...]
        grad = g[...]
        dots = (grad.astype(F32) * o[...].astype(F32)).T
        weighted = jnp.sum(dots, axis=0, keepdims=True)
        level = norm[0]

        def step(j, total, diagonal):
            rows = pl.ds(pl.multiple_of(j * block, block), block)
            scores = mm(k[rows, :], query, NT) * scale
            probs = jnp.exp2(scores - level)
            if diagonal:
                key_at = lax.broadcasted_iota(jnp.int32, scores.shape, 0)
                query_at = lax.broadcasted_iota(jnp.int32, scores.shape, 1)
                probs = jnp.where(key_at <= query_at, probs, 0.0)
            dv_sum[rows, :] += mm(probs.astype(BF), grad)
            d_probs = mm(v[rows, :], grad, NT)
            d_scores = (probs * (d_probs - weighted)).astype(BF)
            dk_sum[rows, :] += mm(d_scores, query)
            return total + mm(kt[j], d_scores)

        total = lax.fori_loop(
            0, i, lambda j, c: step(j, c, False), jnp.zeros((HD, block), F32)
        )
        total = step(i, total, True)
        dq[...] = turn(total.T * root, cos_q[...], -sin_q[...]).astype(BF)

        @pl.when(i == blocks - 1)
        def _():
            for j in range(blocks):
                rows = pl.ds(j * block, block)
                dk[rows, :] = turn(
                    dk_sum[rows, :] * root, cos_k[rows, :], -sin_k[rows, :]
                ).astype(BF)
                dv[rows, :] = dv_sum[rows, :].astype(BF)

    row = pl.BlockSpec((block, HD), lambda h, i: (i, h))
    col = pl.BlockSpec((seq_len, HD), lambda h, i: (0, h))
    pos = pl.BlockSpec((block, HD), lambda h, i: (i, 0))
    all_pos = pl.BlockSpec((seq_len, HD), lambda h, i: (0, 0))
    wide = jax.ShapeDtypeStruct((seq_len, heads * HD), BF)
    pairs = heads * seq_len * (seq_len + block) // 2
    return pl.pallas_call(
        kernel,
        grid=(heads, blocks),
        in_specs=[row, col, col, row, row, pl.BlockSpec((1, 1, block), lambda h, i: (h, 0, i)),
                  pos, pos, all_pos, all_pos],
        out_specs=[row, col, col],
        out_shape=[wide, wide, wide],
        scratch_shapes=[
            pltpu.VMEM((blocks, HD, block), BF),
            pltpu.VMEM((seq_len, HD), F32),
            pltpu.VMEM((seq_len, HD), F32),
        ],
        compiler_params=pltpu.CompilerParams(vmem_limit_bytes=48 << 20),
        cost_estimate=pl.CostEstimate(
            flops=10 * pairs * HD,
            transcendentals=pairs,
            bytes_accessed=seq_len * heads * HD * 16,
        ),
    )(queries, keys, values, outs, grads, norms, cosine, sine, cosine, sine)


def row_total(values):
    return lax.psum(values, "tp")


def swap(values, axis, bit):
    step = 1 << bit
    return lax.ppermute(values, axis, [(i, i ^ step) for i in range(lax.axis_size(axis))])


def high_bits():
    return list(range(1, lax.axis_size("tp").bit_length() - 1))[::-1]


def gather_rows(values):
    rows, cols = values.shape
    half = rows // 2
    n_t, n_c = lax.axis_size("tp"), lax.axis_size("ctx")
    me_t, me_c = lax.axis_index("tp"), lax.axis_index("ctx")
    across = [("tp", b) for b in high_bits()]
    full = jnp.zeros((n_t, n_c * rows, cols), values.dtype)
    for part, plan in enumerate(([("ctx", 0)] + across, across + [("ctx", 0)])):
        held = {(0, 0): values[part * half : (part + 1) * half]}
        for axis, bit in plan + [("tp", 0)]:
            for (dc, dt), piece in list(held.items()):
                key = (1, dt) if axis == "ctx" else (dc, dt | (1 << bit))
                held[key] = swap(piece, axis, bit)
        for (dc, dt), piece in held.items():
            start = (me_t ^ dt, (me_c ^ dc) * rows + part * half, 0)
            full = lax.dynamic_update_slice(full, piece[None], start)
    return with_layout_constraint(full, Layout((0, 1, 2)))


def scatter_rows(block_of):
    n_t, n_c = lax.axis_size("tp"), lax.axis_size("ctx")
    me_t, me_c = lax.axis_index("tp"), lax.axis_index("ctx")
    sums = {}
    for dt in range(0, n_t, 2):
        got = swap(block_of(me_t ^ (dt + 1)).astype(BF), "tp", 0)
        sums[dt] = (block_of(me_t ^ dt) + got.astype(F32)).astype(BF)
    rows = sums[0].shape[0] // n_c
    cols = sums[0].shape[1]
    half = rows // 2
    across = [("tp", b) for b in high_bits()]
    done = []
    for part, plan in enumerate(([("ctx", 0)] + across, across + [("ctx", 0)])):
        held = {}
        for dt, total in sums.items():
            split = total.reshape(n_c, rows, cols)[:, part * half : (part + 1) * half]
            for dc in range(n_c):
                held[(dc, dt)] = lax.dynamic_index_in_dim(split, me_c ^ dc, 0, keepdims=False)
        for axis, bit in plan:
            left = {}
            for (dc, dt), piece in held.items():
                give = dc == 1 if axis == "ctx" else (dt >> bit) & 1
                if not give:
                    away = (1, dt) if axis == "ctx" else (dc, dt | (1 << bit))
                    got = swap(held[away].astype(BF), axis, bit)
                    left[(dc, dt)] = piece.astype(F32) + got.astype(F32)
            held = left
        done.append(held[(0, 0)])
    return jnp.concatenate(done, axis=0)


def ctx_half(weight, axis):
    size = weight.shape[axis] // lax.axis_size("ctx")
    return lax.dynamic_slice_in_dim(weight, lax.axis_index("ctx") * size, size, axis)


def after(value, token):
    value, _ = lax.optimization_barrier((value, token))
    return value


def owners(grad):
    return lax.psum_scatter(grad, "fsdp", scatter_dimension=0, tiled=False)


def spread(weight):
    return lax.all_gather(weight, "fsdp", axis=0, tiled=False)


def trade_ctx(block, axis):
    size = block.shape[axis] // lax.axis_size("ctx")
    me = lax.axis_index("ctx")
    own = lax.dynamic_slice_in_dim(block, me * size, size, axis)
    give = lax.dynamic_slice_in_dim(block, (1 - me) * size, size, axis)
    got = swap(give, "ctx", 0)
    return jnp.where(me == 0, own, got), jnp.where(me == 0, got, own)


def out_grad(block):
    return jnp.concatenate(trade_ctx(block, 1), axis=0).astype(F32)


def total_rows(values):
    values = values + swap(values, "ctx", 0)
    for bit in range(lax.axis_size("fsdp").bit_length() - 1):
        values = values + swap(values, "fsdp", bit)
    return values


def body(
    layer_input, attn_gain, qkv_weight, out_weight, ffn_gain, gate_up_weight, down_weight, cotangent
):
    n_f = lax.axis_size("fsdp")
    d_f = D // n_f
    attn_weights = spread(
        jnp.concatenate(
            [ctx_half(jnp.swapaxes(qkv_weight, 0, 1), 2), ctx_half(out_weight, 0).T[None]]
        )
    )
    qkv_parts = [attn_weights[:, i] for i in range(3)]
    out_full = attn_weights[:, 3]
    gu_full = spread(ctx_half(gate_up_weight, 2).reshape(d_f, -1))
    down_full = spread(ctx_half(down_weight, 0))

    def into(full, weight):
        return mm(full, weight, (((0, 2), (0, 1)), ((), ())))

    def back_out(full, weight):
        return mm(full, weight, (((0, 2), (0, 2)), ((), ())))

    def out_blocks(inner, weight):
        return lambda t: mm(inner, lax.dynamic_index_in_dim(weight, t, 0, keepdims=False))

    def in_blocks(grads, weight):
        return lambda t: mm(grads, lax.dynamic_index_in_dim(weight, t, 0, keepdims=False), NT)

    def in_part(full, grads):
        return mm(full, grads, (((1,), (0,)), ((), ()))).astype(BF)

    def out_part(inner, full):
        return jnp.stack(
            [mm(inner, full[t], (((0,), (0,)), ((), ()))).astype(BF) for t in range(n_f)]
        )

    input_float = layer_input.astype(F32)
    attn_scale = attn_gain.astype(F32)
    ffn_scale = ffn_gain.astype(F32)
    rms_one = lax.rsqrt(row_total(jnp.sum(input_float * input_float, axis=-1)) / D + rms_epsilon)[
        :, None
    ]
    normed_attn = (input_float * rms_one * attn_scale).astype(BF)
    attn_full = gather_rows(normed_attn)
    seq_len = attn_full.shape[1]
    cosine, sine = rope_tables(seq_len)
    cotan_full = gather_rows(after(cotangent, attn_full))
    proj = after([into(attn_full, part) for part in qkv_parts], cotan_full)
    queries, keys, values, head_outs, norms = attend_forward(*proj, cosine, sine)
    resid = input_float + scatter_rows(in_blocks(head_outs, out_full))
    rms_two = lax.rsqrt(row_total(jnp.sum(resid * resid, axis=-1)) / D + rms_epsilon)[:, None]
    normed_ffn = (resid * rms_two * ffn_scale).astype(BF)
    ffn_full = gather_rows(normed_ffn)
    gate_up = into(ffn_full, gu_full)
    units = gate_up.shape[1] // 2
    gate = gate_up[:, :units]
    up_value = gate_up[:, units:]
    sigma = jax.nn.sigmoid(gate)
    hidden = (gate * sigma * up_value).astype(BF)
    down_part = out_part(hidden, cotan_full)
    down_sum = owners(down_part)
    down_full = after(down_full, down_part)
    grad_hidden = back_out(cotan_full, down_full)
    grad_gu = jnp.concatenate(
        [grad_hidden * up_value * sigma * (1.0 + gate * (1.0 - sigma)), grad_hidden * gate * sigma],
        axis=1,
    ).astype(BF)
    gu_part = in_part(ffn_full, grad_gu)
    gu_sum = owners(after(gu_part, down_sum))
    grad_nffn = after(scatter_rows(in_blocks(grad_gu, gu_full)), (gu_part, down_sum))
    ffn_term = grad_nffn * ffn_scale
    ffn_dot = row_total(jnp.sum(ffn_term * resid, axis=-1))[:, None]
    grad_resid = cotangent.astype(F32) + rms_two * ffn_term - resid * rms_two**3 * ffn_dot / D
    ffn_gain_part = jnp.sum(grad_nffn * resid * rms_two, axis=0)
    grad_branch = grad_resid.astype(BF)
    branch_full = gather_rows(grad_branch)
    grad_heads = into(branch_full, out_full).astype(BF)
    grad_proj = attend_backward(
        queries, keys, values, head_outs, norms, grad_heads, cosine, sine
    )
    joined = jnp.concatenate(grad_proj, axis=1)
    qkv_part = in_part(attn_full, joined)
    qkv_sum = [owners(qkv_part)]
    gu_halves = trade_ctx(gu_sum, 0)
    grad_nattn = scatter_rows(in_blocks(joined, jnp.concatenate(qkv_parts, axis=2)))
    grad_nattn = after(grad_nattn, gu_halves)
    part = out_part(after(head_outs, qkv_part), branch_full)
    out_sum = owners(jnp.concatenate(trade_ctx(part, 2), axis=1))
    hidden = after(hidden, qkv_part)
    layer_output = (resid + scatter_rows(out_blocks(hidden, down_full))).astype(BF)
    attn_term = grad_nattn * attn_scale
    attn_dot = row_total(jnp.sum(attn_term * input_float, axis=-1))[:, None]
    grad_input = grad_resid + rms_one * attn_term - input_float * rms_one**3 * attn_dot / D
    attn_gain_part = jnp.sum(grad_nattn * input_float * rms_one, axis=0)
    gain_grads = total_rows(jnp.stack([attn_gain_part, ffn_gain_part]))

    down_grad = out_grad(down_sum)
    gu_grad = jnp.concatenate(
        [v.reshape(v.shape[0], 2, -1) for v in gu_halves], axis=2
    ).astype(F32)
    done = (down_grad, gu_grad, grad_input, layer_output, gain_grads)
    qkv_grad = []
    for part in qkv_sum:
        first, second = trade_ctx(after(part, done), 0)
        wide = queries.shape[1]
        for i in range(0, first.shape[1], wide):
            both = [first[:, i : i + wide], second[:, i : i + wide]]
            qkv_grad.append(jnp.concatenate(both, axis=1).astype(F32))
        done = done + (qkv_grad[-1],)
    qkv_grad = jnp.stack(qkv_grad, axis=1)
    out_weight_grad = after(out_sum, done).astype(F32)

    return (
        layer_output,
        grad_input,
        gain_grads[0],
        qkv_grad,
        out_weight_grad,
        gain_grads[1],
        gu_grad,
        down_grad,
    )


def solution(mesh):
    return jax.shard_map(
        body,
        mesh=mesh,
        in_specs=(
            P(("fsdp", "ctx"), "tp"),
            P("tp"),
            P("fsdp", None, "tp"),
            P("tp", "fsdp"),
            P("tp"),
            P("fsdp", None, "tp"),
            P("tp", "fsdp"),
            P(("fsdp", "ctx"), "tp"),
        ),
        out_specs=(
            P(("fsdp", "ctx"), "tp"),
            P(("fsdp", "ctx"), "tp"),
            P("tp"),
            P(("fsdp", "ctx"), None, "tp"),
            P("tp", ("fsdp", "ctx")),
            P("tp"),
            P(("fsdp", "ctx"), None, "tp"),
            P("tp", ("fsdp", "ctx")),
        ),
        check_vma=False,
    )
```

```python
import math

import jax
import jax.numpy as jnp
from jax import lax
from jax.experimental import pallas as pl
from jax.experimental.layout import Layout, with_layout_constraint
from jax.experimental.pallas import tpu as pltpu
from jax.sharding import PartitionSpec as P

D = 4096
HD = 128
BF = jnp.bfloat16
F32 = jnp.float32
rms_epsilon = 1e-05
NT = (((1,), (1,)), ((), ()))
LOG2E = 1.4426950408889634


def mm(left, right, dims=(((1,), (0,)), ((), ()))):
    return lax.dot_general(left, right, dims, preferred_element_type=F32)


def turn(values, cosine, sine):
    return values * cosine + pltpu.roll(values, HD // 2, 1) * sine


def rope_tables(seq_len):
    half_width = HD // 2
    inv_freq = jnp.exp(-math.log(10000.0) * jnp.arange(half_width, dtype=F32) * 2.0 / HD)
    angles = jnp.arange(seq_len, dtype=F32)[:, None] * inv_freq[None, :]
    cosine, sine = jnp.cos(angles), jnp.sin(angles)
    return jnp.concatenate([cosine, cosine], axis=1), jnp.concatenate([-sine, sine], axis=1)


def attend_forward(query_proj, key_proj, value_proj, cosine, sine):
    seq_len = query_proj.shape[0]
    heads = query_proj.shape[1] // HD
    block = min(512, seq_len)
    blocks = seq_len // block
    scale = LOG2E / math.sqrt(HD)

    def kernel(q_in, k_in, v_in, cos_q, sin_q, cos_k, sin_k, q_out, k_out, v_out, out, norm, vt):
        i = pl.program_id(1)

        @pl.when(i == 0)
        def _():
            for j in range(blocks):
                rows = pl.ds(j * block, block)
                k_out[rows, :] = turn(k_in[rows, :], cos_k[rows, :], sin_k[rows, :]).astype(BF)
                v_out[rows, :] = v_in[rows, :].astype(BF)
                vt[j] = v_in[rows, :].T.astype(BF)

        q_out[...] = turn(q_in[...], cos_q[...], sin_q[...]).astype(BF)
        query = q_out[...]

        def step(j, carry, diagonal):
            top, total, mixed = carry
            rows = pl.ds(pl.multiple_of(j * block, block), block)
            scores = mm(k_out[rows, :], query, NT) * scale
            if diagonal:
                key_at = lax.broadcasted_iota(jnp.int32, scores.shape, 0)
                query_at = lax.broadcasted_iota(jnp.int32, scores.shape, 1)
                scores = jnp.where(key_at <= query_at, scores, -1e30)
            new_top = jnp.maximum(top, jnp.max(scores, axis=0, keepdims=True))
            expo = jnp.exp2(scores - new_top)
            fade = jnp.exp2(top - new_top)
            total = total * fade + jnp.sum(expo, axis=0, keepdims=True)
            mixed = mixed * fade + mm(vt[j], expo.astype(BF))
            return new_top, total, mixed

        carry = (
            jnp.full((1, block), -1e30, F32),
            jnp.zeros((1, block), F32),
            jnp.zeros((HD, block), F32),
        )
        carry = lax.fori_loop(0, i, lambda j, c: step(j, c, False), carry)
        top, total, mixed = step(i, carry, True)
        out[...] = (mixed / total).T.astype(BF)
        norm[0] = top + jnp.log2(total)

    row = pl.BlockSpec((block, HD), lambda h, i: (i, h))
    col = pl.BlockSpec((seq_len, HD), lambda h, i: (0, h))
    pos = pl.BlockSpec((block, HD), lambda h, i: (i, 0))
    all_pos = pl.BlockSpec((seq_len, HD), lambda h, i: (0, 0))
    wide = jax.ShapeDtypeStruct((seq_len, heads * HD), BF)
    pairs = heads * seq_len * (seq_len + block) // 2
    return pl.pallas_call(
        kernel,
        grid=(heads, blocks),
        in_specs=[row, col, col, pos, pos, all_pos, all_pos],
        out_specs=[row, col, col, row, pl.BlockSpec((1, 1, block), lambda h, i: (h, 0, i))],
        out_shape=[wide, wide, wide, wide, jax.ShapeDtypeStruct((heads, 1, seq_len), F32)],
        scratch_shapes=[pltpu.VMEM((blocks, HD, block), BF)],
        compiler_params=pltpu.CompilerParams(vmem_limit_bytes=48 << 20),
        cost_estimate=pl.CostEstimate(
            flops=4 * pairs * HD,
            transcendentals=pairs,
            bytes_accessed=seq_len * heads * HD * (12 + 8),
        ),
    )(query_proj, key_proj, value_proj, cosine, sine, cosine, sine)


def attend_backward(queries, keys, values, outs, norms, grads, cosine, sine):
    seq_len = queries.shape[0]
    heads = queries.shape[1] // HD
    block = min(512, seq_len)
    blocks = seq_len // block
    root = 1.0 / math.sqrt(HD)
    scale = LOG2E * root

    def kernel(q, k, v, o, g, norm, cos_q, sin_q, cos_k, sin_k, dq, dk, dv, kt, dk_sum, dv_sum):
        i = pl.program_id(1)

        @pl.when(i == 0)
        def _():
            for j in range(blocks):
                rows = pl.ds(j * block, block)
                kt[j] = k[rows, :].astype(F32).T.astype(BF)
            dk_sum[...] = jnp.zeros_like(dk_sum)
            dv_sum[...] = jnp.zeros_like(dv_sum)

        query = q[...]
        grad = g[...]
        dots = (grad.astype(F32) * o[...].astype(F32)).T
        weighted = jnp.sum(dots, axis=0, keepdims=True)
        level = norm[0]

        def step(j, total, diagonal):
            rows = pl.ds(pl.multiple_of(j * block, block), block)
            scores = mm(k[rows, :], query, NT) * scale
            probs = jnp.exp2(scores - level)
            if diagonal:
                key_at = lax.broadcasted_iota(jnp.int32, scores.shape, 0)
                query_at = lax.broadcasted_iota(jnp.int32, scores.shape, 1)
                probs = jnp.where(key_at <= query_at, probs, 0.0)
            dv_sum[rows, :] += mm(probs.astype(BF), grad)
            d_probs = mm(v[rows, :], grad, NT)
            d_scores = (probs * (d_probs - weighted)).astype(BF)
            dk_sum[rows, :] += mm(d_scores, query)
            return total + mm(kt[j], d_scores)

        total = lax.fori_loop(
            0, i, lambda j, c: step(j, c, False), jnp.zeros((HD, block), F32)
        )
        total = step(i, total, True)
        dq[...] = turn(total.T * root, cos_q[...], -sin_q[...]).astype(BF)

        @pl.when(i == blocks - 1)
        def _():
            for j in range(blocks):
                rows = pl.ds(j * block, block)
                dk[rows, :] = turn(
                    dk_sum[rows, :] * root, cos_k[rows, :], -sin_k[rows, :]
                ).astype(BF)
                dv[rows, :] = dv_sum[rows, :].astype(BF)

    row = pl.BlockSpec((block, HD), lambda h, i: (i, h))
    col = pl.BlockSpec((seq_len, HD), lambda h, i: (0, h))
    pos = pl.BlockSpec((block, HD), lambda h, i: (i, 0))
    all_pos = pl.BlockSpec((seq_len, HD), lambda h, i: (0, 0))
    wide = jax.ShapeDtypeStruct((seq_len, heads * HD), BF)
    pairs = heads * seq_len * (seq_len + block) // 2
    return pl.pallas_call(
        kernel,
        grid=(heads, blocks),
        in_specs=[row, col, col, row, row, pl.BlockSpec((1, 1, block), lambda h, i: (h, 0, i)),
                  pos, pos, all_pos, all_pos],
        out_specs=[row, col, col],
        out_shape=[wide, wide, wide],
        scratch_shapes=[
            pltpu.VMEM((blocks, HD, block), BF),
            pltpu.VMEM((seq_len, HD), F32),
            pltpu.VMEM((seq_len, HD), F32),
        ],
        compiler_params=pltpu.CompilerParams(vmem_limit_bytes=48 << 20),
        cost_estimate=pl.CostEstimate(
            flops=10 * pairs * HD,
            transcendentals=pairs,
            bytes_accessed=seq_len * heads * HD * 16,
        ),
    )(queries, keys, values, outs, grads, norms, cosine, sine, cosine, sine)


def row_total(values):
    return lax.psum(values, "tp")


def swap(values, axis, bit):
    step = 1 << bit
    return lax.ppermute(values, axis, [(i, i ^ step) for i in range(lax.axis_size(axis))])


def high_bits():
    return list(range(1, lax.axis_size("tp").bit_length() - 1))[::-1]


def gather_rows(values):
    rows, cols = values.shape
    half = rows // 2
    n_t, n_c = lax.axis_size("tp"), lax.axis_size("ctx")
    me_t, me_c = lax.axis_index("tp"), lax.axis_index("ctx")
    across = [("tp", b) for b in high_bits()]
    full = jnp.zeros((n_t, n_c * rows, cols), values.dtype)
    for part, plan in enumerate(([("ctx", 0)] + across, across + [("ctx", 0)])):
        held = {(0, 0): values[part * half : (part + 1) * half]}
        for axis, bit in plan + [("tp", 0)]:
            for (dc, dt), piece in list(held.items()):
                key = (1, dt) if axis == "ctx" else (dc, dt | (1 << bit))
                held[key] = swap(piece, axis, bit)
        for (dc, dt), piece in held.items():
            start = (me_t ^ dt, (me_c ^ dc) * rows + part * half, 0)
            full = lax.dynamic_update_slice(full, piece[None], start)
    return with_layout_constraint(full, Layout((0, 1, 2)))


def core_sums(block_of):
    me_t = lax.axis_index("tp")
    sums = {}
    for dt in range(0, lax.axis_size("tp"), 2):
        got = swap(block_of(me_t ^ (dt + 1)).astype(BF), "tp", 0)
        sums[dt] = (block_of(me_t ^ dt) + got.astype(F32)).astype(BF)
    return sums


def scatter_sums(sums):
    n_c = lax.axis_size("ctx")
    me_c = lax.axis_index("ctx")
    rows = sums[0].shape[0] // n_c
    cols = sums[0].shape[1]
    half = rows // 2
    across = [("tp", b) for b in high_bits()]
    done = []
    for part, plan in enumerate(([("ctx", 0)] + across, across + [("ctx", 0)])):
        held = {}
        for dt, total in sums.items():
            split = total.reshape(n_c, rows, cols)[:, part * half : (part + 1) * half]
            for dc in range(n_c):
                held[(dc, dt)] = lax.dynamic_index_in_dim(split, me_c ^ dc, 0, keepdims=False)
        for axis, bit in plan:
            left = {}
            for (dc, dt), piece in held.items():
                give = dc == 1 if axis == "ctx" else (dt >> bit) & 1
                if not give:
                    away = (1, dt) if axis == "ctx" else (dc, dt | (1 << bit))
                    got = swap(held[away].astype(BF), axis, bit)
                    left[(dc, dt)] = piece.astype(F32) + got.astype(F32)
            held = left
        done.append(held[(0, 0)])
    return jnp.concatenate(done, axis=0)


def scatter_rows(block_of):
    return scatter_sums(core_sums(block_of))


def ctx_half(weight, axis):
    size = weight.shape[axis] // lax.axis_size("ctx")
    return lax.dynamic_slice_in_dim(weight, lax.axis_index("ctx") * size, size, axis)


def after(value, token):
    value, _ = lax.optimization_barrier((value, token))
    return value


def owners(grad):
    return lax.psum_scatter(grad, "fsdp", scatter_dimension=0, tiled=False)


def spread(weight):
    return lax.all_gather(weight, "fsdp", axis=0, tiled=False)


def trade_ctx(block, axis):
    size = block.shape[axis] // lax.axis_size("ctx")
    me = lax.axis_index("ctx")
    own = lax.dynamic_slice_in_dim(block, me * size, size, axis)
    give = lax.dynamic_slice_in_dim(block, (1 - me) * size, size, axis)
    got = swap(give, "ctx", 0)
    return jnp.where(me == 0, own, got), jnp.where(me == 0, got, own)


def out_grad(block):
    return jnp.concatenate(trade_ctx(block, 1), axis=0).astype(F32)


def total_rows(values):
    values = values + swap(values, "ctx", 0)
    for bit in range(lax.axis_size("fsdp").bit_length() - 1):
        values = values + swap(values, "fsdp", bit)
    return values


def body(
    layer_input, attn_gain, qkv_weight, out_weight, ffn_gain, gate_up_weight, down_weight, cotangent
):
    n_f = lax.axis_size("fsdp")
    d_f = D // n_f
    attn_weights = spread(
        jnp.concatenate(
            [ctx_half(jnp.swapaxes(qkv_weight, 0, 1), 2), ctx_half(out_weight, 0).T[None]]
        )
    )
    qkv_parts = [attn_weights[:, i] for i in range(3)]
    out_full = attn_weights[:, 3]
    gu_full = spread(ctx_half(gate_up_weight, 2).reshape(d_f, -1))
    down_full = spread(ctx_half(down_weight, 0))

    def into(full, weight):
        return mm(full, weight, (((0, 2), (0, 1)), ((), ())))

    def back_out(full, weight):
        return mm(full, weight, (((0, 2), (0, 2)), ((), ())))

    def out_blocks(inner, weight):
        return lambda t: mm(inner, lax.dynamic_index_in_dim(weight, t, 0, keepdims=False))

    def in_blocks(grads, weight):
        return lambda t: mm(grads, lax.dynamic_index_in_dim(weight, t, 0, keepdims=False), NT)

    def in_part(full, grads):
        return mm(full, grads, (((1,), (0,)), ((), ()))).astype(BF)

    def out_part(inner, full):
        return jnp.stack(
            [mm(inner, full[t], (((0,), (0,)), ((), ()))).astype(BF) for t in range(n_f)]
        )

    input_float = layer_input.astype(F32)
    attn_scale = attn_gain.astype(F32)
    ffn_scale = ffn_gain.astype(F32)
    rms_one = lax.rsqrt(row_total(jnp.sum(input_float * input_float, axis=-1)) / D + rms_epsilon)[
        :, None
    ]
    normed_attn = (input_float * rms_one * attn_scale).astype(BF)
    attn_full = gather_rows(normed_attn)
    seq_len = attn_full.shape[1]
    cosine, sine = rope_tables(seq_len)
    cotan_full = gather_rows(after(cotangent, attn_full))
    proj = after([into(attn_full, part) for part in qkv_parts], cotan_full)
    queries, keys, values, head_outs, norms = attend_forward(*proj, cosine, sine)
    resid = input_float + scatter_rows(in_blocks(head_outs, out_full))
    rms_two = lax.rsqrt(row_total(jnp.sum(resid * resid, axis=-1)) / D + rms_epsilon)[:, None]
    normed_ffn = (resid * rms_two * ffn_scale).astype(BF)
    ffn_full = gather_rows(normed_ffn)
    gate_up = into(ffn_full, gu_full)
    units = gate_up.shape[1] // 2
    gate = gate_up[:, :units]
    up_value = gate_up[:, units:]
    sigma = jax.nn.sigmoid(gate)
    hidden = (gate * sigma * up_value).astype(BF)
    down_part = out_part(hidden, cotan_full)
    down_sum = owners(down_part)
    down_full = after(down_full, down_part)
    grad_hidden = back_out(cotan_full, down_full)
    grad_gu = jnp.concatenate(
        [grad_hidden * up_value * sigma * (1.0 + gate * (1.0 - sigma)), grad_hidden * gate * sigma],
        axis=1,
    ).astype(BF)
    gu_part = in_part(ffn_full, grad_gu)
    sums = core_sums(out_blocks(after(hidden, gu_part), down_full))
    gu_sum = owners(after(gu_part, (down_sum, tuple(sums.values()))))
    layer_output = (resid + scatter_sums(sums)).astype(BF)
    grad_gu = after(grad_gu, tuple(sums.values()))
    grad_nffn = scatter_rows(in_blocks(grad_gu, gu_full))
    grad_nffn = after(grad_nffn, (gu_part, down_sum, layer_output))
    ffn_term = grad_nffn * ffn_scale
    ffn_dot = row_total(jnp.sum(ffn_term * resid, axis=-1))[:, None]
    grad_resid = cotangent.astype(F32) + rms_two * ffn_term - resid * rms_two**3 * ffn_dot / D
    ffn_gain_part = jnp.sum(grad_nffn * resid * rms_two, axis=0)
    grad_branch = grad_resid.astype(BF)
    branch_full = gather_rows(grad_branch)
    grad_heads = into(branch_full, out_full).astype(BF)
    grad_proj = attend_backward(
        queries, keys, values, head_outs, norms, grad_heads, cosine, sine
    )
    joined = jnp.concatenate(grad_proj, axis=1)
    qkv_part = in_part(attn_full, joined)
    qkv_sum = [owners(qkv_part)]
    gu_halves = trade_ctx(gu_sum, 0)
    grad_nattn = scatter_rows(in_blocks(joined, jnp.concatenate(qkv_parts, axis=2)))
    grad_nattn = after(grad_nattn, gu_halves)
    part = out_part(after(head_outs, qkv_part), branch_full)
    out_sum = owners(jnp.concatenate(trade_ctx(part, 2), axis=1))
    attn_term = grad_nattn * attn_scale
    attn_dot = row_total(jnp.sum(attn_term * input_float, axis=-1))[:, None]
    grad_input = grad_resid + rms_one * attn_term - input_float * rms_one**3 * attn_dot / D
    attn_gain_part = jnp.sum(grad_nattn * input_float * rms_one, axis=0)
    gain_grads = total_rows(jnp.stack([attn_gain_part, ffn_gain_part]))

    down_grad = out_grad(down_sum)
    gu_grad = jnp.concatenate(
        [v.reshape(v.shape[0], 2, -1) for v in gu_halves], axis=2
    ).astype(F32)
    done = (down_grad, gu_grad, grad_input, layer_output, gain_grads)
    qkv_grad = []
    for part in qkv_sum:
        first, second = trade_ctx(after(part, done), 0)
        wide = queries.shape[1]
        for i in range(0, first.shape[1], wide):
            both = [first[:, i : i + wide], second[:, i : i + wide]]
            qkv_grad.append(jnp.concatenate(both, axis=1).astype(F32))
        done = done + (qkv_grad[-1],)
    qkv_grad = jnp.stack(qkv_grad, axis=1)
    out_weight_grad = after(out_sum, done).astype(F32)

    return (
        layer_output,
        grad_input,
        gain_grads[0],
        qkv_grad,
        out_weight_grad,
        gain_grads[1],
        gu_grad,
        down_grad,
    )


def solution(mesh):
    return jax.shard_map(
        body,
        mesh=mesh,
        in_specs=(
            P(("fsdp", "ctx"), "tp"),
            P("tp"),
            P("fsdp", None, "tp"),
            P("tp", "fsdp"),
            P("tp"),
            P("fsdp", None, "tp"),
            P("tp", "fsdp"),
            P(("fsdp", "ctx"), "tp"),
        ),
        out_specs=(
            P(("fsdp", "ctx"), "tp"),
            P(("fsdp", "ctx"), "tp"),
            P("tp"),
            P(("fsdp", "ctx"), None, "tp"),
            P("tp", ("fsdp", "ctx")),
            P("tp"),
            P(("fsdp", "ctx"), None, "tp"),
            P("tp", ("fsdp", "ctx")),
        ),
        check_vma=False,
    )
```

```python
import math

import jax
import jax.numpy as jnp
from jax import lax
from jax.experimental import pallas as pl
from jax.experimental.layout import Layout, with_layout_constraint
from jax.experimental.pallas import tpu as pltpu
from jax.sharding import PartitionSpec as P

D = 4096
HD = 128
BF = jnp.bfloat16
F32 = jnp.float32
rms_epsilon = 1e-05
NT = (((1,), (1,)), ((), ()))
LOG2E = 1.4426950408889634


def mm(left, right, dims=(((1,), (0,)), ((), ()))):
    return lax.dot_general(left, right, dims, preferred_element_type=F32)


def turn(values, cosine, sine):
    return values * cosine + pltpu.roll(values, HD // 2, 1) * sine


def rope_tables(seq_len):
    half_width = HD // 2
    inv_freq = jnp.exp(-math.log(10000.0) * jnp.arange(half_width, dtype=F32) * 2.0 / HD)
    angles = jnp.arange(seq_len, dtype=F32)[:, None] * inv_freq[None, :]
    cosine, sine = jnp.cos(angles), jnp.sin(angles)
    return jnp.concatenate([cosine, cosine], axis=1), jnp.concatenate([-sine, sine], axis=1)


def attend_forward(query_proj, key_proj, value_proj, cosine, sine):
    seq_len = query_proj.shape[0]
    heads = query_proj.shape[1] // HD
    block = min(512, seq_len)
    blocks = seq_len // block
    scale = LOG2E / math.sqrt(HD)

    def kernel(q_in, k_in, v_in, cos_q, sin_q, cos_k, sin_k, q_out, k_out, v_out, out, norm, vt):
        i = pl.program_id(1)

        @pl.when(i == 0)
        def _():
            for j in range(blocks):
                rows = pl.ds(j * block, block)
                k_out[rows, :] = turn(k_in[rows, :], cos_k[rows, :], sin_k[rows, :]).astype(BF)
                v_out[rows, :] = v_in[rows, :].astype(BF)
                vt[j] = v_in[rows, :].T.astype(BF)

        q_out[...] = turn(q_in[...], cos_q[...], sin_q[...]).astype(BF)
        query = q_out[...]

        def step(j, carry, diagonal):
            top, total, mixed = carry
            rows = pl.ds(pl.multiple_of(j * block, block), block)
            scores = mm(k_out[rows, :], query, NT) * scale
            if diagonal:
                key_at = lax.broadcasted_iota(jnp.int32, scores.shape, 0)
                query_at = lax.broadcasted_iota(jnp.int32, scores.shape, 1)
                scores = jnp.where(key_at <= query_at, scores, -1e30)
            new_top = jnp.maximum(top, jnp.max(scores, axis=0, keepdims=True))
            expo = jnp.exp2(scores - new_top)
            fade = jnp.exp2(top - new_top)
            total = total * fade + jnp.sum(expo, axis=0, keepdims=True)
            mixed = mixed * fade + mm(vt[j], expo.astype(BF))
            return new_top, total, mixed

        carry = (
            jnp.full((1, block), -1e30, F32),
            jnp.zeros((1, block), F32),
            jnp.zeros((HD, block), F32),
        )
        carry = lax.fori_loop(0, i, lambda j, c: step(j, c, False), carry)
        top, total, mixed = step(i, carry, True)
        out[...] = (mixed / total).T.astype(BF)
        norm[0] = top + jnp.log2(total)

    row = pl.BlockSpec((block, HD), lambda h, i: (i, h))
    col = pl.BlockSpec((seq_len, HD), lambda h, i: (0, h))
    pos = pl.BlockSpec((block, HD), lambda h, i: (i, 0))
    all_pos = pl.BlockSpec((seq_len, HD), lambda h, i: (0, 0))
    wide = jax.ShapeDtypeStruct((seq_len, heads * HD), BF)
    pairs = heads * seq_len * (seq_len + block) // 2
    return pl.pallas_call(
        kernel,
        grid=(heads, blocks),
        in_specs=[row, col, col, pos, pos, all_pos, all_pos],
        out_specs=[row, col, col, row, pl.BlockSpec((1, 1, block), lambda h, i: (h, 0, i))],
        out_shape=[wide, wide, wide, wide, jax.ShapeDtypeStruct((heads, 1, seq_len), F32)],
        scratch_shapes=[pltpu.VMEM((blocks, HD, block), BF)],
        compiler_params=pltpu.CompilerParams(vmem_limit_bytes=48 << 20),
        cost_estimate=pl.CostEstimate(
            flops=4 * pairs * HD,
            transcendentals=pairs,
            bytes_accessed=seq_len * heads * HD * (12 + 8),
        ),
    )(query_proj, key_proj, value_proj, cosine, sine, cosine, sine)


def attend_backward(queries, keys, values, outs, norms, grads, cosine, sine):
    seq_len = queries.shape[0]
    heads = queries.shape[1] // HD
    block = min(512, seq_len)
    blocks = seq_len // block
    root = 1.0 / math.sqrt(HD)
    scale = LOG2E * root

    def kernel(q, k, v, o, g, norm, cos_q, sin_q, cos_k, sin_k, dq, dk, dv, kt, dk_sum, dv_sum):
        i = pl.program_id(1)

        @pl.when(i == 0)
        def _():
            for j in range(blocks):
                rows = pl.ds(j * block, block)
                kt[j] = k[rows, :].astype(F32).T.astype(BF)
            dk_sum[...] = jnp.zeros_like(dk_sum)
            dv_sum[...] = jnp.zeros_like(dv_sum)

        query = q[...]
        grad = g[...]
        dots = (grad.astype(F32) * o[...].astype(F32)).T
        weighted = jnp.sum(dots, axis=0, keepdims=True)
        level = norm[0]

        def step(j, total, diagonal):
            rows = pl.ds(pl.multiple_of(j * block, block), block)
            scores = mm(k[rows, :], query, NT) * scale
            probs = jnp.exp2(scores - level)
            if diagonal:
                key_at = lax.broadcasted_iota(jnp.int32, scores.shape, 0)
                query_at = lax.broadcasted_iota(jnp.int32, scores.shape, 1)
                probs = jnp.where(key_at <= query_at, probs, 0.0)
            dv_sum[rows, :] += mm(probs.astype(BF), grad)
            d_probs = mm(v[rows, :], grad, NT)
            d_scores = (probs * (d_probs - weighted)).astype(BF)
            dk_sum[rows, :] += mm(d_scores, query)
            return total + mm(kt[j], d_scores)

        total = lax.fori_loop(
            0, i, lambda j, c: step(j, c, False), jnp.zeros((HD, block), F32)
        )
        total = step(i, total, True)
        dq[...] = turn(total.T * root, cos_q[...], -sin_q[...]).astype(BF)

        @pl.when(i == blocks - 1)
        def _():
            for j in range(blocks):
                rows = pl.ds(j * block, block)
                dk[rows, :] = turn(
                    dk_sum[rows, :] * root, cos_k[rows, :], -sin_k[rows, :]
                ).astype(BF)
                dv[rows, :] = dv_sum[rows, :].astype(BF)

    row = pl.BlockSpec((block, HD), lambda h, i: (i, h))
    col = pl.BlockSpec((seq_len, HD), lambda h, i: (0, h))
    pos = pl.BlockSpec((block, HD), lambda h, i: (i, 0))
    all_pos = pl.BlockSpec((seq_len, HD), lambda h, i: (0, 0))
    wide = jax.ShapeDtypeStruct((seq_len, heads * HD), BF)
    pairs = heads * seq_len * (seq_len + block) // 2
    return pl.pallas_call(
        kernel,
        grid=(heads, blocks),
        in_specs=[row, col, col, row, row, pl.BlockSpec((1, 1, block), lambda h, i: (h, 0, i)),
                  pos, pos, all_pos, all_pos],
        out_specs=[row, col, col],
        out_shape=[wide, wide, wide],
        scratch_shapes=[
            pltpu.VMEM((blocks, HD, block), BF),
            pltpu.VMEM((seq_len, HD), F32),
            pltpu.VMEM((seq_len, HD), F32),
        ],
        compiler_params=pltpu.CompilerParams(vmem_limit_bytes=48 << 20),
        cost_estimate=pl.CostEstimate(
            flops=10 * pairs * HD,
            transcendentals=pairs,
            bytes_accessed=seq_len * heads * HD * 16,
        ),
    )(queries, keys, values, outs, grads, norms, cosine, sine, cosine, sine)


def row_total(values):
    return lax.psum(values, "tp")


def swap(values, axis, bit):
    step = 1 << bit
    return lax.ppermute(values, axis, [(i, i ^ step) for i in range(lax.axis_size(axis))])


def high_bits():
    return list(range(1, lax.axis_size("tp").bit_length() - 1))[::-1]


def gather_rows(values):
    rows, cols = values.shape
    half = rows // 2
    n_t, n_c = lax.axis_size("tp"), lax.axis_size("ctx")
    me_t, me_c = lax.axis_index("tp"), lax.axis_index("ctx")
    across = [("tp", b) for b in high_bits()]
    full = jnp.zeros((n_t, n_c * rows, cols), values.dtype)
    for part, plan in enumerate(([("ctx", 0)] + across, across + [("ctx", 0)])):
        held = {(0, 0): values[part * half : (part + 1) * half]}
        for axis, bit in plan + [("tp", 0)]:
            for (dc, dt), piece in list(held.items()):
                key = (1, dt) if axis == "ctx" else (dc, dt | (1 << bit))
                held[key] = swap(piece, axis, bit)
        for (dc, dt), piece in held.items():
            start = (me_t ^ dt, (me_c ^ dc) * rows + part * half, 0)
            full = lax.dynamic_update_slice(full, piece[None], start)
    return with_layout_constraint(full, Layout((0, 1, 2)))


def core_sums(block_of):
    me_t = lax.axis_index("tp")
    sums = {}
    for dt in range(0, lax.axis_size("tp"), 2):
        got = swap(block_of(me_t ^ (dt + 1)).astype(BF), "tp", 0)
        sums[dt] = (block_of(me_t ^ dt) + got.astype(F32)).astype(BF)
    return sums


def scatter_sums(sums):
    n_c = lax.axis_size("ctx")
    me_c = lax.axis_index("ctx")
    rows = sums[0].shape[0] // n_c
    cols = sums[0].shape[1]
    half = rows // 2
    across = [("tp", b) for b in high_bits()]
    done = []
    for part, plan in enumerate(([("ctx", 0)] + across, across + [("ctx", 0)])):
        held = {}
        for dt, total in sums.items():
            split = total.reshape(n_c, rows, cols)[:, part * half : (part + 1) * half]
            for dc in range(n_c):
                held[(dc, dt)] = lax.dynamic_index_in_dim(split, me_c ^ dc, 0, keepdims=False)
        for axis, bit in plan:
            left = {}
            for (dc, dt), piece in held.items():
                give = dc == 1 if axis == "ctx" else (dt >> bit) & 1
                if not give:
                    away = (1, dt) if axis == "ctx" else (dc, dt | (1 << bit))
                    got = swap(held[away].astype(BF), axis, bit)
                    left[(dc, dt)] = piece.astype(F32) + got.astype(F32)
            held = left
        done.append(held[(0, 0)])
    return jnp.concatenate(done, axis=0)


def scatter_rows(block_of):
    return scatter_sums(core_sums(block_of))


def ctx_half(weight, axis):
    size = weight.shape[axis] // lax.axis_size("ctx")
    return lax.dynamic_slice_in_dim(weight, lax.axis_index("ctx") * size, size, axis)


def after(value, token):
    value, _ = lax.optimization_barrier((value, token))
    return value


def owners(grad):
    return lax.psum_scatter(grad, "fsdp", scatter_dimension=0, tiled=False)


def spread(weight):
    return lax.all_gather(weight, "fsdp", axis=0, tiled=False)


def trade_ctx(block, axis):
    size = block.shape[axis] // lax.axis_size("ctx")
    me = lax.axis_index("ctx")
    own = lax.dynamic_slice_in_dim(block, me * size, size, axis)
    give = lax.dynamic_slice_in_dim(block, (1 - me) * size, size, axis)
    got = swap(give, "ctx", 0)
    return jnp.where(me == 0, own, got), jnp.where(me == 0, got, own)


def out_grad(block):
    return jnp.concatenate(trade_ctx(block, 1), axis=0).astype(F32)


def total_rows(values):
    values = values + swap(values, "ctx", 0)
    for bit in range(lax.axis_size("fsdp").bit_length() - 1):
        values = values + swap(values, "fsdp", bit)
    return values


def body(
    layer_input, attn_gain, qkv_weight, out_weight, ffn_gain, gate_up_weight, down_weight, cotangent
):
    n_f = lax.axis_size("fsdp")
    d_f = D // n_f
    attn_weights = spread(
        jnp.concatenate(
            [ctx_half(jnp.swapaxes(qkv_weight, 0, 1), 2), ctx_half(out_weight, 0).T[None]]
        )
    )
    qkv_parts = [attn_weights[:, i] for i in range(3)]
    out_full = attn_weights[:, 3]
    gu_full = spread(ctx_half(gate_up_weight, 2).reshape(d_f, -1))
    down_full = spread(ctx_half(down_weight, 0))

    def into(full, weight):
        return mm(full, weight, (((0, 2), (0, 1)), ((), ())))

    def back_out(full, weight):
        return mm(full, weight, (((0, 2), (0, 2)), ((), ())))

    def out_blocks(inner, weight):
        return lambda t: mm(inner, lax.dynamic_index_in_dim(weight, t, 0, keepdims=False))

    def in_blocks(grads, weight):
        return lambda t: mm(grads, lax.dynamic_index_in_dim(weight, t, 0, keepdims=False), NT)

    def in_part(full, grads):
        return mm(full, grads, (((1,), (0,)), ((), ()))).astype(BF)

    def out_part(inner, full):
        return jnp.stack(
            [mm(inner, full[t], (((0,), (0,)), ((), ()))).astype(BF) for t in range(n_f)]
        )

    input_float = layer_input.astype(F32)
    attn_scale = attn_gain.astype(F32)
    ffn_scale = ffn_gain.astype(F32)
    rms_one = lax.rsqrt(row_total(jnp.sum(input_float * input_float, axis=-1)) / D + rms_epsilon)[
        :, None
    ]
    normed_attn = (input_float * rms_one * attn_scale).astype(BF)
    attn_full = gather_rows(normed_attn)
    seq_len = attn_full.shape[1]
    cosine, sine = rope_tables(seq_len)
    cotan_full = gather_rows(after(cotangent, attn_full))
    proj = after([into(attn_full, part) for part in qkv_parts], cotan_full)
    queries, keys, values, head_outs, norms = attend_forward(*proj, cosine, sine)
    resid = input_float + scatter_rows(in_blocks(head_outs, out_full))
    rms_two = lax.rsqrt(row_total(jnp.sum(resid * resid, axis=-1)) / D + rms_epsilon)[:, None]
    normed_ffn = (resid * rms_two * ffn_scale).astype(BF)
    ffn_full = gather_rows(normed_ffn)
    gate_up = into(ffn_full, gu_full)
    units = gate_up.shape[1] // 2
    gate = gate_up[:, :units]
    up_value = gate_up[:, units:]
    sigma = jax.nn.sigmoid(gate)
    hidden = (gate * sigma * up_value).astype(BF)
    down_part = out_part(hidden, cotan_full)
    down_sum = owners(down_part)
    down_full = after(down_full, down_part)
    grad_hidden = back_out(cotan_full, down_full)
    grad_gu = jnp.concatenate(
        [grad_hidden * up_value * sigma * (1.0 + gate * (1.0 - sigma)), grad_hidden * gate * sigma],
        axis=1,
    ).astype(BF)
    gu_part = in_part(ffn_full, grad_gu)
    sums = core_sums(out_blocks(after(hidden, gu_part), down_full))
    gu_sum = owners(after(gu_part, (down_sum, tuple(sums.values()))))
    layer_output = (resid + scatter_sums(sums)).astype(BF)
    grad_gu = after(grad_gu, tuple(sums.values()))
    grad_nffn = scatter_rows(in_blocks(grad_gu, gu_full))
    grad_nffn = after(grad_nffn, (gu_part, down_sum, layer_output))
    ffn_term = grad_nffn * ffn_scale
    ffn_dot = row_total(jnp.sum(ffn_term * resid, axis=-1))[:, None]
    grad_resid = cotangent.astype(F32) + rms_two * ffn_term - resid * rms_two**3 * ffn_dot / D
    ffn_gain_part = jnp.sum(grad_nffn * resid * rms_two, axis=0)
    grad_branch = grad_resid.astype(BF)
    branch_full = gather_rows(grad_branch)
    grad_heads = into(branch_full, out_full).astype(BF)
    grad_proj = attend_backward(
        queries, keys, values, head_outs, norms, grad_heads, cosine, sine
    )
    joined = jnp.concatenate(grad_proj, axis=1)
    qkv_part = in_part(attn_full, joined)
    qkv_sum = [owners(qkv_part)]
    gu_halves = trade_ctx(gu_sum, 0)
    grad_nattn = scatter_rows(in_blocks(joined, jnp.concatenate(qkv_parts, axis=2)))
    grad_nattn = after(grad_nattn, gu_halves)
    part = out_part(after(head_outs, qkv_part), branch_full)
    out_sum = owners(jnp.concatenate(trade_ctx(part, 2), axis=1))
    attn_term = grad_nattn * attn_scale
    attn_dot = row_total(jnp.sum(attn_term * input_float, axis=-1))[:, None]
    grad_input = grad_resid + rms_one * attn_term - input_float * rms_one**3 * attn_dot / D
    attn_gain_part = jnp.sum(grad_nattn * input_float * rms_one, axis=0)
    gain_grads = total_rows(jnp.stack([attn_gain_part, ffn_gain_part]))

    down_grad = out_grad(down_sum)
    gu_grad = jnp.concatenate(
        [v.reshape(v.shape[0], 2, -1) for v in gu_halves], axis=2
    ).astype(F32)
    done = (down_grad, gu_grad)
    qkv_grad = []
    for part in qkv_sum:
        first, second = trade_ctx(after(part, done), 0)
        wide = queries.shape[1]
        for i in range(0, first.shape[1], wide):
            both = [first[:, i : i + wide], second[:, i : i + wide]]
            qkv_grad.append(jnp.concatenate(both, axis=1).astype(F32))
        done = done + (qkv_grad[-1],)
    qkv_grad = jnp.stack(qkv_grad, axis=1)
    done = (down_grad, gu_grad, grad_input, layer_output, gain_grads, qkv_grad)
    out_weight_grad = after(out_sum, done).astype(F32)

    return (
        layer_output,
        grad_input,
        gain_grads[0],
        qkv_grad,
        out_weight_grad,
        gain_grads[1],
        gu_grad,
        down_grad,
    )


def solution(mesh):
    return jax.shard_map(
        body,
        mesh=mesh,
        in_specs=(
            P(("fsdp", "ctx"), "tp"),
            P("tp"),
            P("fsdp", None, "tp"),
            P("tp", "fsdp"),
            P("tp"),
            P("fsdp", None, "tp"),
            P("tp", "fsdp"),
            P(("fsdp", "ctx"), "tp"),
        ),
        out_specs=(
            P(("fsdp", "ctx"), "tp"),
            P(("fsdp", "ctx"), "tp"),
            P("tp"),
            P(("fsdp", "ctx"), None, "tp"),
            P("tp", ("fsdp", "ctx")),
            P("tp"),
            P(("fsdp", "ctx"), None, "tp"),
            P("tp", ("fsdp", "ctx")),
        ),
        check_vma=False,
    )
```

```python
import math

import jax
import jax.numpy as jnp
from jax import lax
from jax.experimental import pallas as pl
from jax.experimental.layout import Layout, with_layout_constraint
from jax.experimental.pallas import tpu as pltpu
from jax.sharding import PartitionSpec as P

D = 4096
HD = 128
BF = jnp.bfloat16
F32 = jnp.float32
rms_epsilon = 1e-05
NT = (((1,), (1,)), ((), ()))
LOG2E = 1.4426950408889634


def mm(left, right, dims=(((1,), (0,)), ((), ()))):
    return lax.dot_general(left, right, dims, preferred_element_type=F32)


def turn(values, cosine, sine):
    return values * cosine + pltpu.roll(values, HD // 2, 1) * sine


def rope_tables(seq_len):
    half_width = HD // 2
    inv_freq = jnp.exp(-math.log(10000.0) * jnp.arange(half_width, dtype=F32) * 2.0 / HD)
    angles = jnp.arange(seq_len, dtype=F32)[:, None] * inv_freq[None, :]
    cosine, sine = jnp.cos(angles), jnp.sin(angles)
    return jnp.concatenate([cosine, cosine], axis=1), jnp.concatenate([-sine, sine], axis=1)


def attend_forward(query_proj, key_proj, value_proj, cosine, sine):
    seq_len = query_proj.shape[0]
    heads = query_proj.shape[1] // HD
    block = min(512, seq_len)
    blocks = seq_len // block
    scale = LOG2E / math.sqrt(HD)

    def kernel(q_in, k_in, v_in, cos_q, sin_q, cos_k, sin_k, q_out, k_out, v_out, out, norm, vt):
        i = pl.program_id(1)

        @pl.when(i == 0)
        def _():
            for j in range(blocks):
                rows = pl.ds(j * block, block)
                k_out[rows, :] = turn(k_in[rows, :], cos_k[rows, :], sin_k[rows, :]).astype(BF)
                v_out[rows, :] = v_in[rows, :].astype(BF)
                vt[j] = v_in[rows, :].T.astype(BF)

        q_out[...] = turn(q_in[...], cos_q[...], sin_q[...]).astype(BF)
        query = q_out[...]

        def step(j, carry, diagonal):
            top, total, mixed = carry
            rows = pl.ds(pl.multiple_of(j * block, block), block)
            scores = mm(k_out[rows, :], query, NT) * scale
            if diagonal:
                key_at = lax.broadcasted_iota(jnp.int32, scores.shape, 0)
                query_at = lax.broadcasted_iota(jnp.int32, scores.shape, 1)
                scores = jnp.where(key_at <= query_at, scores, -1e30)
            new_top = jnp.maximum(top, jnp.max(scores, axis=0, keepdims=True))
            expo = jnp.exp2(scores - new_top)
            fade = jnp.exp2(top - new_top)
            total = total * fade + jnp.sum(expo, axis=0, keepdims=True)
            mixed = mixed * fade + mm(vt[j], expo.astype(BF))
            return new_top, total, mixed

        carry = (
            jnp.full((1, block), -1e30, F32),
            jnp.zeros((1, block), F32),
            jnp.zeros((HD, block), F32),
        )
        carry = lax.fori_loop(0, i, lambda j, c: step(j, c, False), carry)
        top, total, mixed = step(i, carry, True)
        out[...] = (mixed / total).T.astype(BF)
        norm[0] = top + jnp.log2(total)

    row = pl.BlockSpec((block, HD), lambda h, i: (i, h))
    col = pl.BlockSpec((seq_len, HD), lambda h, i: (0, h))
    pos = pl.BlockSpec((block, HD), lambda h, i: (i, 0))
    all_pos = pl.BlockSpec((seq_len, HD), lambda h, i: (0, 0))
    wide = jax.ShapeDtypeStruct((seq_len, heads * HD), BF)
    pairs = heads * seq_len * (seq_len + block) // 2
    return pl.pallas_call(
        kernel,
        grid=(heads, blocks),
        in_specs=[row, col, col, pos, pos, all_pos, all_pos],
        out_specs=[row, col, col, row, pl.BlockSpec((1, 1, block), lambda h, i: (h, 0, i))],
        out_shape=[wide, wide, wide, wide, jax.ShapeDtypeStruct((heads, 1, seq_len), F32)],
        scratch_shapes=[pltpu.VMEM((blocks, HD, block), BF)],
        compiler_params=pltpu.CompilerParams(vmem_limit_bytes=48 << 20),
        cost_estimate=pl.CostEstimate(
            flops=4 * pairs * HD,
            transcendentals=pairs,
            bytes_accessed=seq_len * heads * HD * (12 + 8),
        ),
    )(query_proj, key_proj, value_proj, cosine, sine, cosine, sine)


def attend_backward(queries, keys, values, outs, norms, grads, cosine, sine):
    seq_len = queries.shape[0]
    heads = queries.shape[1] // HD
    block = min(512, seq_len)
    blocks = seq_len // block
    root = 1.0 / math.sqrt(HD)
    scale = LOG2E * root

    def kernel(q, k, v, o, g, norm, cos_q, sin_q, cos_k, sin_k, dq, dk, dv, kt, dk_sum, dv_sum):
        i = pl.program_id(1)

        @pl.when(i == 0)
        def _():
            for j in range(blocks):
                rows = pl.ds(j * block, block)
                kt[j] = k[rows, :].astype(F32).T.astype(BF)
            dk_sum[...] = jnp.zeros_like(dk_sum)
            dv_sum[...] = jnp.zeros_like(dv_sum)

        query = q[...]
        grad = g[...]
        dots = (grad.astype(F32) * o[...].astype(F32)).T
        weighted = jnp.sum(dots, axis=0, keepdims=True)
        level = norm[0]

        def step(j, total, diagonal):
            rows = pl.ds(pl.multiple_of(j * block, block), block)
            scores = mm(k[rows, :], query, NT) * scale
            probs = jnp.exp2(scores - level)
            if diagonal:
                key_at = lax.broadcasted_iota(jnp.int32, scores.shape, 0)
                query_at = lax.broadcasted_iota(jnp.int32, scores.shape, 1)
                probs = jnp.where(key_at <= query_at, probs, 0.0)
            dv_sum[rows, :] += mm(probs.astype(BF), grad)
            d_probs = mm(v[rows, :], grad, NT)
            d_scores = (probs * (d_probs - weighted)).astype(BF)
            dk_sum[rows, :] += mm(d_scores, query)
            return total + mm(kt[j], d_scores)

        total = lax.fori_loop(
            0, i, lambda j, c: step(j, c, False), jnp.zeros((HD, block), F32)
        )
        total = step(i, total, True)
        dq[...] = turn(total.T * root, cos_q[...], -sin_q[...]).astype(BF)

        @pl.when(i == blocks - 1)
        def _():
            for j in range(blocks):
                rows = pl.ds(j * block, block)
                dk[rows, :] = turn(
                    dk_sum[rows, :] * root, cos_k[rows, :], -sin_k[rows, :]
                ).astype(BF)
                dv[rows, :] = dv_sum[rows, :].astype(BF)

    row = pl.BlockSpec((block, HD), lambda h, i: (i, h))
    col = pl.BlockSpec((seq_len, HD), lambda h, i: (0, h))
    pos = pl.BlockSpec((block, HD), lambda h, i: (i, 0))
    all_pos = pl.BlockSpec((seq_len, HD), lambda h, i: (0, 0))
    wide = jax.ShapeDtypeStruct((seq_len, heads * HD), BF)
    pairs = heads * seq_len * (seq_len + block) // 2
    return pl.pallas_call(
        kernel,
        grid=(heads, blocks),
        in_specs=[row, col, col, row, row, pl.BlockSpec((1, 1, block), lambda h, i: (h, 0, i)),
                  pos, pos, all_pos, all_pos],
        out_specs=[row, col, col],
        out_shape=[wide, wide, wide],
        scratch_shapes=[
            pltpu.VMEM((blocks, HD, block), BF),
            pltpu.VMEM((seq_len, HD), F32),
            pltpu.VMEM((seq_len, HD), F32),
        ],
        compiler_params=pltpu.CompilerParams(vmem_limit_bytes=48 << 20),
        cost_estimate=pl.CostEstimate(
            flops=10 * pairs * HD,
            transcendentals=pairs,
            bytes_accessed=seq_len * heads * HD * 16,
        ),
    )(queries, keys, values, outs, grads, norms, cosine, sine, cosine, sine)


def row_total(values):
    return lax.psum(values, "tp")


def swap(values, axis, bit):
    step = 1 << bit
    return lax.ppermute(values, axis, [(i, i ^ step) for i in range(lax.axis_size(axis))])


def high_bits():
    return list(range(1, lax.axis_size("tp").bit_length() - 1))[::-1]


def gather_rows(values):
    rows, cols = values.shape
    half = rows // 2
    n_t, n_c = lax.axis_size("tp"), lax.axis_size("ctx")
    me_t, me_c = lax.axis_index("tp"), lax.axis_index("ctx")
    across = [("tp", b) for b in high_bits()]
    full = jnp.zeros((n_t, n_c * rows, cols), values.dtype)
    for part, plan in enumerate(([("ctx", 0)] + across, across + [("ctx", 0)])):
        held = {(0, 0): values[part * half : (part + 1) * half]}
        for axis, bit in plan + [("tp", 0)]:
            for (dc, dt), piece in list(held.items()):
                key = (1, dt) if axis == "ctx" else (dc, dt | (1 << bit))
                held[key] = swap(piece, axis, bit)
        for (dc, dt), piece in held.items():
            start = (me_t ^ dt, (me_c ^ dc) * rows + part * half, 0)
            full = lax.dynamic_update_slice(full, piece[None], start)
    return with_layout_constraint(full, Layout((0, 1, 2)))


def core_sums(block_of):
    me_t = lax.axis_index("tp")
    sums = {}
    for dt in range(0, lax.axis_size("tp"), 2):
        got = swap(block_of(me_t ^ (dt + 1)).astype(BF), "tp", 0)
        sums[dt] = (block_of(me_t ^ dt) + got.astype(F32)).astype(BF)
    return sums


def scatter_sums(sums):
    n_c = lax.axis_size("ctx")
    me_c = lax.axis_index("ctx")
    rows = sums[0].shape[0] // n_c
    cols = sums[0].shape[1]
    half = rows // 2
    across = [("tp", b) for b in high_bits()]
    done = []
    for part, plan in enumerate(([("ctx", 0)] + across, across + [("ctx", 0)])):
        held = {}
        for dt, total in sums.items():
            split = total.reshape(n_c, rows, cols)[:, part * half : (part + 1) * half]
            for dc in range(n_c):
                held[(dc, dt)] = lax.dynamic_index_in_dim(split, me_c ^ dc, 0, keepdims=False)
        for axis, bit in plan:
            left = {}
            for (dc, dt), piece in held.items():
                give = dc == 1 if axis == "ctx" else (dt >> bit) & 1
                if not give:
                    away = (1, dt) if axis == "ctx" else (dc, dt | (1 << bit))
                    got = swap(held[away].astype(BF), axis, bit)
                    left[(dc, dt)] = piece.astype(F32) + got.astype(F32)
            held = left
        done.append(held[(0, 0)])
    return jnp.concatenate(done, axis=0)


def scatter_rows(block_of):
    return scatter_sums(core_sums(block_of))


def ctx_half(weight, axis):
    size = weight.shape[axis] // lax.axis_size("ctx")
    return lax.dynamic_slice_in_dim(weight, lax.axis_index("ctx") * size, size, axis)


def after(value, token):
    value, _ = lax.optimization_barrier((value, token))
    return value


def owners(grad):
    return lax.psum_scatter(grad, "fsdp", scatter_dimension=0, tiled=False)


def spread(weight):
    return lax.all_gather(weight, "fsdp", axis=0, tiled=False)


def trade_ctx(block, axis):
    size = block.shape[axis] // lax.axis_size("ctx")
    me = lax.axis_index("ctx")
    own = lax.dynamic_slice_in_dim(block, me * size, size, axis)
    give = lax.dynamic_slice_in_dim(block, (1 - me) * size, size, axis)
    got = swap(give, "ctx", 0)
    return jnp.where(me == 0, own, got), jnp.where(me == 0, got, own)


def out_grad(block):
    return jnp.concatenate(trade_ctx(block, 1), axis=0).astype(F32)


def total_rows(values):
    for bit in range(lax.axis_size("fsdp").bit_length() - 1):
        values = values + swap(values, "fsdp", bit)
    return values


def body(
    layer_input, attn_gain, qkv_weight, out_weight, ffn_gain, gate_up_weight, down_weight, cotangent
):
    n_f = lax.axis_size("fsdp")
    d_f = D // n_f
    attn_weights = spread(
        jnp.concatenate(
            [ctx_half(jnp.swapaxes(qkv_weight, 0, 1), 2), ctx_half(out_weight, 0).T[None]]
        )
    )
    qkv_parts = [attn_weights[:, i] for i in range(3)]
    out_full = attn_weights[:, 3]
    gu_full = spread(ctx_half(gate_up_weight, 2).reshape(d_f, -1))
    down_full = spread(ctx_half(down_weight, 0))

    def into(full, weight):
        return mm(full, weight, (((0, 2), (0, 1)), ((), ())))

    def back_out(full, weight):
        return mm(full, weight, (((0, 2), (0, 2)), ((), ())))

    def out_blocks(inner, weight):
        return lambda t: mm(inner, lax.dynamic_index_in_dim(weight, t, 0, keepdims=False))

    def in_blocks(grads, weight):
        return lambda t: mm(grads, lax.dynamic_index_in_dim(weight, t, 0, keepdims=False), NT)

    def in_part(full, grads):
        return mm(full, grads, (((1,), (0,)), ((), ()))).astype(BF)

    def out_part(inner, full):
        return jnp.stack(
            [mm(inner, full[t], (((0,), (0,)), ((), ()))).astype(BF) for t in range(n_f)]
        )

    input_float = layer_input.astype(F32)
    attn_scale = attn_gain.astype(F32)
    ffn_scale = ffn_gain.astype(F32)
    rms_one = lax.rsqrt(row_total(jnp.sum(input_float * input_float, axis=-1)) / D + rms_epsilon)[
        :, None
    ]
    normed_attn = (input_float * rms_one * attn_scale).astype(BF)
    attn_full = gather_rows(normed_attn)
    seq_len = attn_full.shape[1]
    cosine, sine = rope_tables(seq_len)
    cotan_full = gather_rows(after(cotangent, attn_full))
    proj = after([into(attn_full, part) for part in qkv_parts], cotan_full)
    queries, keys, values, head_outs, norms = attend_forward(*proj, cosine, sine)
    resid = input_float + scatter_rows(in_blocks(head_outs, out_full))
    rms_two = lax.rsqrt(row_total(jnp.sum(resid * resid, axis=-1)) / D + rms_epsilon)[:, None]
    normed_ffn = (resid * rms_two * ffn_scale).astype(BF)
    ffn_full = gather_rows(normed_ffn)
    gate_up = into(ffn_full, gu_full)
    units = gate_up.shape[1] // 2
    gate = gate_up[:, :units]
    up_value = gate_up[:, units:]
    sigma = jax.nn.sigmoid(gate)
    hidden = (gate * sigma * up_value).astype(BF)
    down_part = out_part(hidden, cotan_full)
    down_sum = owners(down_part)
    down_full = after(down_full, down_part)
    grad_hidden = back_out(cotan_full, down_full)
    grad_gu = jnp.concatenate(
        [grad_hidden * up_value * sigma * (1.0 + gate * (1.0 - sigma)), grad_hidden * gate * sigma],
        axis=1,
    ).astype(BF)
    gu_part = in_part(ffn_full, grad_gu)
    sums = core_sums(out_blocks(after(hidden, gu_part), down_full))
    gu_sum = owners(after(gu_part, (down_sum, tuple(sums.values()))))
    layer_output = (resid + scatter_sums(sums)).astype(BF)
    grad_gu = after(grad_gu, tuple(sums.values()))
    grad_nffn = scatter_rows(in_blocks(grad_gu, gu_full))
    grad_nffn = after(grad_nffn, (gu_part, down_sum, layer_output))
    ffn_term = grad_nffn * ffn_scale
    ffn_dot = row_total(jnp.sum(ffn_term * resid, axis=-1))[:, None]
    grad_resid = cotangent.astype(F32) + rms_two * ffn_term - resid * rms_two**3 * ffn_dot / D
    ffn_gain_part = jnp.sum(grad_nffn * resid * rms_two, axis=0)
    grad_branch = grad_resid.astype(BF)
    branch_full = gather_rows(grad_branch)
    grad_heads = into(branch_full, out_full).astype(BF)
    grad_proj = attend_backward(
        queries, keys, values, head_outs, norms, grad_heads, cosine, sine
    )
    joined = jnp.concatenate(grad_proj, axis=1)
    qkv_part = in_part(attn_full, joined)
    qkv_sum = [owners(qkv_part)]
    gu_halves = trade_ctx(gu_sum, 0)
    grad_nattn = scatter_rows(in_blocks(joined, jnp.concatenate(qkv_parts, axis=2)))
    grad_nattn = after(grad_nattn, gu_halves)
    part = out_part(after(head_outs, qkv_part), branch_full)
    out_sum = owners(jnp.concatenate(trade_ctx(part, 2), axis=1))
    attn_term = grad_nattn * attn_scale
    attn_dot = row_total(jnp.sum(attn_term * input_float, axis=-1))[:, None]
    grad_input = grad_resid + rms_one * attn_term - input_float * rms_one**3 * attn_dot / D
    attn_gain_part = jnp.sum(grad_nattn * input_float * rms_one, axis=0)
    gain_parts = jnp.stack([attn_gain_part, ffn_gain_part])
    gain_parts = gain_parts + swap(gain_parts, "ctx", 0)
    gain_grads = total_rows(gain_parts)

    down_grad = out_grad(down_sum)
    gu_grad = jnp.concatenate(
        [v.reshape(v.shape[0], 2, -1) for v in gu_halves], axis=2
    ).astype(F32)
    done = (down_grad, gu_grad, gain_parts)
    qkv_grad = []
    for part in qkv_sum:
        first, second = trade_ctx(after(part, done), 0)
        wide = queries.shape[1]
        for i in range(0, first.shape[1], wide):
            both = [first[:, i : i + wide], second[:, i : i + wide]]
            qkv_grad.append(jnp.concatenate(both, axis=1).astype(F32))
        done = done + (qkv_grad[-1],)
    qkv_grad = jnp.stack(qkv_grad, axis=1)
    done = (down_grad, gu_grad, grad_input, layer_output, gain_grads, qkv_grad)
    out_weight_grad = after(out_sum, done).astype(F32)

    return (
        layer_output,
        grad_input,
        gain_grads[0],
        qkv_grad,
        out_weight_grad,
        gain_grads[1],
        gu_grad,
        down_grad,
    )


def solution(mesh):
    return jax.shard_map(
        body,
        mesh=mesh,
        in_specs=(
            P(("fsdp", "ctx"), "tp"),
            P("tp"),
            P("fsdp", None, "tp"),
            P("tp", "fsdp"),
            P("tp"),
            P("fsdp", None, "tp"),
            P("tp", "fsdp"),
            P(("fsdp", "ctx"), "tp"),
        ),
        out_specs=(
            P(("fsdp", "ctx"), "tp"),
            P(("fsdp", "ctx"), "tp"),
            P("tp"),
            P(("fsdp", "ctx"), None, "tp"),
            P("tp", ("fsdp", "ctx")),
            P("tp"),
            P(("fsdp", "ctx"), None, "tp"),
            P("tp", ("fsdp", "ctx")),
        ),
        check_vma=False,
    )
```
